128 devices in a mesh: cam: 8 (over x, core), tile: 16 (over y, z).
Axes of the slice: x: 4, y: 4, z: 4, core: 2. Of those that a mesh axis runs over, the one named last changes fastest.
Arguments:
- features: bfloat16 [96, 704, 256], P('cam', 'tile'), may hold values from -6 to 6
- w_depth: bfloat16 [256, 64], replicated, may hold values from -0.375 to 0.375
- w_conv: bfloat16 [3, 3, 256, 256], replicated, may hold values from -0.125 to 0.125
- w_pred: bfloat16 [16, 256], replicated, may hold values from -0.375 to 0.375
- send_row: int32 [128, 128, 32], P(('cam', 'tile')), may hold values from 0 to 527, as said below
- send_bin: int32 [128, 128, 32], P(('cam', 'tile')), may hold values from 0 to 63, as said below
- recv_cell: int32 [128, 128, 32], P(('cam', 'tile')), may hold values from 0 to 4096, as said below
- labels: int32 [16, 512, 256], P(None, ('cam', 'tile')), may hold values 0 or 1
Outputs:
- occ_logits: float32 [16, 512, 256], P(None, ('cam', 'tile'))
- grad_features: float32 [96, 704, 256], P('cam', 'tile')
The draws below stay inside these ranges and needn't reach their ends.
Inputs may be any that keep to these rules, and one draw needn't show every extreme that they name: send_row[s, d, k] is the row of source block s that fills slot k toward tile d. send_bin[s, d, k] is the depth bin of that slot. recv_cell[d, s, k] is the cell of tile d into which slot k from source block s adds, or 4096 for an empty slot. In each pair of source and tile the live slots come first and number from 4 up to 32; 16 tiles receive all 32 slots live from every source.
All inputs are finite; a program needn't handle non-finite values. No bound on the sum of `labels` on one device may be relied on, other than what follows from the above.
Results may differ from the reference program's by a relative error of at most 0.0058.
Values may be sent and summed in bfloat16 or wider, within the bound.
No kernel may reach another device: no remote copies, remote signals or barrier semaphores. Data moves between devices by JAX's collectives and lax.ppermute only.
A program may use at most 64 MiB of HBM per device.

```python
import jax
import jax.numpy as jnp
from jax import lax

C = 256
DB = 64
HZ = 16
GY = 512
IMG_DEV = 12
PIX_DEV = 44
CAP = 32
SOURCES = 128
PIX_BLOCKS = 16
IMAGES = 96
PIX = 704
ROWS_SRC = 528
CELLS_DEV = 4096
GX = 1024
HEAVY = 16


def filled_slots(key):
    center = jax.random.randint(jax.random.fold_in(key, 11), (), 0, SOURCES)
    targets = jnp.arange(SOURCES, dtype=jnp.int32)
    crowded = jnp.mod(targets - center, SOURCES) < HEAVY
    baseline = jax.random.randint(jax.random.fold_in(key, 12), (SOURCES, SOURCES), CAP // 8, CAP // 2 + 1)
    counts = jnp.where(crowded[None, :], CAP, baseline)
    positions = jnp.arange(CAP, dtype=jnp.int32)
    return positions[None, None, :] < counts[:, :, None]


def draw_send_row(key, part):
    filled = filled_slots(key)
    chosen = jax.random.randint(jax.random.fold_in(key, 13), (SOURCES, SOURCES, CAP), 0, ROWS_SRC)
    return jnp.where(filled, chosen, 0).astype(jnp.int32)


def draw_send_bin(key, part):
    filled = filled_slots(key)
    chosen = jax.random.randint(jax.random.fold_in(key, 14), (SOURCES, SOURCES, CAP), 0, DB)
    return jnp.where(filled, chosen, 0).astype(jnp.int32)


def draw_recv_cell(key, part):
    filled = filled_slots(key)
    chosen = jax.random.randint(jax.random.fold_in(key, 15), (SOURCES, SOURCES, CAP), 0, CELLS_DEV)
    marked = jnp.where(filled, chosen, CELLS_DEV).astype(jnp.int32)
    return jnp.transpose(marked, (1, 0, 2))


def plant(result, rng, low, largest):
    longest = result.shape.index(max(result.shape))
    spots = []
    for shift in (0, 1):
        where = [jax.random.randint(jax.random.fold_in(rng, axis), (), 0, length) for axis, length in enumerate(result.shape)]
        where[longest] = (where[longest] + shift) % result.shape[longest]
        spots.append(tuple(where))
    return result.at[spots[0]].set(low).at[spots[1]].set(largest)


def shard_levels(stream_key, extent, split, smallest, largest):
    def one(dim, blocks):
        draws = jax.random.uniform(jax.random.fold_in(jax.random.fold_in(stream_key, 6), dim), (blocks,), jnp.float32, smallest / len(split), largest / len(split))
        return jnp.repeat(jnp.exp(draws), extent[dim] // blocks).reshape((-1,) + (1,) * (len(extent) - dim - 1))

    level = one(*split[0])
    for cut in split[1:]:
        level = level * one(*cut)
    return level


def bell_draw(rng, dims, deviation, most, shards=(), kind=jnp.bfloat16):
    loudness = shard_levels(rng, dims, shards, -0.22, 0.18) if shards else 1.0
    result = jax.random.normal(rng, dims, jnp.float32) * deviation * loudness
    return jnp.minimum(jnp.maximum(result, -most), most).astype(kind)


def setup_inputs(seed: int = 0) -> dict:
    key_of = jax.random.split(jax.random.key(seed), 9)
    return {
        "features": bell_draw(key_of[0], (IMAGES, PIX, C), 1.0, 6.0, ((0, 8), (1, 16))),
        "w_depth": bell_draw(key_of[1], (C, DB), C ** -0.5, 0.375),
        "w_conv": bell_draw(key_of[2], (3, 3, C, C), (9 * C) ** -0.5, 0.125),
        "w_pred": bell_draw(key_of[3], (HZ, C), C ** -0.5, 0.375),
        "send_row": draw_send_row(jax.random.fold_in(key_of[8], 71), 0),
        "send_bin": draw_send_bin(jax.random.fold_in(key_of[8], 71), 0),
        "recv_cell": draw_recv_cell(jax.random.fold_in(key_of[8], 71), 0),
        "labels": plant((jax.random.randint(key_of[7], (HZ, GX // 2, GY // 2), 0, 3) < 1).astype(jnp.int32), jax.random.fold_in(key_of[7], 1), 0, 1),
    }


loss_weight = 16.0


def silu_slope(inputs):
    sigmoid_part = jax.nn.sigmoid(inputs)
    return sigmoid_part * (1.0 + inputs * (1.0 - sigmoid_part))


def reference(features, w_depth, w_conv, w_pred, send_row, send_bin, recv_cell, labels):
    cam_count = IMAGES // IMG_DEV
    blocked = features.reshape(cam_count, IMG_DEV, PIX_BLOCKS, PIX_DEV, C)
    source_rows = jnp.transpose(blocked, (0, 2, 1, 3, 4)).reshape(SOURCES, ROWS_SRC, C)
    depth_prob = jax.nn.sigmoid(jnp.dot(source_rows.reshape(-1, C), w_depth, preferred_element_type=jnp.float32)).reshape(SOURCES, ROWS_SRC, DB)
    recv_by_source = jnp.transpose(recv_cell, (1, 0, 2))
    total_cells = SOURCES * CELLS_DEV
    tile_base = (jnp.arange(SOURCES, dtype=jnp.int32) * CELLS_DEV)[:, None]

    def splat_one(grid_flat, sliced):
        rows_here, depth_here, row_ids, bin_ids, cell_ids = sliced
        picked = rows_here[row_ids]
        depth_slot = depth_here[row_ids, bin_ids]
        payload = (depth_slot[..., None] * picked.astype(jnp.float32)).astype(jnp.bfloat16)
        target = jnp.where(cell_ids == CELLS_DEV, total_cells, tile_base + cell_ids).astype(jnp.int32)
        grid_flat = grid_flat.at[target.reshape(-1)].add(payload.reshape(-1, C).astype(jnp.float32), mode="drop")
        return grid_flat, None

    grid_flat, unused = lax.scan(splat_one, jnp.zeros((total_cells, C), jnp.float32), (source_rows, depth_prob, send_row, send_bin, recv_by_source))
    grid = grid_flat.astype(jnp.bfloat16).reshape(GX, GY, C)
    padded = jnp.pad(grid, ((1, 0), (1, 0), (0, 0)))
    out_rows = GX // 2
    out_cols = GY // 2
    conv_sum = jnp.zeros((out_rows * out_cols, C), jnp.float32)
    for tap_row in range(3):
        for tap_col in range(3):
            window = padded[tap_row:tap_row + GX - 1:2, tap_col:tap_col + GY - 1:2]
            conv_sum = conv_sum + jnp.dot(window.reshape(-1, C), w_conv[tap_row, tap_col], preferred_element_type=jnp.float32)
    activation = jax.nn.silu(conv_sum).astype(jnp.bfloat16)
    logits = jnp.dot(activation, w_pred.T, preferred_element_type=jnp.float32).T
    occ_logits = logits.reshape(HZ, out_rows, out_cols)
    dlogit = (loss_weight * (jax.nn.sigmoid(logits) - labels.reshape(HZ, -1).astype(jnp.float32))).astype(jnp.bfloat16)
    grad_act = jnp.dot(dlogit.T, w_pred, preferred_element_type=jnp.float32)
    grad_conv = (grad_act * silu_slope(conv_sum)).astype(jnp.bfloat16)
    grad_pad = jnp.zeros((GX + 1, GY + 1, C), jnp.float32)
    for tap_row in range(3):
        for tap_col in range(3):
            tap_term = jnp.dot(grad_conv, w_conv[tap_row, tap_col].T, preferred_element_type=jnp.float32).reshape(out_rows, out_cols, C)
            grad_pad = grad_pad.at[tap_row:tap_row + GX - 1:2, tap_col:tap_col + GY - 1:2].add(tap_term)
    grad_grid = grad_pad[1:, 1:].astype(jnp.bfloat16).reshape(SOURCES, CELLS_DEV, C)
    bordered = jnp.concatenate([grad_grid, jnp.zeros((SOURCES, 1, C), jnp.bfloat16)], axis=1)
    tile_index = jnp.arange(SOURCES, dtype=jnp.int32)[:, None]

    def back_one(state_in, sliced):
        rows_here, depth_here, row_ids, bin_ids, cell_ids = sliced
        grad_slots = bordered[tile_index, cell_ids]
        picked = rows_here[row_ids]
        depth_slot = depth_here[row_ids, bin_ids]
        weighted = (depth_slot[..., None] * grad_slots.astype(jnp.float32)).astype(jnp.bfloat16)
        grad_rows = jax.ops.segment_sum(weighted.reshape(-1, C).astype(jnp.float32), row_ids.reshape(-1), num_segments=ROWS_SRC)
        inner_prod = jnp.sum(picked.astype(jnp.float32) * grad_slots.astype(jnp.float32), axis=-1)
        grad_depth = jnp.zeros((ROWS_SRC, DB), jnp.float32).at[row_ids.reshape(-1), bin_ids.reshape(-1)].add(inner_prod.reshape(-1))
        grad_logit = (depth_here * (1.0 - depth_here) * grad_depth).astype(jnp.bfloat16)
        return state_in, grad_rows + jnp.dot(grad_logit, w_depth.T, preferred_element_type=jnp.float32)

    unused_state, grad_all = lax.scan(back_one, jnp.zeros((), jnp.float32), (source_rows, depth_prob, send_row, send_bin, recv_by_source))
    grad_blocked = grad_all.reshape(cam_count, PIX_BLOCKS, IMG_DEV, PIX_DEV, C)
    grad_features = jnp.transpose(grad_blocked, (0, 2, 1, 3, 4)).reshape(IMAGES, PIX, C)
    return occ_logits, grad_features
```

```python
import jax
import jax.numpy as jnp
from jax import lax
from jax.experimental import pallas as pl
from jax.experimental.pallas import tpu as pltpu
from jax.sharding import PartitionSpec as P

loss_weight = 16.0
BF = jnp.bfloat16
F32 = jnp.float32
AXES = ("cam", "tile")
SLOT_BLOCK = 512
CELL_BLOCK = 512
IMG_PAD = 48
VMEM_LIMIT = 48 * 1024 * 1024


def shifted(shard, by):
    devices = lax.axis_size(AXES)
    pairs = [(i, i + by) for i in range(devices) if 0 <= i + by < devices]
    return lax.ppermute(shard, AXES, pairs)


def dot(a, b):
    return jnp.dot(a, b, preferred_element_type=F32)


def dot_t(a, b):
    return lax.dot_general(a, b, (((1,), (1,)), ((), ())), preferred_element_type=F32)


def sigmoid(v):
    return 1.0 / (1.0 + jnp.exp(-v))


def padded_row(row):
    return row + 4 * ((row * 1490) >> 16)


def cell_place(cell):
    u = cell >> 9
    v = cell & 511
    col = v >> 1
    odd = v & 1
    half = (u >> 1) * 256 + col
    even_rows = odd * 1024 + half
    odd_rows = 2048 + odd * 768 + half
    last_row = 3584 + odd * 256 + col
    place = jnp.where((u & 1) == 0, even_rows, jnp.where(u == 7, last_row, odd_rows))
    return jnp.where(u >= 8, -1, place)


def one_hot(mask):
    return jnp.where(mask, 1.0, 0.0).astype(BF)


def fill_rows(feat_ref, x_ref):
    for i in range(feat_ref.shape[0]):
        rows = feat_ref[i].astype(F32)
        rows = jnp.concatenate([rows, jnp.zeros((IMG_PAD - rows.shape[0], rows.shape[1]), F32)], axis=0)
        x_ref[i * IMG_PAD : (i + 1) * IMG_PAD, :] = rows.astype(BF)


def pick_kernel(feat_ref, wd_ref, row_ref, bin_ref, pay_ref, picked_ref, depth_ref, x_ref):
    @pl.when(pl.program_id(0) == 0)
    def _():
        fill_rows(feat_ref, x_ref)

    ids = padded_row(row_ref[...])
    rows = x_ref.shape[0]
    groups, cap = ids.shape
    count = groups * cap
    chooser = one_hot(lax.broadcasted_iota(jnp.int32, (groups, cap, rows), 2) == ids[:, :, None]).reshape(count, rows)
    picked = dot(chooser, x_ref[...])
    picked_b = picked.astype(BF)
    logits = dot(picked_b, wd_ref[...])
    bins = logits.shape[1]
    mask = lax.broadcasted_iota(jnp.int32, (groups, cap, bins), 2) == bin_ref[...][:, :, None]
    chosen = jnp.sum(jnp.where(mask, logits.reshape(groups, cap, bins), 0.0), axis=2, keepdims=True)
    depth = sigmoid(chosen).reshape(count, 1)
    pay_ref[...] = (depth * picked).astype(BF)
    picked_ref[...] = picked_b
    depth_ref[...] = jnp.broadcast_to(depth, (count, 128))


def splat_kernel(first, cell_ref, val_ref, out_ref):
    rows = out_ref.shape[0]
    base = first + pl.program_id(0) * rows
    place = cell_place(cell_ref[...]) - base
    count = place.shape[1]
    placer = one_hot(lax.broadcasted_iota(jnp.int32, (rows, count), 0) == place)
    out_ref[...] = dot(placer, val_ref[...]).astype(BF)


def shift_down(v):
    col = lax.broadcasted_iota(jnp.int32, v.shape, 0) & 255
    return jnp.where(col == 0, 0.0, pltpu.roll(v, 1, 0))


def shift_up(v):
    n = v.shape[0]
    col = lax.broadcasted_iota(jnp.int32, v.shape, 0) & 255
    return jnp.where(col == 255, 0.0, pltpu.roll(v, n - 1, 0))


def conv_kernel(grid_ref, rim_ref, halo_ref, w_ref, wp_ref, lab_ref, logit_ref, dz_ref, low_ref):
    lines = lab_ref.shape[1]
    for i in range(lines):
        r = i * 256
        ee = grid_ref[r : r + 256, :]
        eo = grid_ref[1024 + r : 1280 + r, :]
        if i == lines - 1:
            oe, oo = rim_ref[0:256, :], rim_ref[256:512, :]
        else:
            oe, oo = grid_ref[2048 + r : 2304 + r, :], grid_ref[2816 + r : 3072 + r, :]
        if i == 0:
            ue, uo = halo_ref[0:256, :], halo_ref[256:512, :]
        else:
            ue, uo = grid_ref[1792 + r : 2048 + r, :], grid_ref[2560 + r : 2816 + r, :]
        z = dot(ue, w_ref[0, 1]) + dot(uo, w_ref[0, 2])
        z = z + dot(ee, w_ref[1, 1]) + dot(eo, w_ref[1, 2])
        z = z + dot(oe, w_ref[2, 1]) + dot(oo, w_ref[2, 2])
        z = z + shift_down(dot(uo, w_ref[0, 0]) + dot(eo, w_ref[1, 0]) + dot(oo, w_ref[2, 0]))
        s = sigmoid(z)
        act = (z * s).astype(BF)
        logits = dot_t(wp_ref[...], act)
        logit_ref[:, i, :] = logits
        dlogit = (loss_weight * (sigmoid(logits) - lab_ref[:, i, :].astype(F32))).astype(BF)
        grad_act = lax.dot_general(dlogit, wp_ref[...], (((0,), (0,)), ((), ())), preferred_element_type=F32)
        dz_ref[r : r + 256, :] = (grad_act * (s * (1.0 + z * (1.0 - s)))).astype(BF)


def conv_back_kernel(dz_ref, w_ref, out_ref):
    for i in range(4):
        r = i * 256
        dz = dz_ref[r : r + 256, :]
        dzs = shift_up(dz.astype(F32)).astype(BF)
        out_ref[r : r + 256, :] = dot_t(dz, w_ref[1, 1]).astype(BF)
        out_ref[1024 + r : 1280 + r, :] = (dot_t(dz, w_ref[1, 2]) + dot_t(dzs, w_ref[1, 0])).astype(BF)
        if i < 3:
            dn = dz_ref[r + 256 : r + 512, :]
            dns = shift_up(dn.astype(F32)).astype(BF)
            out_ref[2048 + r : 2304 + r, :] = (dot_t(dz, w_ref[2, 1]) + dot_t(dn, w_ref[0, 1])).astype(BF)
            out_ref[2816 + r : 3072 + r, :] = (
                dot_t(dz, w_ref[2, 2]) + dot_t(dzs, w_ref[2, 0]) + dot_t(dn, w_ref[0, 2]) + dot_t(dns, w_ref[0, 0])
            ).astype(BF)


def gather_kernel(main_ref, dz_ref, halo_ref, w_ref, cell_ref, out_ref, all_ref):
    @pl.when(pl.program_id(0) == 0)
    def _():
        all_ref[0:3584, :] = main_ref[...]
        dz = dz_ref[...]
        dzs = shift_up(dz.astype(F32)).astype(BF)
        dn = halo_ref[...]
        dns = shift_up(dn.astype(F32)).astype(BF)
        all_ref[3584:3840, :] = (dot_t(dz, w_ref[2, 1]) + dot_t(dn, w_ref[0, 1])).astype(BF)
        all_ref[3840:4096, :] = (
            dot_t(dz, w_ref[2, 2]) + dot_t(dzs, w_ref[2, 0]) + dot_t(dn, w_ref[0, 2]) + dot_t(dns, w_ref[0, 0])
        ).astype(BF)

    place = cell_place(cell_ref[...])
    groups, cap = place.shape
    cells = all_ref.shape[0]
    chooser = one_hot(lax.broadcasted_iota(jnp.int32, (groups, cap, cells), 2) == place[:, :, None]).reshape(
        groups * cap, cells
    )
    out_ref[...] = dot(chooser, all_ref[...]).astype(BF)


def grad_kernel(feat_ref, wd_ref, row_ref, bin_ref, picked_ref, depth_ref, inc_ref, out_ref, x_ref, acc_ref, accd_ref):
    step = pl.program_id(0)

    @pl.when(step == 0)
    def _():
        fill_rows(feat_ref, x_ref)
        acc_ref[...] = jnp.zeros_like(acc_ref)
        accd_ref[...] = jnp.zeros_like(accd_ref)

    rows = x_ref.shape[0]
    bins = wd_ref.shape[1]
    inc = inc_ref[...].astype(F32)
    count = inc.shape[0]
    depth = depth_ref[...]
    weighted = (inc * jnp.concatenate([depth, depth], axis=1)).astype(BF)
    inner = jnp.sum(picked_ref[...].astype(F32) * inc, axis=1, keepdims=True)
    groups, cap = bin_ref.shape
    mask = lax.broadcasted_iota(jnp.int32, (groups, cap, 128), 2) & 63
    mask = mask == bin_ref[...][:, :, None]
    terms = jnp.where(mask, inner.reshape(groups, cap, 1), 0.0).reshape(count, 128)
    high = terms.astype(BF)
    low = (terms - high.astype(F32)).astype(BF)
    lane = lax.broadcasted_iota(jnp.int32, (count, 128), 1)
    both = jnp.where(lane < bins, high.astype(F32), low.astype(F32)).astype(BF)
    ids = padded_row(row_ref[...].reshape(1, count))
    chooser = one_hot(lax.broadcasted_iota(jnp.int32, (rows, count), 0) == ids)
    acc_ref[...] += dot(chooser, weighted)
    accd_ref[...] += dot(chooser, both)

    @pl.when(step == pl.num_programs(0) - 1)
    def _():
        prob = sigmoid(dot(x_ref[...], wd_ref[...]))
        sums = accd_ref[...]
        grad_depth = sums[:, :bins] + sums[:, bins:]
        grad_logit = (prob * (1.0 - prob) * grad_depth).astype(BF)
        total = acc_ref[...] + dot_t(grad_logit, wd_ref[...])
        for i in range(out_ref.shape[0]):
            out_ref[i] = total[i * IMG_PAD : i * IMG_PAD + out_ref.shape[1], :]


def params():
    return pltpu.CompilerParams(vmem_limit_bytes=VMEM_LIMIT)


def whole(shape):
    return pl.BlockSpec(shape, lambda i: (0,) * len(shape))


def per_device(features, w_depth, w_conv, w_pred, send_row, send_bin, recv_cell, labels):
    imgs, pix, chan = features.shape
    bins = w_depth.shape[1]
    heights = w_pred.shape[0]
    sources, cap = send_row.shape[1], send_row.shape[2]
    slots = sources * cap
    blocks = slots // SLOT_BLOCK
    group = SLOT_BLOCK // cap
    rows = imgs * IMG_PAD
    row2 = send_row.reshape(sources, cap)
    bin2 = send_bin.reshape(sources, cap)
    cell2 = recv_cell.reshape(sources, cap)
    row_line = send_row.reshape(blocks, 1, SLOT_BLOCK)
    cell_line = recv_cell.reshape(1, slots)
    table_spec = pl.BlockSpec((group, cap), lambda i: (i, 0))
    slot_spec = pl.BlockSpec((SLOT_BLOCK, chan), lambda i: (i, 0))
    depth_spec = pl.BlockSpec((SLOT_BLOCK, 128), lambda i: (i, 0))

    payload, picked, depth = pl.pallas_call(
        pick_kernel,
        out_shape=(
            jax.ShapeDtypeStruct((slots, chan), BF),
            jax.ShapeDtypeStruct((slots, chan), BF),
            jax.ShapeDtypeStruct((slots, 128), F32),
        ),
        grid=(blocks,),
        in_specs=[whole(features.shape), whole(w_depth.shape), table_spec, table_spec],
        out_specs=(slot_spec, slot_spec, depth_spec),
        scratch_shapes=[pltpu.VMEM((rows, chan), BF)],
        compiler_params=params(),
        name="pick",
    )(features, w_depth, row2, bin2)

    arrived = lax.all_to_all(payload.reshape(sources, cap, chan), AXES, split_axis=0, concat_axis=0, tiled=True)
    arrived = arrived.reshape(slots, chan)

    def splat(first, count, name):
        return pl.pallas_call(
            lambda *refs: splat_kernel(first, *refs),
            out_shape=jax.ShapeDtypeStruct((count, chan), BF),
            grid=(count // CELL_BLOCK,),
            in_specs=[whole((1, slots)), whole((slots, chan))],
            out_specs=pl.BlockSpec((CELL_BLOCK, chan), lambda i: (i, 0)),
            compiler_params=params(),
            name=name,
        )(cell_line, arrived)

    rim = splat(3584, 512, "splat_rim")
    halo = shifted(rim, 1)
    main = splat(0, 3584, "splat_main")

    logits, dz = pl.pallas_call(
        lambda *refs: conv_kernel(*refs, None),
        out_shape=(jax.ShapeDtypeStruct(labels.shape, F32), jax.ShapeDtypeStruct((1024, chan), BF)),
        compiler_params=params(),
        name="conv",
    )(main, rim, halo, w_conv, w_pred, labels)
    dz_next = shifted(dz[0:256], -1)
    dmain = pl.pallas_call(
        conv_back_kernel,
        out_shape=jax.ShapeDtypeStruct((3584, chan), BF),
        compiler_params=params(),
        name="conv_back",
    )(dz, w_conv)

    outgoing = pl.pallas_call(
        gather_kernel,
        out_shape=jax.ShapeDtypeStruct((slots, chan), BF),
        grid=(blocks,),
        in_specs=[
            whole((3584, chan)),
            pl.BlockSpec((256, chan), lambda i: (3, 0)),
            whole((256, chan)),
            whole(w_conv.shape),
            table_spec,
        ],
        out_specs=slot_spec,
        scratch_shapes=[pltpu.VMEM((4096, chan), BF)],
        compiler_params=params(),
        name="pick_back",
    )(dmain, dz, dz_next, w_conv, cell2)

    returned = lax.all_to_all(outgoing.reshape(sources, cap, chan), AXES, split_axis=0, concat_axis=0, tiled=True)
    returned = returned.reshape(slots, chan)

    grad = pl.pallas_call(
        grad_kernel,
        out_shape=jax.ShapeDtypeStruct((imgs, pix, chan), F32),
        grid=(blocks,),
        in_specs=[
            whole(features.shape),
            whole(w_depth.shape),
            pl.BlockSpec((1, 1, SLOT_BLOCK), lambda i: (i, 0, 0)),
            table_spec,
            slot_spec,
            depth_spec,
            slot_spec,
        ],
        out_specs=whole((imgs, pix, chan)),
        scratch_shapes=[
            pltpu.VMEM((rows, chan), BF),
            pltpu.VMEM((rows, chan), F32),
            pltpu.VMEM((rows, 128), F32),
        ],
        compiler_params=params(),
        name="grad",
    )(features, w_depth, row_line, bin2, picked, depth, returned)
    return logits, grad


def solution(mesh):
    in_specs = (
        P("cam", "tile", None),
        P(),
        P(),
        P(),
        P(("cam", "tile"), None, None),
        P(("cam", "tile"), None, None),
        P(("cam", "tile"), None, None),
        P(None, ("cam", "tile"), None),
    )
    out_specs = (P(None, ("cam", "tile"), None), P("cam", "tile", None))
    return jax.shard_map(
        per_device, mesh=mesh, in_specs=in_specs, out_specs=out_specs, check_vma=False
    )
```

```python
import jax
import jax.numpy as jnp
from jax import lax
from jax.experimental import pallas as pl
from jax.experimental.pallas import tpu as pltpu
from jax.sharding import PartitionSpec as P

loss_weight = 16.0
BF = jnp.bfloat16
F32 = jnp.float32
AXES = ("cam", "tile")
PICK_BLOCK = 2048
TAKE_BLOCK = 1024
GRAD_BLOCK = 1024
CELL_BLOCK = 512
CELLS = 4096
IMG_PAD = 48
VMEM_LIMIT = 48 * 1024 * 1024


def shifted(shard, by):
    devices = lax.axis_size(AXES)
    pairs = [(i, i + by) for i in range(devices) if 0 <= i + by < devices]
    return lax.ppermute(shard, AXES, pairs)


def dot(a, b):
    return jnp.dot(a, b, preferred_element_type=F32)


def dot_t(a, b):
    return lax.dot_general(a, b, (((1,), (1,)), ((), ())), preferred_element_type=F32)


def sigmoid(v):
    return 1.0 / (1.0 + jnp.exp(-v))


def padded_row(row):
    return row + 4 * ((row * 1490) >> 16)


def cell_place(cell):
    u = cell >> 9
    v = cell & 511
    col = v >> 1
    odd = v & 1
    half = (u >> 1) * 256 + col
    even_rows = odd * 1024 + half
    odd_rows = 2048 + odd * 768 + half
    last_row = 3584 + odd * 256 + col
    place = jnp.where((u & 1) == 0, even_rows, jnp.where(u == 7, last_row, odd_rows))
    return jnp.where(u >= 8, -1, place)


def one_hot(mask):
    return jnp.where(mask, 1.0, 0.0).astype(BF)


def fill_rows(feat_ref, x_ref):
    for i in range(feat_ref.shape[0]):
        rows = feat_ref[i].astype(F32)
        rows = jnp.concatenate([rows, jnp.zeros((IMG_PAD - rows.shape[0], rows.shape[1]), F32)], axis=0)
        x_ref[i * IMG_PAD : (i + 1) * IMG_PAD, :] = rows.astype(BF)


def pick_rows(ids, x):
    groups, per = ids.shape
    rows = x.shape[0]
    chooser = one_hot(lax.broadcasted_iota(jnp.int32, (groups, per, rows), 2) == ids[:, :, None])
    return dot(chooser.reshape(groups * per, rows), x)


def pick_kernel(feat_ref, wd_ref, row_ref, bin_ref, pay_ref, tie_ref, x_ref, rid_ref, bid_ref):
    step = pl.program_id(0)

    @pl.when(step == 0)
    def _():
        fill_rows(feat_ref, x_ref)
        rid_ref[...] = padded_row(jnp.transpose(row_ref[...]))
        bid_ref[...] = jnp.transpose(bin_ref[...])
        tie_ref[...] = jnp.zeros_like(tie_ref)

    count = pay_ref.shape[0]
    per = rid_ref.shape[1]
    groups = count // per
    at = pl.ds(pl.multiple_of(step * groups, groups), groups)
    picked = pick_rows(rid_ref[at, :], x_ref[...])
    logits = dot_t(picked.astype(BF), wd_ref[...])
    bins = logits.shape[1]
    mask = lax.broadcasted_iota(jnp.int32, (groups, per, bins), 2) == bid_ref[at, :][:, :, None]
    chosen = jnp.sum(jnp.where(mask, logits.reshape(groups, per, bins), 0.0), axis=2, keepdims=True)
    pay_ref[...] = (sigmoid(chosen).reshape(count, 1) * picked).astype(BF)


def line_up(table_ref, wide_ref):
    per, partners = table_ref.shape
    wide_ref[:, 0:per] = jnp.transpose(table_ref[...])
    fold = 128 // per
    lane = lax.broadcasted_iota(jnp.int32, (partners // fold, 128), 1) // per
    out = jnp.zeros((partners // fold, 128), jnp.int32)
    for j in range(fold):
        part = wide_ref[pl.ds(j, partners // fold, stride=fold), :]
        if j:
            part = pltpu.roll(part, j * per, 1)
        out = jnp.where(lane == j, part, out)
    return out


def as_line(table):
    return jnp.concatenate([table[g : g + 1, :] for g in range(table.shape[0])], axis=1)


def places_kernel(cell_ref, tie_ref, line_ref, twice_ref, wide_ref):
    line_ref[...] = cell_place(line_up(cell_ref, wide_ref))
    place = cell_place(cell_ref[...])
    twice_ref[...] = 2 * jnp.where(place < 0, CELLS, place)


def again_kernel(feat_ref, wd_ref, row_ref, bin_ref, tie_ref, picked_ref, depth_ref, line_ref, slope_ref, x_ref, rid_ref, bid_ref, wide_ref):
    step = pl.program_id(0)

    @pl.when(step == 0)
    def _():
        fill_rows(feat_ref, x_ref)
        rid_ref[...] = padded_row(jnp.transpose(row_ref[...]))
        line_ref[...] = padded_row(line_up(row_ref, wide_ref))
        bid_ref[...] = line_up(bin_ref, wide_ref)
        prob = sigmoid(dot_t(x_ref[...], wd_ref[...]))
        slope_ref[...] = prob * (1.0 - prob)

    count = picked_ref.shape[0]
    groups = count // rid_ref.shape[1]
    at = pl.ds(pl.multiple_of(step * groups, groups), groups)
    picked = pick_rows(rid_ref[at, :], x_ref[...]).astype(BF)
    picked_ref[...] = picked
    logits = dot_t(wd_ref[...], picked)
    lines = count // 128
    bins = as_line(bid_ref[pl.ds(pl.multiple_of(step * lines, lines), lines), :])
    mask = lax.broadcasted_iota(jnp.int32, logits.shape, 0) == bins
    depth_ref[0] = sigmoid(jnp.sum(jnp.where(mask, logits, 0.0), axis=0, keepdims=True))


def splat_kernel(first, line_ref, val_ref, out_ref):
    rows = out_ref.shape[0]
    place = as_line(line_ref[...]) - (first + pl.program_id(0) * rows)
    placer = one_hot(lax.broadcasted_iota(jnp.int32, (rows, place.shape[1]), 0) == place)
    out_ref[...] = dot(placer, val_ref[...]).astype(BF)


def shift_down(v):
    col = lax.broadcasted_iota(jnp.int32, v.shape, 0) & 255
    return jnp.where(col == 0, 0.0, pltpu.roll(v, 1, 0))


def shift_up(v):
    n = v.shape[0]
    col = lax.broadcasted_iota(jnp.int32, v.shape, 0) & 255
    return jnp.where(col == 255, 0.0, pltpu.roll(v, n - 1, 0))


def conv_lines(ue, uo, ee, eo, oe, oo, w_ref, wp_ref, labels):
    z = dot(ue, w_ref[0, 1]) + dot(uo, w_ref[0, 2])
    z = z + dot(ee, w_ref[1, 1]) + dot(eo, w_ref[1, 2])
    z = z + dot(oe, w_ref[2, 1]) + dot(oo, w_ref[2, 2])
    z = z + shift_down(dot(uo, w_ref[0, 0]) + dot(eo, w_ref[1, 0]) + dot(oo, w_ref[2, 0]))
    s = sigmoid(z)
    act = (z * s).astype(BF)
    logits = dot_t(wp_ref[...], act)
    dlogit = (loss_weight * (sigmoid(logits) - labels.astype(F32))).astype(BF)
    grad_act = lax.dot_general(dlogit, wp_ref[...], (((0,), (0,)), ((), ())), preferred_element_type=F32)
    return logits, (grad_act * (s * (1.0 + z * (1.0 - s)))).astype(BF)


def conv_first_kernel(grid_ref, halo_ref, w_ref, wp_ref, lab_ref, logit_ref, dz_ref):
    logits, dz = conv_lines(
        halo_ref[0:256, :],
        halo_ref[256:512, :],
        grid_ref[0:256, :],
        grid_ref[1024:1280, :],
        grid_ref[2048:2304, :],
        grid_ref[2816:3072, :],
        w_ref,
        wp_ref,
        lab_ref[:, 0, :],
    )
    logit_ref[...] = logits
    dz_ref[...] = dz


def conv_rest_kernel(grid_ref, rim_ref, w_ref, wp_ref, lab_ref, first_ref, dzf_ref, logit_ref, last_ref, out_ref, dz_ref):
    logit_ref[:, 0, :] = first_ref[...]
    dz_ref[0:256, :] = dzf_ref[...]
    logits, dz = conv_lines(
        grid_ref[2048:2816, :],
        grid_ref[2816:3584, :],
        grid_ref[256:1024, :],
        grid_ref[1280:2048, :],
        jnp.concatenate([grid_ref[2304:2816, :], rim_ref[0:256, :]], axis=0),
        jnp.concatenate([grid_ref[3072:3584, :], rim_ref[256:512, :]], axis=0),
        w_ref,
        wp_ref,
        jnp.concatenate([lab_ref[:, i, :] for i in range(1, 4)], axis=1),
    )
    for i in range(1, 4):
        logit_ref[:, i, :] = logits[:, (i - 1) * 256 : i * 256]
    dz_ref[256:1024, :] = dz
    last_ref[...] = dz[512:768, :]
    dz = dz_ref[...]
    dzs = shift_up(dz.astype(F32)).astype(BF)
    out_ref[0:1024, :] = dot_t(dz, w_ref[1, 1]).astype(BF)
    out_ref[1024:2048, :] = (dot_t(dz, w_ref[1, 2]) + dot_t(dzs, w_ref[1, 0])).astype(BF)
    out_ref[2048:2816, :] = (dot_t(dz[0:768], w_ref[2, 1]) + dot_t(dz[256:1024], w_ref[0, 1])).astype(BF)
    out_ref[2816:3584, :] = (
        dot_t(dz[0:768], w_ref[2, 2])
        + dot_t(dzs[0:768], w_ref[2, 0])
        + dot_t(dz[256:1024], w_ref[0, 2])
        + dot_t(dzs[256:1024], w_ref[0, 0])
    ).astype(BF)


def take_kernel(twice_ref, main_ref, dz_ref, halo_ref, w_ref, out_ref, tie_ref, src_ref, dst_ref):
    step = pl.program_id(0)

    @pl.when(step == 0)
    def _():
        def put(first, rows):
            src_ref[pl.ds(2 * first, rows.shape[0], stride=2), :] = rows[:, :128]
            src_ref[pl.ds(2 * first + 1, rows.shape[0], stride=2), :] = rows[:, 128:]

        put(0, main_ref[...].astype(F32))
        dz = dz_ref[...]
        dzs = shift_up(dz.astype(F32)).astype(BF)
        dn = halo_ref[...]
        dns = shift_up(dn.astype(F32)).astype(BF)
        put(3584, (dot_t(dz, w_ref[2, 1]) + dot_t(dn, w_ref[0, 1])).astype(BF).astype(F32))
        rim_odd = dot_t(dz, w_ref[2, 2]) + dot_t(dzs, w_ref[2, 0]) + dot_t(dn, w_ref[0, 2]) + dot_t(dns, w_ref[0, 0])
        put(3840, rim_odd.astype(BF).astype(F32))
        src_ref[2 * CELLS : 2 * CELLS + 8, :] = jnp.zeros((8, 128), F32)
        tie_ref[...] = jnp.zeros_like(tie_ref)

    count = out_ref.shape[0]
    per = twice_ref.shape[0]
    groups = count // per

    def one(g, carry):
        rows = dst_ref.at[pl.ds(pl.multiple_of(g * (2 * per), 2 * per), 2 * per), :]
        for k in range(per):
            at = pl.multiple_of(twice_ref[k, step * groups + g], 2)
            rows[2 * k : 2 * k + 2, :] = src_ref[pl.ds(at, 2), :]
        return carry

    lax.fori_loop(0, groups, one, 0)
    out_ref[:, :128] = dst_ref[pl.ds(0, count, stride=2), :].astype(BF)
    out_ref[:, 128:] = dst_ref[pl.ds(1, count, stride=2), :].astype(BF)


def grad_kernel(wd_ref, line_ref, bin_ref, depth_ref, slope_ref, picked_ref, inc_ref, out_ref, bid_ref, acc_ref, accd_ref):
    step = pl.program_id(0)

    @pl.when(step == 0)
    def _():
        bid_ref[...] = jnp.transpose(bin_ref[...])
        acc_ref[...] = jnp.zeros_like(acc_ref)
        accd_ref[...] = jnp.zeros_like(accd_ref)

    rows = acc_ref.shape[0]
    inc = inc_ref[...]
    count = inc.shape[0]
    per = bid_ref.shape[1]
    groups = count // per
    terms = picked_ref[...].astype(F32) * inc.astype(F32)
    terms = terms[:, :128] + terms[:, 128:]
    high = terms.astype(BF)
    halves = jnp.concatenate([high, (terms - high.astype(F32)).astype(BF)], axis=1)
    inner = dot(halves, jnp.ones((256, 128), BF)).reshape(groups, per, 128)
    at = pl.ds(pl.multiple_of(step * groups, groups), groups)
    mask = (lax.broadcasted_iota(jnp.int32, (groups, per, 128), 2) & 63) == bid_ref[at, :][:, :, None]
    binned = jnp.where(mask, inner, 0.0).reshape(count, 128)
    high = binned.astype(BF).astype(F32)
    lane = lax.broadcasted_iota(jnp.int32, (count, 128), 1)
    both = jnp.where(lane < 64, high, binned - high).astype(BF)
    lines = count // 128
    hot = lax.broadcasted_iota(jnp.int32, (rows, count), 0) == as_line(
        line_ref[pl.ds(pl.multiple_of(step * lines, lines), lines), :]
    )
    acc_ref[...] += dot(jnp.where(hot, depth_ref[0], 0.0).astype(BF), inc)
    accd_ref[...] += dot(one_hot(hot), both)

    @pl.when(step == pl.num_programs(0) - 1)
    def _():
        sums = accd_ref[...]
        grad_logit = (slope_ref[...] * (sums[:, :64] + sums[:, 64:])).astype(BF)
        total = acc_ref[...] + dot(grad_logit, wd_ref[...])
        for i in range(out_ref.shape[0]):
            out_ref[i] = total[i * IMG_PAD : i * IMG_PAD + out_ref.shape[1], :]


def params():
    return pltpu.CompilerParams(vmem_limit_bytes=VMEM_LIMIT)


def whole(shape):
    return pl.BlockSpec(shape, lambda i: (0,) * len(shape))


def per_device(features, w_depth, w_conv, w_pred, send_row, send_bin, recv_cell, labels):
    imgs, pix, chan = features.shape
    sources, cap = send_row.shape[1], send_row.shape[2]
    slots = sources * cap
    rows = imgs * IMG_PAD
    row_t = jnp.transpose(send_row.reshape(sources, cap))
    bin_t = jnp.transpose(send_bin.reshape(sources, cap))
    cell_t = jnp.transpose(recv_cell.reshape(sources, cap))
    wd_t = jnp.transpose(w_depth)
    bins = wd_t.shape[0]
    table = whole((cap, sources))
    lines = slots // 128
    ids_scratch = pltpu.VMEM((sources, cap), jnp.int32)
    wide_scratch = pltpu.VMEM((sources, 128), jnp.int32)
    x_scratch = pltpu.VMEM((rows, chan), BF)
    tie_spec = whole((8, 128))
    tie_shape = jax.ShapeDtypeStruct((8, 128), F32)

    def slot_spec(block):
        return pl.BlockSpec((block, chan), lambda i: (i, 0))

    def exchange(v):
        out = lax.all_to_all(v.reshape(sources, cap, chan), AXES, split_axis=0, concat_axis=0, tiled=True)
        return out.reshape(slots, chan)

    payload, tie = pl.pallas_call(
        pick_kernel,
        out_shape=(pltpu.HBM((slots, chan), BF), tie_shape),
        grid=(slots // PICK_BLOCK,),
        in_specs=[whole(features.shape), whole(wd_t.shape), table, table],
        out_specs=(slot_spec(PICK_BLOCK), tie_spec),
        scratch_shapes=[x_scratch, ids_scratch, ids_scratch],
        compiler_params=params(),
        name="pick",
    )(features, wd_t, row_t, bin_t)
    arrived = exchange(payload)

    place_line, place_twice = pl.pallas_call(
        places_kernel,
        out_shape=(
            jax.ShapeDtypeStruct((lines, 128), jnp.int32),
            jax.ShapeDtypeStruct((cap, sources), jnp.int32),
        ),
        grid=(1,),
        in_specs=[table, tie_spec],
        out_specs=(whole((lines, 128)), table),
        scratch_shapes=[wide_scratch],
        compiler_params=params(),
        name="places",
    )(cell_t, tie)

    def splat(first, count, name):
        return pl.pallas_call(
            lambda *refs: splat_kernel(first, *refs),
            out_shape=jax.ShapeDtypeStruct((count, chan), BF),
            grid=(count // CELL_BLOCK,),
            in_specs=[whole((lines, 128)), whole((slots, chan))],
            out_specs=pl.BlockSpec((CELL_BLOCK, chan), lambda i: (i, 0)),
            compiler_params=params(),
            name=name,
        )(place_line, arrived)

    rim = splat(3584, 512, "splat_rim")
    halo = shifted(rim, 1)
    main = splat(0, 3584, "splat_main")

    logits0, dz0 = pl.pallas_call(
        conv_first_kernel,
        out_shape=(jax.ShapeDtypeStruct((w_pred.shape[0], 256), F32), jax.ShapeDtypeStruct((256, chan), BF)),
        compiler_params=params(),
        name="conv_first",
    )(main, halo, w_conv, w_pred, labels)
    dz_next = shifted(dz0, -1)
    logits, dz_last, dmain = pl.pallas_call(
        conv_rest_kernel,
        out_shape=(
            jax.ShapeDtypeStruct(labels.shape, F32),
            jax.ShapeDtypeStruct((256, chan), BF),
            jax.ShapeDtypeStruct((3584, chan), BF),
        ),
        scratch_shapes=[pltpu.VMEM((1024, chan), BF)],
        compiler_params=params(),
        name="conv_rest",
    )(main, rim, w_conv, w_pred, labels, logits0, dz0)

    outgoing, tie = pl.pallas_call(
        take_kernel,
        out_shape=(pltpu.HBM((slots, chan), BF), tie_shape),
        grid=(slots // TAKE_BLOCK,),
        in_specs=[
            pl.BlockSpec(memory_space=pltpu.SMEM),
            whole((3584, chan)),
            whole((256, chan)),
            whole((256, chan)),
            whole(w_conv.shape),
        ],
        out_specs=(slot_spec(TAKE_BLOCK), tie_spec),
        scratch_shapes=[pltpu.VMEM((2 * CELLS + 8, 128), F32), pltpu.VMEM((2 * TAKE_BLOCK, 128), F32)],
        compiler_params=params(),
        name="take",
    )(place_twice, dmain, dz_last, dz_next, w_conv)
    returned = exchange(outgoing)

    picked, depth, row_line, slope = pl.pallas_call(
        again_kernel,
        out_shape=(
            pltpu.HBM((slots, chan), BF),
            jax.ShapeDtypeStruct((slots // GRAD_BLOCK, 1, GRAD_BLOCK), F32),
            jax.ShapeDtypeStruct((lines, 128), jnp.int32),
            jax.ShapeDtypeStruct((rows, bins), F32),
        ),
        grid=(slots // GRAD_BLOCK,),
        in_specs=[whole(features.shape), whole(wd_t.shape), table, table, tie_spec],
        out_specs=(
            slot_spec(GRAD_BLOCK),
            pl.BlockSpec((1, 1, GRAD_BLOCK), lambda i: (i, 0, 0)),
            whole((lines, 128)),
            whole((rows, bins)),
        ),
        scratch_shapes=[x_scratch, ids_scratch, pltpu.VMEM((lines, 128), jnp.int32), wide_scratch],
        compiler_params=params(),
        name="pick_again",
    )(features, wd_t, row_t, bin_t, tie)
    picked = pltpu.with_memory_space_constraint(picked, pltpu.HBM)

    grad = pl.pallas_call(
        grad_kernel,
        out_shape=jax.ShapeDtypeStruct((imgs, pix, chan), F32),
        grid=(slots // GRAD_BLOCK,),
        in_specs=[
            whole(wd_t.shape),
            whole((lines, 128)),
            table,
            pl.BlockSpec((1, 1, GRAD_BLOCK), lambda i: (i, 0, 0)),
            whole((rows, bins)),
            slot_spec(GRAD_BLOCK),
            slot_spec(GRAD_BLOCK),
        ],
        out_specs=whole((imgs, pix, chan)),
        scratch_shapes=[ids_scratch, pltpu.VMEM((rows, chan), F32), pltpu.VMEM((rows, 128), F32)],
        compiler_params=params(),
        name="grad",
    )(wd_t, row_line, bin_t, depth, slope, picked, returned)
    return logits, grad


def solution(mesh):
    in_specs = (
        P("cam", "tile", None),
        P(),
        P(),
        P(),
        P(("cam", "tile"), None, None),
        P(("cam", "tile"), None, None),
        P(("cam", "tile"), None, None),
        P(None, ("cam", "tile"), None),
    )
    out_specs = (P(None, ("cam", "tile"), None), P("cam", "tile", None))
    return jax.shard_map(
        per_device, mesh=mesh, in_specs=in_specs, out_specs=out_specs, check_vma=False
    )
```

```python
import jax
import jax.numpy as jnp
from jax import lax
from jax.experimental import pallas as pl
from jax.experimental.pallas import tpu as pltpu
from jax.sharding import PartitionSpec as P

loss_weight = 16.0
BF = jnp.bfloat16
F32 = jnp.float32
AXES = ("cam", "tile")
PICK_BLOCK = 2048
TAKE_BLOCK = 1024
GRAD_BLOCK = 1024
CELL_BLOCK = 512
CELLS = 4096
IMG_PAD = 48
VMEM_LIMIT = 48 * 1024 * 1024


def shifted(shard, by):
    devices = lax.axis_size(AXES)
    pairs = [(i, i + by) for i in range(devices) if 0 <= i + by < devices]
    return lax.ppermute(shard, AXES, pairs)


def dot(a, b):
    return jnp.dot(a, b, preferred_element_type=F32)


def dot_t(a, b):
    return lax.dot_general(a, b, (((1,), (1,)), ((), ())), preferred_element_type=F32)


def sigmoid(v):
    return 1.0 / (1.0 + jnp.exp(-v))


def padded_row(row):
    return row + 4 * ((row * 1490) >> 16)


def cell_place(cell):
    u = cell >> 9
    v = cell & 511
    col = v >> 1
    odd = v & 1
    half = (u >> 1) * 256 + col
    even_rows = odd * 1024 + half
    odd_rows = 2048 + odd * 768 + half
    last_row = 3584 + odd * 256 + col
    place = jnp.where((u & 1) == 0, even_rows, jnp.where(u == 7, last_row, odd_rows))
    return jnp.where(u >= 8, -1, place)


def splat_place(cell):
    u = cell >> 9
    v = cell & 511
    odd = v & 1
    line = ((u >> 1) & 1) * 256 + (v >> 1)
    early = 512 + (u & 1) * 1024 + odd * 512 + line
    late_even = 2560 + odd * 512 + line
    late_odd = 3584 + odd * 256 + (v >> 1)
    last_row = odd * 256 + (v >> 1)
    late = jnp.where((u & 1) == 0, late_even, jnp.where(u == 7, last_row, late_odd))
    return jnp.where(u >= 8, -1, jnp.where(u < 4, early, late))


def one_hot(mask):
    return jnp.where(mask, 1.0, 0.0).astype(BF)


def fill_rows(feat_ref, x_ref):
    for i in range(feat_ref.shape[0]):
        rows = feat_ref[i].astype(F32)
        rows = jnp.concatenate([rows, jnp.zeros((IMG_PAD - rows.shape[0], rows.shape[1]), F32)], axis=0)
        x_ref[i * IMG_PAD : (i + 1) * IMG_PAD, :] = rows.astype(BF)


def pick_rows(ids, x):
    groups, per = ids.shape
    rows = x.shape[0]
    chooser = one_hot(lax.broadcasted_iota(jnp.int32, (groups, per, rows), 2) == ids[:, :, None])
    return dot(chooser.reshape(groups * per, rows), x)


def pick_kernel(feat_ref, wd_ref, row_ref, bin_ref, pay_ref, tie_ref, x_ref, rid_ref, bid_ref):
    step = pl.program_id(0)

    @pl.when(step == 0)
    def _():
        fill_rows(feat_ref, x_ref)
        rid_ref[...] = padded_row(jnp.transpose(row_ref[...]))
        bid_ref[...] = jnp.transpose(bin_ref[...])
        tie_ref[...] = jnp.zeros_like(tie_ref)

    count = pay_ref.shape[0]
    per = rid_ref.shape[1]
    groups = count // per
    at = pl.ds(pl.multiple_of(step * groups, groups), groups)
    picked = pick_rows(rid_ref[at, :], x_ref[...])
    logits = dot_t(picked.astype(BF), wd_ref[...])
    bins = logits.shape[1]
    mask = lax.broadcasted_iota(jnp.int32, (groups, per, bins), 2) == bid_ref[at, :][:, :, None]
    chosen = jnp.sum(jnp.where(mask, logits.reshape(groups, per, bins), 0.0), axis=2, keepdims=True)
    pay_ref[...] = (sigmoid(chosen).reshape(count, 1) * picked).astype(BF)


def line_up(table_ref, wide_ref):
    per, partners = table_ref.shape
    wide_ref[:, 0:per] = jnp.transpose(table_ref[...])
    fold = 128 // per
    lane = lax.broadcasted_iota(jnp.int32, (partners // fold, 128), 1) // per
    out = jnp.zeros((partners // fold, 128), jnp.int32)
    for j in range(fold):
        part = wide_ref[pl.ds(j, partners // fold, stride=fold), :]
        if j:
            part = pltpu.roll(part, j * per, 1)
        out = jnp.where(lane == j, part, out)
    return out


def as_line(table):
    return jnp.concatenate([table[g : g + 1, :] for g in range(table.shape[0])], axis=1)


def places_kernel(cell_ref, tie_ref, line_ref, twice_ref, wide_ref):
    line_ref[...] = splat_place(line_up(cell_ref, wide_ref))
    place = cell_place(cell_ref[...])
    twice_ref[...] = 2 * jnp.where(place < 0, CELLS, place)


def again_kernel(feat_ref, wd_ref, row_ref, bin_ref, tie_ref, picked_ref, depth_ref, line_ref, slope_ref, x_ref, rid_ref, bid_ref, wide_ref):
    step = pl.program_id(0)

    @pl.when(step == 0)
    def _():
        fill_rows(feat_ref, x_ref)
        rid_ref[...] = padded_row(jnp.transpose(row_ref[...]))
        line_ref[...] = padded_row(line_up(row_ref, wide_ref))
        bid_ref[...] = line_up(bin_ref, wide_ref)
        prob = sigmoid(dot_t(x_ref[...], wd_ref[...]))
        slope_ref[...] = prob * (1.0 - prob)

    count = picked_ref.shape[0]
    groups = count // rid_ref.shape[1]
    at = pl.ds(pl.multiple_of(step * groups, groups), groups)
    picked = pick_rows(rid_ref[at, :], x_ref[...]).astype(BF)
    picked_ref[...] = picked
    logits = dot_t(wd_ref[...], picked)
    lines = count // 128
    bins = as_line(bid_ref[pl.ds(pl.multiple_of(step * lines, lines), lines), :])
    mask = lax.broadcasted_iota(jnp.int32, logits.shape, 0) == bins
    depth_ref[0] = sigmoid(jnp.sum(jnp.where(mask, logits, 0.0), axis=0, keepdims=True))


def splat_kernel(first, line_ref, val_ref, out_ref):
    rows = out_ref.shape[0]
    place = as_line(line_ref[...]) - (first + pl.program_id(0) * rows)
    placer = one_hot(lax.broadcasted_iota(jnp.int32, (rows, place.shape[1]), 0) == place)
    out_ref[...] = dot(placer, val_ref[...]).astype(BF)


def shift_down(v):
    col = lax.broadcasted_iota(jnp.int32, v.shape, 0) & 255
    return jnp.where(col == 0, 0.0, pltpu.roll(v, 1, 0))


def shift_up(v):
    n = v.shape[0]
    col = lax.broadcasted_iota(jnp.int32, v.shape, 0) & 255
    return jnp.where(col == 255, 0.0, pltpu.roll(v, n - 1, 0))


def conv_lines(ue, uo, ee, eo, oe, oo, w_ref, wp_ref, labels):
    z = dot(ue, w_ref[0, 1]) + dot(uo, w_ref[0, 2])
    z = z + dot(ee, w_ref[1, 1]) + dot(eo, w_ref[1, 2])
    z = z + dot(oe, w_ref[2, 1]) + dot(oo, w_ref[2, 2])
    z = z + shift_down(dot(uo, w_ref[0, 0]) + dot(eo, w_ref[1, 0]) + dot(oo, w_ref[2, 0]))
    s = sigmoid(z)
    act = (z * s).astype(BF)
    logits = dot_t(wp_ref[...], act)
    dlogit = (loss_weight * (sigmoid(logits) - labels.astype(F32))).astype(BF)
    grad_act = lax.dot_general(dlogit, wp_ref[...], (((0,), (0,)), ((), ())), preferred_element_type=F32)
    return logits, (grad_act * (s * (1.0 + z * (1.0 - s)))).astype(BF)


def conv_first_kernel(early_ref, halo_ref, w_ref, wp_ref, lab_ref, logit_ref, dz_ref):
    logits, dz = conv_lines(
        halo_ref[0:256, :],
        halo_ref[256:512, :],
        early_ref[0:256, :],
        early_ref[512:768, :],
        early_ref[1024:1280, :],
        early_ref[1536:1792, :],
        w_ref,
        wp_ref,
        lab_ref[:, 0, :],
    )
    logit_ref[...] = logits
    dz_ref[...] = dz


def stack(*parts):
    return jnp.concatenate(parts, axis=0)


def conv_rest_kernel(
    early_ref, late_ref, rim_ref, w_ref, wp_ref, lab_ref, first_ref, dzf_ref, logit_ref, last_ref, out_ref, dz_ref
):
    logit_ref[:, 0, :] = first_ref[...]
    dz_ref[0:256, :] = dzf_ref[...]
    logits, dz = conv_lines(
        stack(early_ref[1024:1536, :], late_ref[1024:1280, :]),
        stack(early_ref[1536:2048, :], late_ref[1280:1536, :]),
        stack(early_ref[256:512, :], late_ref[0:512, :]),
        stack(early_ref[768:1024, :], late_ref[512:1024, :]),
        stack(early_ref[1280:1536, :], late_ref[1024:1280, :], rim_ref[0:256, :]),
        stack(early_ref[1792:2048, :], late_ref[1280:1536, :], rim_ref[256:512, :]),
        w_ref,
        wp_ref,
        jnp.concatenate([lab_ref[:, i, :] for i in range(1, 4)], axis=1),
    )
    for i in range(1, 4):
        logit_ref[:, i, :] = logits[:, (i - 1) * 256 : i * 256]
    dz_ref[256:1024, :] = dz
    last_ref[...] = dz[512:768, :]
    dz = dz_ref[...]
    dzs = shift_up(dz.astype(F32)).astype(BF)
    out_ref[0:1024, :] = dot_t(dz, w_ref[1, 1]).astype(BF)
    out_ref[1024:2048, :] = (dot_t(dz, w_ref[1, 2]) + dot_t(dzs, w_ref[1, 0])).astype(BF)
    out_ref[2048:2816, :] = (dot_t(dz[0:768], w_ref[2, 1]) + dot_t(dz[256:1024], w_ref[0, 1])).astype(BF)
    out_ref[2816:3584, :] = (
        dot_t(dz[0:768], w_ref[2, 2])
        + dot_t(dzs[0:768], w_ref[2, 0])
        + dot_t(dz[256:1024], w_ref[0, 2])
        + dot_t(dzs[256:1024], w_ref[0, 0])
    ).astype(BF)


def take_kernel(twice_ref, main_ref, dz_ref, halo_ref, w_ref, out_ref, tie_ref, src_ref, dst_ref):
    step = pl.program_id(0)

    @pl.when(step == 0)
    def _():
        def put(first, rows):
            src_ref[pl.ds(2 * first, rows.shape[0], stride=2), :] = rows[:, :128]
            src_ref[pl.ds(2 * first + 1, rows.shape[0], stride=2), :] = rows[:, 128:]

        put(0, main_ref[...].astype(F32))
        dz = dz_ref[...]
        dzs = shift_up(dz.astype(F32)).astype(BF)
        dn = halo_ref[...]
        dns = shift_up(dn.astype(F32)).astype(BF)
        put(3584, (dot_t(dz, w_ref[2, 1]) + dot_t(dn, w_ref[0, 1])).astype(BF).astype(F32))
        rim_odd = dot_t(dz, w_ref[2, 2]) + dot_t(dzs, w_ref[2, 0]) + dot_t(dn, w_ref[0, 2]) + dot_t(dns, w_ref[0, 0])
        put(3840, rim_odd.astype(BF).astype(F32))
        src_ref[2 * CELLS : 2 * CELLS + 8, :] = jnp.zeros((8, 128), F32)
        tie_ref[...] = jnp.zeros_like(tie_ref)

    count = out_ref.shape[0]
    per = twice_ref.shape[0]
    groups = count // per

    def one(g, carry):
        rows = dst_ref.at[pl.ds(pl.multiple_of(g * (2 * per), 2 * per), 2 * per), :]
        for k in range(per):
            at = pl.multiple_of(twice_ref[k, step * groups + g], 2)
            rows[2 * k : 2 * k + 2, :] = src_ref[pl.ds(at, 2), :]
        return carry

    lax.fori_loop(0, groups, one, 0)
    out_ref[:, :128] = dst_ref[pl.ds(0, count, stride=2), :].astype(BF)
    out_ref[:, 128:] = dst_ref[pl.ds(1, count, stride=2), :].astype(BF)


def grad_kernel(wd_ref, line_ref, bin_ref, depth_ref, slope_ref, picked_ref, inc_ref, out_ref, bid_ref, acc_ref, accd_ref):
    step = pl.program_id(0)

    @pl.when(step == 0)
    def _():
        bid_ref[...] = jnp.transpose(bin_ref[...])
        acc_ref[...] = jnp.zeros_like(acc_ref)
        accd_ref[...] = jnp.zeros_like(accd_ref)

    rows = acc_ref.shape[0]
    inc = inc_ref[...]
    count = inc.shape[0]
    per = bid_ref.shape[1]
    groups = count // per
    terms = picked_ref[...].astype(F32) * inc.astype(F32)
    terms = terms[:, :128] + terms[:, 128:]
    high = terms.astype(BF)
    halves = jnp.concatenate([high, (terms - high.astype(F32)).astype(BF)], axis=1)
    inner = dot(halves, jnp.ones((256, 128), BF)).reshape(groups, per, 128)
    at = pl.ds(pl.multiple_of(step * groups, groups), groups)
    mask = (lax.broadcasted_iota(jnp.int32, (groups, per, 128), 2) & 63) == bid_ref[at, :][:, :, None]
    binned = jnp.where(mask, inner, 0.0).reshape(count, 128)
    high = binned.astype(BF).astype(F32)
    lane = lax.broadcasted_iota(jnp.int32, (count, 128), 1)
    both = jnp.where(lane < 64, high, binned - high).astype(BF)
    lines = count // 128
    hot = lax.broadcasted_iota(jnp.int32, (rows, count), 0) == as_line(
        line_ref[pl.ds(pl.multiple_of(step * lines, lines), lines), :]
    )
    acc_ref[...] += dot(jnp.where(hot, depth_ref[0], 0.0).astype(BF), inc)
    accd_ref[...] += dot(one_hot(hot), both)

    @pl.when(step == pl.num_programs(0) - 1)
    def _():
        sums = accd_ref[...]
        grad_logit = (slope_ref[...] * (sums[:, :64] + sums[:, 64:])).astype(BF)
        total = acc_ref[...] + dot(grad_logit, wd_ref[...])
        for i in range(out_ref.shape[0]):
            out_ref[i] = total[i * IMG_PAD : i * IMG_PAD + out_ref.shape[1], :]


def params():
    return pltpu.CompilerParams(vmem_limit_bytes=VMEM_LIMIT)


def whole(shape):
    return pl.BlockSpec(shape, lambda i: (0,) * len(shape))


def per_device(features, w_depth, w_conv, w_pred, send_row, send_bin, recv_cell, labels):
    imgs, pix, chan = features.shape
    sources, cap = send_row.shape[1], send_row.shape[2]
    slots = sources * cap
    rows = imgs * IMG_PAD
    row_t = jnp.transpose(send_row.reshape(sources, cap))
    bin_t = jnp.transpose(send_bin.reshape(sources, cap))
    cell_t = jnp.transpose(recv_cell.reshape(sources, cap))
    wd_t = jnp.transpose(w_depth)
    bins = wd_t.shape[0]
    table = whole((cap, sources))
    lines = slots // 128
    ids_scratch = pltpu.VMEM((sources, cap), jnp.int32)
    wide_scratch = pltpu.VMEM((sources, 128), jnp.int32)
    x_scratch = pltpu.VMEM((rows, chan), BF)
    tie_spec = whole((8, 128))
    tie_shape = jax.ShapeDtypeStruct((8, 128), F32)

    def slot_spec(block):
        return pl.BlockSpec((block, chan), lambda i: (i, 0))

    def exchange(v):
        out = lax.all_to_all(v.reshape(sources, cap, chan), AXES, split_axis=0, concat_axis=0, tiled=True)
        return out.reshape(slots, chan)

    payload, tie = pl.pallas_call(
        pick_kernel,
        out_shape=(pltpu.HBM((slots, chan), BF), tie_shape),
        grid=(slots // PICK_BLOCK,),
        in_specs=[whole(features.shape), whole(wd_t.shape), table, table],
        out_specs=(slot_spec(PICK_BLOCK), tie_spec),
        scratch_shapes=[x_scratch, ids_scratch, ids_scratch],
        compiler_params=params(),
        name="pick",
    )(*(pltpu.with_memory_space_constraint(v, pltpu.HBM) for v in (features, wd_t, row_t, bin_t)))
    arrived = exchange(payload)

    place_line, place_twice = pl.pallas_call(
        places_kernel,
        out_shape=(
            jax.ShapeDtypeStruct((lines, 128), jnp.int32),
            jax.ShapeDtypeStruct((cap, sources), jnp.int32),
        ),
        grid=(1,),
        in_specs=[table, tie_spec],
        out_specs=(whole((lines, 128)), table),
        scratch_shapes=[wide_scratch],
        compiler_params=params(),
        name="places",
    )(cell_t, tie)

    def splat(first, count, name, line):
        return pl.pallas_call(
            lambda *refs: splat_kernel(first, *refs),
            out_shape=jax.ShapeDtypeStruct((count, chan), BF),
            grid=(count // CELL_BLOCK,),
            in_specs=[whole((lines, 128)), whole((slots, chan))],
            out_specs=pl.BlockSpec((CELL_BLOCK, chan), lambda i: (i, 0)),
            compiler_params=params(),
            name=name,
        )(line, arrived)

    rim = splat(0, 512, "splat_rim", place_line)
    halo = shifted(rim, 1)
    line_b, _ = lax.optimization_barrier((place_line, rim))
    early = splat(512, 2048, "splat_early", line_b)
    logits0, dz0 = pl.pallas_call(
        conv_first_kernel,
        out_shape=(jax.ShapeDtypeStruct((w_pred.shape[0], 256), F32), jax.ShapeDtypeStruct((256, chan), BF)),
        compiler_params=params(),
        name="conv_first",
    )(early, halo, w_conv, w_pred, labels)
    dz_next = shifted(dz0, -1)
    line_c, _ = lax.optimization_barrier((place_line, dz0))
    late = splat(2560, 1536, "splat_late", line_c)
    logits, dz_last, dmain = pl.pallas_call(
        conv_rest_kernel,
        out_shape=(
            jax.ShapeDtypeStruct(labels.shape, F32),
            jax.ShapeDtypeStruct((256, chan), BF),
            jax.ShapeDtypeStruct((3584, chan), BF),
        ),
        scratch_shapes=[pltpu.VMEM((1024, chan), BF)],
        compiler_params=params(),
        name="conv_rest",
    )(early, late, rim, w_conv, w_pred, labels, logits0, dz0)

    outgoing, tie = pl.pallas_call(
        take_kernel,
        out_shape=(pltpu.HBM((slots, chan), BF), tie_shape),
        grid=(slots // TAKE_BLOCK,),
        in_specs=[
            pl.BlockSpec(memory_space=pltpu.SMEM),
            whole((3584, chan)),
            whole((256, chan)),
            whole((256, chan)),
            whole(w_conv.shape),
        ],
        out_specs=(slot_spec(TAKE_BLOCK), tie_spec),
        scratch_shapes=[pltpu.VMEM((2 * CELLS + 8, 128), F32), pltpu.VMEM((2 * TAKE_BLOCK, 128), F32)],
        compiler_params=params(),
        name="take",
    )(place_twice, dmain, dz_last, dz_next, w_conv)
    returned = exchange(outgoing)

    picked, depth, row_line, slope = pl.pallas_call(
        again_kernel,
        out_shape=(
            pltpu.HBM((slots, chan), BF),
            jax.ShapeDtypeStruct((slots // GRAD_BLOCK, 1, GRAD_BLOCK), F32),
            jax.ShapeDtypeStruct((lines, 128), jnp.int32),
            jax.ShapeDtypeStruct((rows, bins), F32),
        ),
        grid=(slots // GRAD_BLOCK,),
        in_specs=[whole(features.shape), whole(wd_t.shape), table, table, tie_spec],
        out_specs=(
            slot_spec(GRAD_BLOCK),
            pl.BlockSpec((1, 1, GRAD_BLOCK), lambda i: (i, 0, 0)),
            whole((lines, 128)),
            whole((rows, bins)),
        ),
        scratch_shapes=[x_scratch, ids_scratch, pltpu.VMEM((lines, 128), jnp.int32), wide_scratch],
        compiler_params=params(),
        name="pick_again",
    )(features, wd_t, row_t, bin_t, tie)
    picked = pltpu.with_memory_space_constraint(picked, pltpu.HBM)

    grad = pl.pallas_call(
        grad_kernel,
        out_shape=jax.ShapeDtypeStruct((imgs, pix, chan), F32),
        grid=(slots // GRAD_BLOCK,),
        in_specs=[
            whole(wd_t.shape),
            whole((lines, 128)),
            table,
            pl.BlockSpec((1, 1, GRAD_BLOCK), lambda i: (i, 0, 0)),
            whole((rows, bins)),
            slot_spec(GRAD_BLOCK),
            slot_spec(GRAD_BLOCK),
        ],
        out_specs=whole((imgs, pix, chan)),
        scratch_shapes=[ids_scratch, pltpu.VMEM((rows, chan), F32), pltpu.VMEM((rows, 128), F32)],
        compiler_params=params(),
        name="grad",
    )(wd_t, row_line, bin_t, depth, slope, picked, returned)
    return logits, grad


def solution(mesh):
    in_specs = (
        P("cam", "tile", None),
        P(),
        P(),
        P(),
        P(("cam", "tile"), None, None),
        P(("cam", "tile"), None, None),
        P(("cam", "tile"), None, None),
        P(None, ("cam", "tile"), None),
    )
    out_specs = (P(None, ("cam", "tile"), None), P("cam", "tile", None))
    return jax.shard_map(
        per_device, mesh=mesh, in_specs=in_specs, out_specs=out_specs, check_vma=False
    )
```

```python
import jax
import jax.numpy as jnp
from jax import lax
from jax.experimental import pallas as pl
from jax.experimental.pallas import tpu as pltpu
from jax.sharding import PartitionSpec as P

loss_weight = 16.0
BF = jnp.bfloat16
F32 = jnp.float32
AXES = ("cam", "tile")
PICK_BLOCK = 2048
TAKE_BLOCK = 1024
TAKE_UNROLL = 4
GRAD_BLOCK = 2048
EARLY_ROWS = 5
CELL_BLOCK = 512
CELLS = 4096
IMG_PAD = 48
VMEM_LIMIT = 48 * 1024 * 1024


def shifted(shard, by):
    devices = lax.axis_size(AXES)
    pairs = [(i, i + by) for i in range(devices) if 0 <= i + by < devices]
    return lax.ppermute(shard, AXES, pairs)


def dot(a, b):
    return jnp.dot(a, b, preferred_element_type=F32)


def dot_t(a, b):
    return lax.dot_general(a, b, (((1,), (1,)), ((), ())), preferred_element_type=F32)


def sigmoid(v):
    return 1.0 / (1.0 + jnp.exp(-v))


def padded_row(row):
    return row + 4 * ((row * 1490) >> 16)


def cell_place(cell):
    u = cell >> 9
    v = cell & 511
    col = v >> 1
    odd = v & 1
    half = (u >> 1) * 256 + col
    even_rows = odd * 1024 + half
    odd_rows = 2048 + odd * 768 + half
    last_row = 3584 + odd * 256 + col
    place = jnp.where((u & 1) == 0, even_rows, jnp.where(u == 7, last_row, odd_rows))
    return jnp.where(u >= 8, -1, place)


def splat_place(cell):
    u = cell >> 9
    v = cell & 511
    return jnp.where(u >= 8, -1, ((u + 1) & 7) * 512 + (v & 1) * 256 + (v >> 1))


def one_hot(mask):
    return jnp.where(mask, 1.0, 0.0).astype(BF)


def row_hot(rows, ids):
    hot = lax.broadcasted_iota(jnp.int16, (rows, ids.shape[1]), 0) == ids.astype(jnp.int16)
    return jnp.where(hot, jnp.ones((), BF), jnp.zeros((), BF))


def fill_rows(feat_ref, x_ref):
    for i in range(feat_ref.shape[0]):
        rows = feat_ref[i].astype(F32)
        rows = jnp.concatenate([rows, jnp.zeros((IMG_PAD - rows.shape[0], rows.shape[1]), F32)], axis=0)
        x_ref[i * IMG_PAD : (i + 1) * IMG_PAD, :] = rows.astype(BF)


def pick_rows(ids, x):
    groups, per = ids.shape
    rows = x.shape[0]
    chooser = one_hot(lax.broadcasted_iota(jnp.int32, (groups, per, rows), 2) == ids[:, :, None])
    return dot(chooser.reshape(groups * per, rows), x)


def pick_kernel(feat_ref, wd_ref, row_ref, bin_ref, pay_ref, tie_ref, x_ref, rid_ref, bid_ref):
    step = pl.program_id(0)

    @pl.when(step == 0)
    def _():
        fill_rows(feat_ref, x_ref)
        rid_ref[...] = padded_row(jnp.transpose(row_ref[...]))
        bid_ref[...] = jnp.transpose(bin_ref[...])
        tie_ref[...] = jnp.zeros_like(tie_ref)

    count = pay_ref.shape[0]
    per = rid_ref.shape[1]
    groups = count // per
    at = pl.ds(pl.multiple_of(step * groups, groups), groups)
    picked = pick_rows(rid_ref[at, :], x_ref[...])
    logits = dot_t(picked.astype(BF), wd_ref[...])
    bins = logits.shape[1]
    mask = lax.broadcasted_iota(jnp.int32, (groups, per, bins), 2) == bid_ref[at, :][:, :, None]
    chosen = jnp.sum(jnp.where(mask, logits.reshape(groups, per, bins), 0.0), axis=2, keepdims=True)
    pay_ref[...] = (sigmoid(chosen).reshape(count, 1) * picked).astype(BF)


def line_up(table_ref, wide_ref):
    per, partners = table_ref.shape
    wide_ref[:, 0:per] = jnp.transpose(table_ref[...])
    fold = 128 // per
    lane = lax.broadcasted_iota(jnp.int32, (partners // fold, 128), 1) // per
    out = jnp.zeros((partners // fold, 128), jnp.int32)
    for j in range(fold):
        part = wide_ref[pl.ds(j, partners // fold, stride=fold), :]
        if j:
            part = pltpu.roll(part, j * per, 1)
        out = jnp.where(lane == j, part, out)
    return out


def as_line(table):
    return jnp.concatenate([table[g : g + 1, :] for g in range(table.shape[0])], axis=1)


def places_kernel(cell_ref, tie_ref, line_ref, twice_ref, wide_ref):
    line_ref[...] = splat_place(line_up(cell_ref, wide_ref))
    place = cell_place(cell_ref[...])
    twice_ref[...] = 2 * jnp.where(place < 0, CELLS, place)


def again_kernel(feat_ref, wd_ref, row_ref, bin_ref, tie_ref, picked_ref, depth_ref, line_ref, slope_ref, x_ref, rid_ref, bid_ref, wide_ref):
    step = pl.program_id(0)

    @pl.when(step == 0)
    def _():
        fill_rows(feat_ref, x_ref)
        rid_ref[...] = padded_row(jnp.transpose(row_ref[...]))
        line_ref[...] = padded_row(line_up(row_ref, wide_ref))
        bid_ref[...] = line_up(bin_ref, wide_ref)
        prob = sigmoid(dot_t(x_ref[...], wd_ref[...]))
        slope_ref[...] = prob * (1.0 - prob)

    count = picked_ref.shape[0]
    groups = count // rid_ref.shape[1]
    at = pl.ds(pl.multiple_of(step * groups, groups), groups)
    picked = pick_rows(rid_ref[at, :], x_ref[...]).astype(BF)
    picked_ref[...] = picked
    logits = dot_t(wd_ref[...], picked)
    lines = count // 128
    bins = as_line(bid_ref[pl.ds(pl.multiple_of(step * lines, lines), lines), :])
    mask = lax.broadcasted_iota(jnp.int32, logits.shape, 0) == bins
    depth_ref[0] = sigmoid(jnp.sum(jnp.where(mask, logits, 0.0), axis=0, keepdims=True))


def splat_kernel(first, line_ref, val_ref, out_ref):
    rows = out_ref.shape[0]
    place = as_line(line_ref[...]) - (first + pl.program_id(0) * rows)
    placer = one_hot(lax.broadcasted_iota(jnp.int32, (rows, place.shape[1]), 0) == place)
    out_ref[...] = dot(placer, val_ref[...]).astype(BF)


def shift_down(v):
    col = lax.broadcasted_iota(jnp.int32, v.shape, 0) & 255
    return jnp.where(col == 0, 0.0, pltpu.roll(v, 1, 0))


def shift_up(v):
    n = v.shape[0]
    col = lax.broadcasted_iota(jnp.int32, v.shape, 0) & 255
    return jnp.where(col == 255, 0.0, pltpu.roll(v, n - 1, 0))


def top_taps(ue, uo, w):
    return dot(ue, w[1]) + dot(uo, w[2]) + shift_down(dot(uo, w[0]))


def top_kernel(rim_ref, w_ref, out_ref):
    out_ref[...] = top_taps(rim_ref[0:256, :], rim_ref[256:512, :], w_ref).astype(BF)


def conv_lines(above, ee, eo, oe, oo, w_ref, wp_ref, labels):
    z = dot(ee, w_ref[1, 1]) + dot(eo, w_ref[1, 2])
    z = z + dot(oe, w_ref[2, 1]) + dot(oo, w_ref[2, 2])
    z = z + shift_down(dot(eo, w_ref[1, 0]) + dot(oo, w_ref[2, 0])) + above
    s = sigmoid(z)
    act = (z * s).astype(BF)
    logits = dot_t(wp_ref[...], act)
    dlogit = (loss_weight * (sigmoid(logits) - labels.astype(F32))).astype(BF)
    grad_act = lax.dot_general(dlogit, wp_ref[...], (((0,), (0,)), ((), ())), preferred_element_type=F32)
    return logits, (grad_act * (s * (1.0 + z * (1.0 - s)))).astype(BF)


def conv_first_kernel(early_ref, halo_ref, w_ref, wp_ref, lab_ref, logit_ref, dz_ref):
    logits, dz = conv_lines(
        halo_ref[...].astype(F32),
        early_ref[0:256, :],
        early_ref[256:512, :],
        early_ref[512:768, :],
        early_ref[768:1024, :],
        w_ref,
        wp_ref,
        lab_ref[:, 0, :],
    )
    logit_ref[...] = logits
    dz_ref[...] = dz


def conv_rest_kernel(
    early_ref, late_ref, rim_ref, w_ref, wp_ref, lab_ref, first_ref, dzf_ref, logit_ref, last_ref, out_ref, dz_ref
):
    logit_ref[:, 0, :] = first_ref[...]
    dz_ref[0:256, :] = dzf_ref[...]
    early_rows = early_ref.shape[0] // 512

    def half(odd, *grid_rows):
        parts = []
        for u in grid_rows:
            ref, at = (early_ref, u) if u < early_rows else (late_ref, u - early_rows) if u < 7 else (rim_ref, 0)
            at = at * 512 + odd * 256
            parts.append(ref[at : at + 256, :])
        return jnp.concatenate(parts, axis=0)

    logits, dz = conv_lines(
        top_taps(half(0, 1, 3, 5), half(1, 1, 3, 5), w_ref.at[0]),
        half(0, 2, 4, 6),
        half(1, 2, 4, 6),
        half(0, 3, 5, 7),
        half(1, 3, 5, 7),
        w_ref,
        wp_ref,
        jnp.concatenate([lab_ref[:, i, :] for i in range(1, 4)], axis=1),
    )
    for i in range(1, 4):
        logit_ref[:, i, :] = logits[:, (i - 1) * 256 : i * 256]
    dz_ref[256:1024, :] = dz
    last_ref[...] = dz[512:768, :]
    dz = dz_ref[...]
    dzs = shift_up(dz.astype(F32)).astype(BF)
    out_ref[0:1024, :] = dot_t(dz, w_ref[1, 1]).astype(BF)
    out_ref[1024:2048, :] = (dot_t(dz, w_ref[1, 2]) + dot_t(dzs, w_ref[1, 0])).astype(BF)
    out_ref[2048:2816, :] = (dot_t(dz[0:768], w_ref[2, 1]) + dot_t(dz[256:1024], w_ref[0, 1])).astype(BF)
    out_ref[2816:3584, :] = (
        dot_t(dz[0:768], w_ref[2, 2])
        + dot_t(dzs[0:768], w_ref[2, 0])
        + dot_t(dz[256:1024], w_ref[0, 2])
        + dot_t(dzs[256:1024], w_ref[0, 0])
    ).astype(BF)


def take_kernel(twice_ref, main_ref, dz_ref, halo_ref, w_ref, out_ref, tie_ref, src_ref, dst_ref):
    step = pl.program_id(0)

    @pl.when(step == 0)
    def _():
        def put(first, rows):
            src_ref[pl.ds(2 * first, rows.shape[0], stride=2), :] = rows[:, :128]
            src_ref[pl.ds(2 * first + 1, rows.shape[0], stride=2), :] = rows[:, 128:]

        put(0, main_ref[...].astype(F32))
        dz = dz_ref[...]
        dzs = shift_up(dz.astype(F32)).astype(BF)
        dn = halo_ref[...]
        dns = shift_up(dn.astype(F32)).astype(BF)
        put(3584, (dot_t(dz, w_ref[2, 1]) + dot_t(dn, w_ref[0, 1])).astype(BF).astype(F32))
        rim_odd = dot_t(dz, w_ref[2, 2]) + dot_t(dzs, w_ref[2, 0]) + dot_t(dn, w_ref[0, 2]) + dot_t(dns, w_ref[0, 0])
        put(3840, rim_odd.astype(BF).astype(F32))
        src_ref[2 * CELLS : 2 * CELLS + 8, :] = jnp.zeros((8, 128), F32)
        tie_ref[...] = jnp.zeros_like(tie_ref)

    count = out_ref.shape[0]
    per = twice_ref.shape[0]
    groups = count // per

    turn = 2 * per * TAKE_UNROLL

    def some(g, carry):
        rows = dst_ref.at[pl.ds(pl.multiple_of(g * turn, turn), turn), :]
        for j in range(TAKE_UNROLL):
            for k in range(per):
                at = pl.multiple_of(twice_ref[k, step * groups + g * TAKE_UNROLL + j], 2)
                to = 2 * (j * per + k)
                rows[to : to + 2, :] = src_ref[pl.ds(at, 2), :]
        return carry

    lax.fori_loop(0, groups // TAKE_UNROLL, some, 0)
    out_ref[:, :128] = dst_ref[pl.ds(0, count, stride=2), :].astype(BF)
    out_ref[:, 128:] = dst_ref[pl.ds(1, count, stride=2), :].astype(BF)


def grad_kernel(wd_ref, line_ref, bin_ref, depth_ref, slope_ref, picked_ref, inc_ref, out_ref, bid_ref, acc_ref, accd_ref):
    step = pl.program_id(0)

    @pl.when(step == 0)
    def _():
        bid_ref[...] = jnp.transpose(bin_ref[...])
        acc_ref[...] = jnp.zeros_like(acc_ref)
        accd_ref[...] = jnp.zeros_like(accd_ref)

    rows = acc_ref.shape[0]
    inc = inc_ref[...]
    count = inc.shape[0]
    per = bid_ref.shape[1]
    groups = count // per
    terms = picked_ref[...].astype(F32) * inc.astype(F32)
    terms = terms[:, :128] + terms[:, 128:]
    high = terms.astype(BF)
    halves = jnp.concatenate([high, (terms - high.astype(F32)).astype(BF)], axis=1)
    inner = dot(halves, jnp.ones((256, 128), BF)).reshape(groups, per, 128)
    at = pl.ds(pl.multiple_of(step * groups, groups), groups)
    mask = (lax.broadcasted_iota(jnp.int32, (groups, per, 128), 2) & 63) == bid_ref[at, :][:, :, None]
    binned = jnp.where(mask, inner, 0.0).reshape(count, 128)
    high = binned.astype(BF).astype(F32)
    lane = lax.broadcasted_iota(jnp.int32, (count, 128), 1)
    both = jnp.where(lane < 64, high, binned - high).astype(BF)
    lines = count // 128
    chooser = row_hot(rows, as_line(line_ref[pl.ds(pl.multiple_of(step * lines, lines), lines), :]))
    acc_ref[...] += dot(chooser * depth_ref[0].astype(BF), inc)
    accd_ref[...] += dot(chooser, both)

    @pl.when(step == pl.num_programs(0) - 1)
    def _():
        sums = accd_ref[...]
        grad_logit = (slope_ref[...] * (sums[:, :64] + sums[:, 64:])).astype(BF)
        total = acc_ref[...] + dot(grad_logit, wd_ref[...])
        for i in range(out_ref.shape[0]):
            out_ref[i] = total[i * IMG_PAD : i * IMG_PAD + out_ref.shape[1], :]


def params():
    return pltpu.CompilerParams(vmem_limit_bytes=VMEM_LIMIT)


def whole(shape):
    return pl.BlockSpec(shape, lambda i: (0,) * len(shape))


def per_device(features, w_depth, w_conv, w_pred, send_row, send_bin, recv_cell, labels):
    imgs, pix, chan = features.shape
    sources, cap = send_row.shape[1], send_row.shape[2]
    slots = sources * cap
    rows = imgs * IMG_PAD
    row_t = jnp.transpose(send_row.reshape(sources, cap))
    bin_t = jnp.transpose(send_bin.reshape(sources, cap))
    cell_t = jnp.transpose(recv_cell.reshape(sources, cap))
    wd_t = jnp.transpose(w_depth)
    bins = wd_t.shape[0]
    table = whole((cap, sources))
    lines = slots // 128
    ids_scratch = pltpu.VMEM((sources, cap), jnp.int32)
    wide_scratch = pltpu.VMEM((sources, 128), jnp.int32)
    x_scratch = pltpu.VMEM((rows, chan), BF)
    tie_spec = whole((8, 128))
    tie_shape = jax.ShapeDtypeStruct((8, 128), F32)

    def slot_spec(block):
        return pl.BlockSpec((block, chan), lambda i: (i, 0))

    def exchange(v):
        out = lax.all_to_all(v.reshape(sources, cap, chan), AXES, split_axis=0, concat_axis=0, tiled=True)
        return out.reshape(slots, chan)

    payload, tie = pl.pallas_call(
        pick_kernel,
        out_shape=(pltpu.HBM((slots, chan), BF), tie_shape),
        grid=(slots // PICK_BLOCK,),
        in_specs=[whole(features.shape), whole(wd_t.shape), table, table],
        out_specs=(slot_spec(PICK_BLOCK), tie_spec),
        scratch_shapes=[x_scratch, ids_scratch, ids_scratch],
        compiler_params=params(),
        name="pick",
    )(*(pltpu.with_memory_space_constraint(v, pltpu.HBM) for v in (features, wd_t, row_t, bin_t)))
    arrived = exchange(payload)

    place_line, place_twice = pl.pallas_call(
        places_kernel,
        out_shape=(
            jax.ShapeDtypeStruct((lines, 128), jnp.int32),
            jax.ShapeDtypeStruct((cap, sources), jnp.int32),
        ),
        grid=(1,),
        in_specs=[table, tie_spec],
        out_specs=(whole((lines, 128)), table),
        scratch_shapes=[wide_scratch],
        compiler_params=params(),
        name="places",
    )(cell_t, tie)

    def splat(first, count, name, line):
        return pl.pallas_call(
            lambda *refs: splat_kernel(first, *refs),
            out_shape=jax.ShapeDtypeStruct((count, chan), BF),
            grid=(count // CELL_BLOCK,),
            in_specs=[whole((lines, 128)), whole((slots, chan))],
            out_specs=pl.BlockSpec((CELL_BLOCK, chan), lambda i: (i, 0)),
            compiler_params=params(),
            name=name,
        )(line, arrived)

    rim = splat(0, 512, "splat_rim", place_line)
    top = pl.pallas_call(
        top_kernel,
        out_shape=jax.ShapeDtypeStruct((256, chan), BF),
        compiler_params=params(),
        name="top",
    )(rim, w_conv[0])
    halo = shifted(top, 1)
    split = 512 * (1 + EARLY_ROWS)
    line_b, _ = lax.optimization_barrier((place_line, top))
    early = splat(512, split - 512, "splat_early", line_b)
    logits0, dz0 = pl.pallas_call(
        conv_first_kernel,
        out_shape=(jax.ShapeDtypeStruct((w_pred.shape[0], 256), F32), jax.ShapeDtypeStruct((256, chan), BF)),
        compiler_params=params(),
        name="conv_first",
    )(early, halo, w_conv, w_pred, labels)
    dz_next = shifted(dz0, -1)
    line_c, _ = lax.optimization_barrier((place_line, dz0))
    late = splat(split, CELLS - split, "splat_late", line_c)
    logits, dz_last, dmain = pl.pallas_call(
        conv_rest_kernel,
        out_shape=(
            jax.ShapeDtypeStruct(labels.shape, F32),
            jax.ShapeDtypeStruct((256, chan), BF),
            jax.ShapeDtypeStruct((3584, chan), BF),
        ),
        scratch_shapes=[pltpu.VMEM((1024, chan), BF)],
        compiler_params=params(),
        name="conv_rest",
    )(early, late, rim, w_conv, w_pred, labels, logits0, dz0)

    outgoing, tie = pl.pallas_call(
        take_kernel,
        out_shape=(pltpu.HBM((slots, chan), BF), tie_shape),
        grid=(slots // TAKE_BLOCK,),
        in_specs=[
            pl.BlockSpec(memory_space=pltpu.SMEM),
            whole((3584, chan)),
            whole((256, chan)),
            whole((256, chan)),
            whole(w_conv.shape),
        ],
        out_specs=(slot_spec(TAKE_BLOCK), tie_spec),
        scratch_shapes=[pltpu.VMEM((2 * CELLS + 8, 128), F32), pltpu.VMEM((2 * TAKE_BLOCK, 128), F32)],
        compiler_params=params(),
        name="take",
    )(place_twice, dmain, dz_last, dz_next, w_conv)
    returned = exchange(outgoing)

    picked, depth, row_line, slope = pl.pallas_call(
        again_kernel,
        out_shape=(
            pltpu.HBM((slots, chan), BF),
            jax.ShapeDtypeStruct((slots // GRAD_BLOCK, 1, GRAD_BLOCK), F32),
            jax.ShapeDtypeStruct((lines, 128), jnp.int32),
            jax.ShapeDtypeStruct((rows, bins), F32),
        ),
        grid=(slots // GRAD_BLOCK,),
        in_specs=[whole(features.shape), whole(wd_t.shape), table, table, tie_spec],
        out_specs=(
            slot_spec(GRAD_BLOCK),
            pl.BlockSpec((1, 1, GRAD_BLOCK), lambda i: (i, 0, 0)),
            whole((lines, 128)),
            whole((rows, bins)),
        ),
        scratch_shapes=[x_scratch, ids_scratch, pltpu.VMEM((lines, 128), jnp.int32), wide_scratch],
        compiler_params=params(),
        name="pick_again",
    )(features, wd_t, row_t, bin_t, tie)
    picked = pltpu.with_memory_space_constraint(picked, pltpu.HBM)

    grad = pl.pallas_call(
        grad_kernel,
        out_shape=jax.ShapeDtypeStruct((imgs, pix, chan), F32),
        grid=(slots // GRAD_BLOCK,),
        in_specs=[
            whole(wd_t.shape),
            whole((lines, 128)),
            table,
            pl.BlockSpec((1, 1, GRAD_BLOCK), lambda i: (i, 0, 0)),
            whole((rows, bins)),
            slot_spec(GRAD_BLOCK),
            slot_spec(GRAD_BLOCK),
        ],
        out_specs=whole((imgs, pix, chan)),
        scratch_shapes=[ids_scratch, pltpu.VMEM((rows, chan), F32), pltpu.VMEM((rows, 128), F32)],
        compiler_params=params(),
        name="grad",
    )(wd_t, row_line, bin_t, depth, slope, picked, returned)
    return logits, grad


def solution(mesh):
    in_specs = (
        P("cam", "tile", None),
        P(),
        P(),
        P(),
        P(("cam", "tile"), None, None),
        P(("cam", "tile"), None, None),
        P(("cam", "tile"), None, None),
        P(None, ("cam", "tile"), None),
    )
    out_specs = (P(None, ("cam", "tile"), None), P("cam", "tile", None))
    return jax.shard_map(
        per_device, mesh=mesh, in_specs=in_specs, out_specs=out_specs, check_vma=False
    )
```

```python
import jax
import jax.numpy as jnp
from jax import lax
from jax.experimental import pallas as pl
from jax.experimental.pallas import tpu as pltpu
from jax.sharding import PartitionSpec as P

loss_weight = 16.0
BF = jnp.bfloat16
F32 = jnp.float32
AXES = ("cam", "tile")
PICK_BLOCK = 2048
TAKE_BLOCK = 1024
TAKE_UNROLL = 4
GRAD_BLOCK = 2048
FIRST_CELLS = 1536
CELL_BLOCK = 512
CELLS = 4096
IMG_PAD = 48
VMEM_LIMIT = 48 * 1024 * 1024


def swapped(shard, first):
    pairs = []
    for i in range(first, lax.axis_size(AXES) - 1, 2):
        pairs += [(i, i + 1), (i + 1, i)]
    return lax.ppermute(shard, AXES, pairs)


def dot(a, b):
    return jnp.dot(a, b, preferred_element_type=F32)


def dot_t(a, b):
    return lax.dot_general(a, b, (((1,), (1,)), ((), ())), preferred_element_type=F32)


def sigmoid(v):
    return 1.0 / (1.0 + jnp.exp(-v))


def padded_row(row):
    return row + 4 * ((row * 1490) >> 16)


def cell_place(cell):
    u = cell >> 9
    v = cell & 511
    return jnp.where(u >= 8, -1, (u & 1) * 2048 + (v & 1) * 1024 + (u >> 1) * 256 + (v >> 1))


def splat_place(cell):
    u = cell >> 9
    v = cell & 511
    return jnp.where(u >= 8, -1, ((u + 1) & 7) * 512 + (v & 1) * 256 + (v >> 1))


def one_hot(mask):
    return jnp.where(mask, 1.0, 0.0).astype(BF)


def row_hot(rows, ids):
    hot = lax.broadcasted_iota(jnp.int16, (rows, ids.shape[1]), 0) == ids.astype(jnp.int16)
    return jnp.where(hot, jnp.ones((), BF), jnp.zeros((), BF))


def fill_rows(feat_ref, x_ref):
    for i in range(feat_ref.shape[0]):
        rows = feat_ref[i].astype(F32)
        rows = jnp.concatenate([rows, jnp.zeros((IMG_PAD - rows.shape[0], rows.shape[1]), F32)], axis=0)
        x_ref[i * IMG_PAD : (i + 1) * IMG_PAD, :] = rows.astype(BF)


def pick_rows(ids, x):
    groups, per = ids.shape
    rows = x.shape[0]
    chooser = one_hot(lax.broadcasted_iota(jnp.int32, (groups, per, rows), 2) == ids[:, :, None])
    return dot(chooser.reshape(groups * per, rows), x)


def pick_kernel(feat_ref, wd_ref, row_ref, bin_ref, pay_ref, tie_ref, x_ref, rid_ref, bid_ref):
    step = pl.program_id(0)

    @pl.when(step == 0)
    def _():
        fill_rows(feat_ref, x_ref)
        rid_ref[...] = padded_row(jnp.transpose(row_ref[...]))
        bid_ref[...] = jnp.transpose(bin_ref[...])
        tie_ref[...] = jnp.zeros_like(tie_ref)

    count = pay_ref.shape[0]
    per = rid_ref.shape[1]
    groups = count // per
    at = pl.ds(pl.multiple_of(step * groups, groups), groups)
    picked = pick_rows(rid_ref[at, :], x_ref[...])
    logits = dot_t(picked.astype(BF), wd_ref[...])
    bins = logits.shape[1]
    mask = lax.broadcasted_iota(jnp.int32, (groups, per, bins), 2) == bid_ref[at, :][:, :, None]
    chosen = jnp.sum(jnp.where(mask, logits.reshape(groups, per, bins), 0.0), axis=2, keepdims=True)
    pay_ref[...] = (sigmoid(chosen).reshape(count, 1) * picked).astype(BF)


def line_up(table_ref, wide_ref):
    per, partners = table_ref.shape
    wide_ref[:, 0:per] = jnp.transpose(table_ref[...])
    fold = 128 // per
    lane = lax.broadcasted_iota(jnp.int32, (partners // fold, 128), 1) // per
    out = jnp.zeros((partners // fold, 128), jnp.int32)
    for j in range(fold):
        part = wide_ref[pl.ds(j, partners // fold, stride=fold), :]
        if j:
            part = pltpu.roll(part, j * per, 1)
        out = jnp.where(lane == j, part, out)
    return out


def as_line(table):
    return jnp.concatenate([table[g : g + 1, :] for g in range(table.shape[0])], axis=1)


def places_kernel(cell_ref, tie_ref, line_ref, twice_ref, wide_ref):
    line_ref[...] = splat_place(line_up(cell_ref, wide_ref))
    place = cell_place(cell_ref[...])
    twice_ref[...] = 2 * jnp.where(place < 0, CELLS, place)


def again_kernel(feat_ref, wd_ref, row_ref, bin_ref, tie_ref, picked_ref, depth_ref, line_ref, slope_ref, x_ref, rid_ref, bid_ref, wide_ref):
    step = pl.program_id(0)

    @pl.when(step == 0)
    def _():
        fill_rows(feat_ref, x_ref)
        rid_ref[...] = padded_row(jnp.transpose(row_ref[...]))
        line_ref[...] = padded_row(line_up(row_ref, wide_ref))
        bid_ref[...] = line_up(bin_ref, wide_ref)
        prob = sigmoid(dot_t(x_ref[...], wd_ref[...]))
        slope_ref[...] = prob * (1.0 - prob)

    count = picked_ref.shape[0]
    groups = count // rid_ref.shape[1]
    at = pl.ds(pl.multiple_of(step * groups, groups), groups)
    picked = pick_rows(rid_ref[at, :], x_ref[...]).astype(BF)
    picked_ref[...] = picked
    logits = dot_t(wd_ref[...], picked)
    lines = count // 128
    bins = as_line(bid_ref[pl.ds(pl.multiple_of(step * lines, lines), lines), :])
    mask = lax.broadcasted_iota(jnp.int32, logits.shape, 0) == bins
    depth_ref[0] = sigmoid(jnp.sum(jnp.where(mask, logits, 0.0), axis=0, keepdims=True))


def splat_kernel(first, line_ref, val_ref, out_ref):
    rows = out_ref.shape[0]
    place = as_line(line_ref[...]) - (first + pl.program_id(0) * rows)
    placer = one_hot(lax.broadcasted_iota(jnp.int32, (rows, place.shape[1]), 0) == place)
    out_ref[...] = dot(placer, val_ref[...]).astype(BF)


def shift_down(v):
    col = lax.broadcasted_iota(jnp.int32, v.shape, 0) & 255
    return jnp.where(col == 0, 0.0, pltpu.roll(v, 1, 0))


def shift_up(v):
    n = v.shape[0]
    col = lax.broadcasted_iota(jnp.int32, v.shape, 0) & 255
    return jnp.where(col == 255, 0.0, pltpu.roll(v, n - 1, 0))


def top_taps(ue, uo, w_ref):
    return dot(ue, w_ref[0, 1]) + dot(uo, w_ref[0, 2]) + shift_down(dot(uo, w_ref[0, 0]))


def lower_taps(ee, eo, oe, oo, w_ref):
    z = dot(ee, w_ref[1, 1]) + dot(eo, w_ref[1, 2])
    z = z + dot(oe, w_ref[2, 1]) + dot(oo, w_ref[2, 2])
    return z + shift_down(dot(eo, w_ref[1, 0]) + dot(oo, w_ref[2, 0]))


def rim_kernel(me_ref, first_ref, w_ref, lab_ref, top_ref, own_ref, even_ref, odd_ref):
    top = top_taps(first_ref[0:256, :], first_ref[256:512, :], w_ref).astype(BF)
    own = lower_taps(
        first_ref[512:768, :], first_ref[768:1024, :], first_ref[1024:1280, :], first_ref[1280:1536, :], w_ref
    )
    labels = lab_ref[:, 0, :].astype(F32).astype(BF)
    top_ref[...] = top
    own_ref[...] = own
    even_ref[256:272, :] = labels
    odd_ref[256:272, :] = labels
    leads = (me_ref[0] & 1) == 0

    @pl.when(leads)
    def _():
        even_ref[0:256, :] = top
        odd_ref[0:256, :] = own.astype(BF)

    @pl.when(jnp.logical_not(leads))
    def _():
        even_ref[0:256, :] = own.astype(BF)
        odd_ref[0:256, :] = top


def conv_take_kernel(
    me_ref,
    twice_ref,
    first_ref,
    rest_ref,
    top_ref,
    own_ref,
    even_ref,
    odd_ref,
    w_ref,
    wp_ref,
    lab_ref,
    out_ref,
    tie_ref,
    logit_ref,
    src_ref,
    dst_ref,
):
    step = pl.program_id(0)

    @pl.when(step == 0)
    def _():
        def put(at, rows):
            rows = rows.astype(BF).astype(F32)
            src_ref[pl.ds(2 * at, rows.shape[0], stride=2), :] = rows[:, :128]
            src_ref[pl.ds(2 * at + 1, rows.shape[0], stride=2), :] = rows[:, 128:]

        def half(odd, *grid_rows):
            parts = []
            for u in grid_rows:
                ref, at = (first_ref, (u + 1) & 7) if u < 2 or u == 7 else (rest_ref, u - 2)
                at = at * 512 + odd * 256
                parts.append(ref[at : at + 256, :])
            return jnp.concatenate(parts, axis=0)

        leads = (me_ref[0] & 1) == 0
        even = even_ref[...].astype(F32)
        odd = odd_ref[...].astype(F32)
        above = jnp.where(leads, odd[0:256], even[0:256])
        below = jnp.where(leads, even, odd)
        z = top_taps(half(0, 1, 3, 5), half(1, 1, 3, 5), w_ref)
        z = z + lower_taps(half(0, 2, 4, 6), half(1, 2, 4, 6), half(0, 3, 5, 7), half(1, 3, 5, 7), w_ref)
        z = jnp.concatenate([own_ref[...] + above, z, top_ref[...].astype(F32) + below[0:256]], axis=0)
        labels = jnp.concatenate([lab_ref[:, i, :].astype(F32) for i in range(4)] + [below[256:272]], axis=1)
        s = sigmoid(z)
        act = (z * s).astype(BF)
        logits = dot_t(wp_ref[...], act)
        for i in range(4):
            logit_ref[:, i, :] = logits[:, i * 256 : (i + 1) * 256]
        dlogit = (loss_weight * (sigmoid(logits) - labels)).astype(BF)
        grad_act = lax.dot_general(dlogit, wp_ref[...], (((0,), (0,)), ((), ())), preferred_element_type=F32)
        dz = grad_act * (s * (1.0 + z * (1.0 - s)))
        row = lax.broadcasted_iota(jnp.int32, dz.shape, 0)
        dz = jnp.where(row < jnp.where(me_ref[1] == 0, 1024, 1280), dz, 0.0)
        dzs = shift_up(dz).astype(BF)
        dz = dz.astype(BF)
        put(0, dot_t(dz[0:1024], w_ref[1, 1]))
        put(1024, dot_t(dz[0:1024], w_ref[1, 2]) + dot_t(dzs[0:1024], w_ref[1, 0]))
        put(2048, dot_t(dz[0:1024], w_ref[2, 1]) + dot_t(dz[256:1280], w_ref[0, 1]))
        put(
            3072,
            dot_t(dz[0:1024], w_ref[2, 2])
            + dot_t(dzs[0:1024], w_ref[2, 0])
            + dot_t(dz[256:1280], w_ref[0, 2])
            + dot_t(dzs[256:1280], w_ref[0, 0]),
        )
        src_ref[2 * CELLS : 2 * CELLS + 8, :] = jnp.zeros((8, 128), F32)
        tie_ref[...] = jnp.zeros_like(tie_ref)

    count = out_ref.shape[0]
    per = twice_ref.shape[0]
    groups = count // per
    turn = 2 * per * TAKE_UNROLL

    def some(g, carry):
        rows = dst_ref.at[pl.ds(pl.multiple_of(g * turn, turn), turn), :]
        for j in range(TAKE_UNROLL):
            for k in range(per):
                at = pl.multiple_of(twice_ref[k, step * groups + g * TAKE_UNROLL + j], 2)
                to = 2 * (j * per + k)
                rows[to : to + 2, :] = src_ref[pl.ds(at, 2), :]
        return carry

    lax.fori_loop(0, groups // TAKE_UNROLL, some, 0)
    out_ref[:, :128] = dst_ref[pl.ds(0, count, stride=2), :].astype(BF)
    out_ref[:, 128:] = dst_ref[pl.ds(1, count, stride=2), :].astype(BF)


def grad_kernel(wd_ref, line_ref, bin_ref, depth_ref, slope_ref, picked_ref, inc_ref, out_ref, bid_ref, acc_ref, accd_ref):
    step = pl.program_id(0)

    @pl.when(step == 0)
    def _():
        bid_ref[...] = jnp.transpose(bin_ref[...])
        acc_ref[...] = jnp.zeros_like(acc_ref)
        accd_ref[...] = jnp.zeros_like(accd_ref)

    rows = acc_ref.shape[0]
    inc = inc_ref[...]
    count = inc.shape[0]
    per = bid_ref.shape[1]
    groups = count // per
    terms = picked_ref[...].astype(F32) * inc.astype(F32)
    terms = terms[:, :128] + terms[:, 128:]
    high = terms.astype(BF)
    halves = jnp.concatenate([high, (terms - high.astype(F32)).astype(BF)], axis=1)
    inner = dot(halves, jnp.ones((256, 128), BF)).reshape(groups, per, 128)
    at = pl.ds(pl.multiple_of(step * groups, groups), groups)
    mask = (lax.broadcasted_iota(jnp.int32, (groups, per, 128), 2) & 63) == bid_ref[at, :][:, :, None]
    binned = jnp.where(mask, inner, 0.0).reshape(count, 128)
    high = binned.astype(BF).astype(F32)
    lane = lax.broadcasted_iota(jnp.int32, (count, 128), 1)
    both = jnp.where(lane < 64, high, binned - high).astype(BF)
    lines = count // 128
    chooser = row_hot(rows, as_line(line_ref[pl.ds(pl.multiple_of(step * lines, lines), lines), :]))
    acc_ref[...] += dot(chooser * depth_ref[0].astype(BF), inc)
    accd_ref[...] += dot(chooser, both)

    @pl.when(step == pl.num_programs(0) - 1)
    def _():
        sums = accd_ref[...]
        grad_logit = (slope_ref[...] * (sums[:, :64] + sums[:, 64:])).astype(BF)
        total = acc_ref[...] + dot(grad_logit, wd_ref[...])
        for i in range(out_ref.shape[0]):
            out_ref[i] = total[i * IMG_PAD : i * IMG_PAD + out_ref.shape[1], :]


def params():
    return pltpu.CompilerParams(vmem_limit_bytes=VMEM_LIMIT)


def whole(shape):
    return pl.BlockSpec(shape, lambda i: (0,) * len(shape))


def per_device(features, w_depth, w_conv, w_pred, send_row, send_bin, recv_cell, labels):
    imgs, pix, chan = features.shape
    sources, cap = send_row.shape[1], send_row.shape[2]
    slots = sources * cap
    rows = imgs * IMG_PAD
    row_t = jnp.transpose(send_row.reshape(sources, cap))
    bin_t = jnp.transpose(send_bin.reshape(sources, cap))
    cell_t = jnp.transpose(recv_cell.reshape(sources, cap))
    wd_t = jnp.transpose(w_depth)
    bins = wd_t.shape[0]
    table = whole((cap, sources))
    lines = slots // 128
    ids_scratch = pltpu.VMEM((sources, cap), jnp.int32)
    wide_scratch = pltpu.VMEM((sources, 128), jnp.int32)
    x_scratch = pltpu.VMEM((rows, chan), BF)
    tie_spec = whole((8, 128))
    tie_shape = jax.ShapeDtypeStruct((8, 128), F32)

    def slot_spec(block):
        return pl.BlockSpec((block, chan), lambda i: (i, 0))

    def exchange(v):
        out = lax.all_to_all(v.reshape(sources, cap, chan), AXES, split_axis=0, concat_axis=0, tiled=True)
        return out.reshape(slots, chan)

    payload, tie = pl.pallas_call(
        pick_kernel,
        out_shape=(pltpu.HBM((slots, chan), BF), tie_shape),
        grid=(slots // PICK_BLOCK,),
        in_specs=[whole(features.shape), whole(wd_t.shape), table, table],
        out_specs=(slot_spec(PICK_BLOCK), tie_spec),
        scratch_shapes=[x_scratch, ids_scratch, ids_scratch],
        compiler_params=params(),
        name="pick",
    )(*(pltpu.with_memory_space_constraint(v, pltpu.HBM) for v in (features, wd_t, row_t, bin_t)))
    arrived = exchange(payload)

    place_line, place_twice = pl.pallas_call(
        places_kernel,
        out_shape=(
            jax.ShapeDtypeStruct((lines, 128), jnp.int32),
            jax.ShapeDtypeStruct((cap, sources), jnp.int32),
        ),
        grid=(1,),
        in_specs=[table, tie_spec],
        out_specs=(whole((lines, 128)), table),
        scratch_shapes=[wide_scratch],
        compiler_params=params(),
        name="places",
    )(cell_t, tie)

    def splat(first, count, name, line):
        return pl.pallas_call(
            lambda *refs: splat_kernel(first, *refs),
            out_shape=jax.ShapeDtypeStruct((count, chan), BF),
            grid=(count // CELL_BLOCK,),
            in_specs=[whole((lines, 128)), whole((slots, chan))],
            out_specs=pl.BlockSpec((CELL_BLOCK, chan), lambda i: (i, 0)),
            compiler_params=params(),
            name=name,
        )(line, arrived)

    index = lax.axis_index(AXES)
    me = jnp.stack([index, lax.axis_size(AXES) - 1 - index]).astype(jnp.int32)
    scalars = pl.BlockSpec(memory_space=pltpu.SMEM)
    vmem = pl.BlockSpec(memory_space=pltpu.VMEM)
    first = splat(0, FIRST_CELLS, "splat_first", place_line)
    message = jax.ShapeDtypeStruct((272, chan), BF)
    top, own, even, odd = pl.pallas_call(
        rim_kernel,
        out_shape=(
            jax.ShapeDtypeStruct((256, chan), BF),
            jax.ShapeDtypeStruct((256, chan), F32),
            message,
            message,
        ),
        in_specs=[scalars, vmem, vmem, vmem],
        compiler_params=params(),
        name="rim",
    )(me, first, w_conv, labels)
    got_even = swapped(even, 0)
    got_odd = swapped(odd, 1)
    line_b, _ = lax.optimization_barrier((place_line, top))
    rest = splat(FIRST_CELLS, CELLS - FIRST_CELLS, "splat_rest", line_b)

    outgoing, tie, logits = pl.pallas_call(
        conv_take_kernel,
        out_shape=(pltpu.HBM((slots, chan), BF), tie_shape, jax.ShapeDtypeStruct(labels.shape, F32)),
        grid=(slots // TAKE_BLOCK,),
        in_specs=[
            scalars,
            scalars,
            whole((FIRST_CELLS, chan)),
            whole((CELLS - FIRST_CELLS, chan)),
            whole((256, chan)),
            whole((256, chan)),
            whole((272, chan)),
            whole((272, chan)),
            whole(w_conv.shape),
            whole(w_pred.shape),
            whole(labels.shape),
        ],
        out_specs=(slot_spec(TAKE_BLOCK), tie_spec, whole(labels.shape)),
        scratch_shapes=[pltpu.VMEM((2 * CELLS + 8, 128), F32), pltpu.VMEM((2 * TAKE_BLOCK, 128), F32)],
        compiler_params=params(),
        name="conv_take",
    )(me, place_twice, first, rest, top, own, got_even, got_odd, w_conv, w_pred, labels)
    returned = exchange(outgoing)

    picked, depth, row_line, slope = pl.pallas_call(
        again_kernel,
        out_shape=(
            pltpu.HBM((slots, chan), BF),
            jax.ShapeDtypeStruct((slots // GRAD_BLOCK, 1, GRAD_BLOCK), F32),
            jax.ShapeDtypeStruct((lines, 128), jnp.int32),
            jax.ShapeDtypeStruct((rows, bins), F32),
        ),
        grid=(slots // GRAD_BLOCK,),
        in_specs=[whole(features.shape), whole(wd_t.shape), table, table, tie_spec],
        out_specs=(
            slot_spec(GRAD_BLOCK),
            pl.BlockSpec((1, 1, GRAD_BLOCK), lambda i: (i, 0, 0)),
            whole((lines, 128)),
            whole((rows, bins)),
        ),
        scratch_shapes=[x_scratch, ids_scratch, pltpu.VMEM((lines, 128), jnp.int32), wide_scratch],
        compiler_params=params(),
        name="pick_again",
    )(features, wd_t, row_t, bin_t, tie)
    picked = pltpu.with_memory_space_constraint(picked, pltpu.HBM)

    grad = pl.pallas_call(
        grad_kernel,
        out_shape=jax.ShapeDtypeStruct((imgs, pix, chan), F32),
        grid=(slots // GRAD_BLOCK,),
        in_specs=[
            whole(wd_t.shape),
            whole((lines, 128)),
            table,
            pl.BlockSpec((1, 1, GRAD_BLOCK), lambda i: (i, 0, 0)),
            whole((rows, bins)),
            slot_spec(GRAD_BLOCK),
            slot_spec(GRAD_BLOCK),
        ],
        out_specs=whole((imgs, pix, chan)),
        scratch_shapes=[ids_scratch, pltpu.VMEM((rows, chan), F32), pltpu.VMEM((rows, 128), F32)],
        compiler_params=params(),
        name="grad",
    )(wd_t, row_line, bin_t, depth, slope, picked, returned)
    return logits, grad


def solution(mesh):
    in_specs = (
        P("cam", "tile", None),
        P(),
        P(),
        P(),
        P(("cam", "tile"), None, None),
        P(("cam", "tile"), None, None),
        P(("cam", "tile"), None, None),
        P(None, ("cam", "tile"), None),
    )
    out_specs = (P(None, ("cam", "tile"), None), P("cam", "tile", None))
    return jax.shard_map(
        per_device, mesh=mesh, in_specs=in_specs, out_specs=out_specs, check_vma=False
    )
```

```python
import jax
import jax.numpy as jnp
from jax import lax
from jax.experimental import pallas as pl
from jax.experimental.pallas import tpu as pltpu
from jax.sharding import PartitionSpec as P

loss_weight = 16.0
BF = jnp.bfloat16
F32 = jnp.float32
AXES = ("cam", "tile")
PICK_BLOCK = 2048
TAKE_BLOCK = 1024
TAKE_UNROLL = 4
FIRST_CELLS = 1536
CELL_BLOCK = 512
CELLS = 4096
IMG_PAD = 48
VMEM_LIMIT = 48 * 1024 * 1024


def swapped(shard, first):
    pairs = []
    for i in range(first, lax.axis_size(AXES) - 1, 2):
        pairs += [(i, i + 1), (i + 1, i)]
    return lax.ppermute(shard, AXES, pairs)


def dot(a, b):
    return jnp.dot(a, b, preferred_element_type=F32)


def dot_t(a, b):
    return lax.dot_general(a, b, (((1,), (1,)), ((), ())), preferred_element_type=F32)


def sigmoid(v):
    return 1.0 / (1.0 + jnp.exp(-v))


def padded_row(row):
    return row + 4 * ((row * 1490) >> 16)


def cell_place(cell):
    u = cell >> 9
    v = cell & 511
    return jnp.where(u >= 8, -1, (u & 1) * 2048 + (v & 1) * 1024 + (u >> 1) * 256 + (v >> 1))


def splat_place(cell):
    u = cell >> 9
    v = cell & 511
    return jnp.where(u >= 8, -1, ((u + 1) & 7) * 512 + (v & 1) * 256 + (v >> 1))


def one_hot(mask):
    return jnp.where(mask, 1.0, 0.0).astype(BF)


def row_hot(rows, ids):
    hot = lax.broadcasted_iota(jnp.int16, (rows, ids.shape[1]), 0) == ids.astype(jnp.int16)
    return jnp.where(hot, jnp.ones((), BF), jnp.zeros((), BF))


def fill_rows(feat_ref, x_ref):
    for i in range(feat_ref.shape[0]):
        rows = feat_ref[i].astype(F32)
        rows = jnp.concatenate([rows, jnp.zeros((IMG_PAD - rows.shape[0], rows.shape[1]), F32)], axis=0)
        x_ref[i * IMG_PAD : (i + 1) * IMG_PAD, :] = rows.astype(BF)


def pick_rows(ids, x):
    groups, per = ids.shape
    rows = x.shape[0]
    chooser = one_hot(lax.broadcasted_iota(jnp.int32, (groups, per, rows), 2) == ids[:, :, None])
    return dot(chooser.reshape(groups * per, rows), x)


def pick_kernel(feat_ref, wd_ref, row_ref, bin_ref, pay_ref, tie_ref, x_ref, rid_ref, bid_ref):
    step = pl.program_id(0)

    @pl.when(step == 0)
    def _():
        fill_rows(feat_ref, x_ref)
        rid_ref[...] = padded_row(jnp.transpose(row_ref[...]))
        bid_ref[...] = jnp.transpose(bin_ref[...])
        tie_ref[...] = jnp.zeros_like(tie_ref)

    count = pay_ref.shape[0]
    per = rid_ref.shape[1]
    groups = count // per
    at = pl.ds(pl.multiple_of(step * groups, groups), groups)
    picked = pick_rows(rid_ref[at, :], x_ref[...])
    logits = dot_t(picked.astype(BF), wd_ref[...])
    bins = logits.shape[1]
    mask = lax.broadcasted_iota(jnp.int32, (groups, per, bins), 2) == bid_ref[at, :][:, :, None]
    chosen = jnp.sum(jnp.where(mask, logits.reshape(groups, per, bins), 0.0), axis=2, keepdims=True)
    pay_ref[...] = (sigmoid(chosen).reshape(count, 1) * picked).astype(BF)


def line_up(table_ref, wide_ref):
    per, partners = table_ref.shape
    wide_ref[:, 0:per] = jnp.transpose(table_ref[...])
    fold = 128 // per
    lane = lax.broadcasted_iota(jnp.int32, (partners // fold, 128), 1) // per
    out = jnp.zeros((partners // fold, 128), jnp.int32)
    for j in range(fold):
        part = wide_ref[pl.ds(j, partners // fold, stride=fold), :]
        if j:
            part = pltpu.roll(part, j * per, 1)
        out = jnp.where(lane == j, part, out)
    return out


def as_line(table):
    return jnp.concatenate([table[g : g + 1, :] for g in range(table.shape[0])], axis=1)


def places_kernel(cell_ref, tie_ref, line_ref, twice_ref, wide_ref):
    line_ref[...] = splat_place(line_up(cell_ref, wide_ref))
    place = cell_place(cell_ref[...])
    twice_ref[...] = 2 * jnp.where(place < 0, CELLS, place)


def again_kernel(
    feat_ref, wd_ref, row_ref, bin_ref, tie_ref, near_ref, far_ref, depth_ref, line_ref, slope_ref, x_ref, rid_ref, bid_ref, wide_ref
):
    step = pl.program_id(0)

    @pl.when(step == 0)
    def _():
        fill_rows(feat_ref, x_ref)
        rid_ref[...] = padded_row(jnp.transpose(row_ref[...]))
        line_ref[...] = padded_row(line_up(row_ref, wide_ref))
        bid_ref[...] = line_up(bin_ref, wide_ref)
        prob = sigmoid(dot_t(x_ref[...], wd_ref[...]))
        slope_ref[...] = prob * (1.0 - prob)

    count = near_ref.shape[0]
    groups = count // rid_ref.shape[1]
    at = pl.ds(pl.multiple_of(step * groups, groups), groups)
    picked = pick_rows(rid_ref[at, :], x_ref[...]).astype(BF)

    @pl.when(step == 0)
    def _():
        near_ref[...] = picked

    @pl.when(step == 1)
    def _():
        far_ref[...] = picked

    logits = dot_t(wd_ref[...], picked)
    lines = count // 128
    bins = as_line(bid_ref[pl.ds(pl.multiple_of(step * lines, lines), lines), :])
    mask = lax.broadcasted_iota(jnp.int32, logits.shape, 0) == bins
    depth_ref[...] = sigmoid(jnp.sum(jnp.where(mask, logits, 0.0), axis=0, keepdims=True))


def splat_kernel(first, line_ref, val_ref, out_ref):
    rows = out_ref.shape[0]
    place = as_line(line_ref[...]) - (first + pl.program_id(0) * rows)
    placer = one_hot(lax.broadcasted_iota(jnp.int32, (rows, place.shape[1]), 0) == place)
    out_ref[...] = dot(placer, val_ref[...]).astype(BF)


def shift_down(v):
    col = lax.broadcasted_iota(jnp.int32, v.shape, 0) & 255
    return jnp.where(col == 0, 0.0, pltpu.roll(v, 1, 0))


def shift_up(v):
    n = v.shape[0]
    col = lax.broadcasted_iota(jnp.int32, v.shape, 0) & 255
    return jnp.where(col == 255, 0.0, pltpu.roll(v, n - 1, 0))


def top_taps(ue, uo, w_ref):
    return dot(ue, w_ref[0, 1]) + dot(uo, w_ref[0, 2]) + shift_down(dot(uo, w_ref[0, 0]))


def lower_taps(ee, eo, oe, oo, w_ref):
    z = dot(ee, w_ref[1, 1]) + dot(eo, w_ref[1, 2])
    z = z + dot(oe, w_ref[2, 1]) + dot(oo, w_ref[2, 2])
    return z + shift_down(dot(eo, w_ref[1, 0]) + dot(oo, w_ref[2, 0]))


def rim_kernel(me_ref, first_ref, w_ref, lab_ref, top_ref, own_ref, even_ref, odd_ref):
    top = top_taps(first_ref[0:256, :], first_ref[256:512, :], w_ref).astype(BF)
    own = lower_taps(
        first_ref[512:768, :], first_ref[768:1024, :], first_ref[1024:1280, :], first_ref[1280:1536, :], w_ref
    )
    labels = lab_ref[:, 0, :].astype(F32).astype(BF)
    top_ref[...] = top
    own_ref[...] = own
    even_ref[256:272, :] = labels
    odd_ref[256:272, :] = labels
    leads = (me_ref[0] & 1) == 0

    @pl.when(leads)
    def _():
        even_ref[0:256, :] = top
        odd_ref[0:256, :] = own.astype(BF)

    @pl.when(jnp.logical_not(leads))
    def _():
        even_ref[0:256, :] = own.astype(BF)
        odd_ref[0:256, :] = top


def conv_take_kernel(
    me_ref,
    twice_ref,
    first_ref,
    rest_ref,
    top_ref,
    own_ref,
    even_ref,
    odd_ref,
    w_ref,
    wp_ref,
    lab_ref,
    out_ref,
    tie_ref,
    logit_ref,
    src_ref,
    dst_ref,
):
    step = pl.program_id(0)

    @pl.when(step == 0)
    def _():
        def put(at, rows):
            rows = rows.astype(BF).astype(F32)
            src_ref[pl.ds(2 * at, rows.shape[0], stride=2), :] = rows[:, :128]
            src_ref[pl.ds(2 * at + 1, rows.shape[0], stride=2), :] = rows[:, 128:]

        def half(odd, *grid_rows):
            parts = []
            for u in grid_rows:
                ref, at = (first_ref, (u + 1) & 7) if u < 2 or u == 7 else (rest_ref, u - 2)
                at = at * 512 + odd * 256
                parts.append(ref[at : at + 256, :])
            return jnp.concatenate(parts, axis=0)

        leads = (me_ref[0] & 1) == 0
        even = even_ref[...].astype(F32)
        odd = odd_ref[...].astype(F32)
        above = jnp.where(leads, odd[0:256], even[0:256])
        below = jnp.where(leads, even, odd)
        z = top_taps(half(0, 1, 3, 5), half(1, 1, 3, 5), w_ref)
        z = z + lower_taps(half(0, 2, 4, 6), half(1, 2, 4, 6), half(0, 3, 5, 7), half(1, 3, 5, 7), w_ref)
        z = jnp.concatenate([own_ref[...] + above, z, top_ref[...].astype(F32) + below[0:256]], axis=0)
        labels = jnp.concatenate([lab_ref[:, i, :].astype(F32) for i in range(4)] + [below[256:272]], axis=1)
        s = sigmoid(z)
        act = (z * s).astype(BF)
        logits = dot_t(wp_ref[...], act)
        for i in range(4):
            logit_ref[:, i, :] = logits[:, i * 256 : (i + 1) * 256]
        dlogit = (loss_weight * (sigmoid(logits) - labels)).astype(BF)
        grad_act = lax.dot_general(dlogit, wp_ref[...], (((0,), (0,)), ((), ())), preferred_element_type=F32)
        dz = grad_act * (s * (1.0 + z * (1.0 - s)))
        row = lax.broadcasted_iota(jnp.int32, dz.shape, 0)
        dz = jnp.where(row < jnp.where(me_ref[1] == 0, 1024, 1280), dz, 0.0)
        dzs = shift_up(dz).astype(BF)
        dz = dz.astype(BF)
        put(0, dot_t(dz[0:1024], w_ref[1, 1]))
        put(1024, dot_t(dz[0:1024], w_ref[1, 2]) + dot_t(dzs[0:1024], w_ref[1, 0]))
        put(2048, dot_t(dz[0:1024], w_ref[2, 1]) + dot_t(dz[256:1280], w_ref[0, 1]))
        put(
            3072,
            dot_t(dz[0:1024], w_ref[2, 2])
            + dot_t(dzs[0:1024], w_ref[2, 0])
            + dot_t(dz[256:1280], w_ref[0, 2])
            + dot_t(dzs[256:1280], w_ref[0, 0]),
        )
        src_ref[2 * CELLS : 2 * CELLS + 8, :] = jnp.zeros((8, 128), F32)
        tie_ref[...] = jnp.zeros_like(tie_ref)

    count = out_ref.shape[0]
    per = twice_ref.shape[0]
    groups = count // per
    turn = 2 * per * TAKE_UNROLL

    def some(g, carry):
        rows = dst_ref.at[pl.ds(pl.multiple_of(g * turn, turn), turn), :]
        for j in range(TAKE_UNROLL):
            for k in range(per):
                at = pl.multiple_of(twice_ref[k, step * groups + g * TAKE_UNROLL + j], 2)
                to = 2 * (j * per + k)
                rows[to : to + 2, :] = src_ref[pl.ds(at, 2), :]
        return carry

    lax.fori_loop(0, groups // TAKE_UNROLL, some, 0)
    out_ref[:, :128] = dst_ref[pl.ds(0, count, stride=2), :].astype(BF)
    out_ref[:, 128:] = dst_ref[pl.ds(1, count, stride=2), :].astype(BF)


def grad_kernel(
    wd_ref, line_ref, bin_ref, depth_ref, near_ref, slope_hbm, far_hbm, inc_ref, out_ref, acc_ref, accd_ref, slope_ref, far_ref, sems
):
    fetch = pltpu.make_async_copy(far_hbm, far_ref, sems.at[0])
    fetch.start()
    fetch_slope = pltpu.make_async_copy(slope_hbm, slope_ref, sems.at[1])
    fetch_slope.start()
    bin_ids = jnp.transpose(bin_ref[...])
    rows = acc_ref.shape[0]
    count = near_ref.shape[0]
    per = bin_ids.shape[1]
    groups = count // per
    lines = count // 128
    for h in range(2):
        if h:
            fetch.wait()
            fetch_slope.wait()
        picked = (far_ref if h else near_ref)[...]
        inc = inc_ref[h * count : (h + 1) * count, :]
        terms = picked.astype(F32) * inc.astype(F32)
        terms = terms[:, :128] + terms[:, 128:]
        high = terms.astype(BF)
        halves = jnp.concatenate([high, (terms - high.astype(F32)).astype(BF)], axis=1)
        inner = dot(halves, jnp.ones((256, 128), BF)).reshape(groups, per, 128)
        mine = bin_ids[h * groups : (h + 1) * groups, :]
        mask = (lax.broadcasted_iota(jnp.int32, (groups, per, 128), 2) & 63) == mine[:, :, None]
        binned = jnp.where(mask, inner, 0.0).reshape(count, 128)
        high = binned.astype(BF).astype(F32)
        lane = lax.broadcasted_iota(jnp.int32, (count, 128), 1)
        both = jnp.where(lane < 64, high, binned - high).astype(BF)
        chooser = row_hot(rows, as_line(line_ref[h * lines : (h + 1) * lines, :]))
        taken = dot(chooser * depth_ref[:, h * count : (h + 1) * count].astype(BF), inc)
        sums = dot(chooser, both)
        if h:
            acc_ref[...] += taken
            accd_ref[...] += sums
        else:
            acc_ref[...] = taken
            accd_ref[...] = sums
    sums = accd_ref[...]
    grad_logit = (slope_ref[...] * (sums[:, :64] + sums[:, 64:])).astype(BF)
    total = acc_ref[...] + dot(grad_logit, wd_ref[...])
    for i in range(out_ref.shape[0]):
        out_ref[i] = total[i * IMG_PAD : i * IMG_PAD + out_ref.shape[1], :]


def params():
    return pltpu.CompilerParams(vmem_limit_bytes=VMEM_LIMIT)


def whole(shape):
    return pl.BlockSpec(shape, lambda i: (0,) * len(shape))


def per_device(features, w_depth, w_conv, w_pred, send_row, send_bin, recv_cell, labels):
    imgs, pix, chan = features.shape
    sources, cap = send_row.shape[1], send_row.shape[2]
    slots = sources * cap
    rows = imgs * IMG_PAD
    row_t = jnp.transpose(send_row.reshape(sources, cap))
    bin_t = jnp.transpose(send_bin.reshape(sources, cap))
    cell_t = jnp.transpose(recv_cell.reshape(sources, cap))
    wd_t = jnp.transpose(w_depth)
    bins = wd_t.shape[0]
    table = whole((cap, sources))
    lines = slots // 128
    ids_scratch = pltpu.VMEM((sources, cap), jnp.int32)
    wide_scratch = pltpu.VMEM((sources, 128), jnp.int32)
    x_scratch = pltpu.VMEM((rows, chan), BF)
    tie_spec = whole((8, 128))
    tie_shape = jax.ShapeDtypeStruct((8, 128), F32)

    def slot_spec(block):
        return pl.BlockSpec((block, chan), lambda i: (i, 0))

    def exchange(v):
        out = lax.all_to_all(v.reshape(sources, cap, chan), AXES, split_axis=0, concat_axis=0, tiled=True)
        return out.reshape(slots, chan)

    payload, tie = pl.pallas_call(
        pick_kernel,
        out_shape=(pltpu.HBM((slots, chan), BF), tie_shape),
        grid=(slots // PICK_BLOCK,),
        in_specs=[whole(features.shape), whole(wd_t.shape), table, table],
        out_specs=(slot_spec(PICK_BLOCK), tie_spec),
        scratch_shapes=[x_scratch, ids_scratch, ids_scratch],
        compiler_params=params(),
        name="pick",
    )(*(pltpu.with_memory_space_constraint(v, pltpu.HBM) for v in (features, wd_t, row_t, bin_t)))
    arrived = exchange(payload)

    place_line, place_twice = pl.pallas_call(
        places_kernel,
        out_shape=(
            jax.ShapeDtypeStruct((lines, 128), jnp.int32),
            jax.ShapeDtypeStruct((cap, sources), jnp.int32),
        ),
        grid=(1,),
        in_specs=[table, tie_spec],
        out_specs=(whole((lines, 128)), table),
        scratch_shapes=[wide_scratch],
        compiler_params=params(),
        name="places",
    )(cell_t, tie)

    def splat(first, count, name, line):
        return pl.pallas_call(
            lambda *refs: splat_kernel(first, *refs),
            out_shape=jax.ShapeDtypeStruct((count, chan), BF),
            grid=(count // CELL_BLOCK,),
            in_specs=[whole((lines, 128)), whole((slots, chan))],
            out_specs=pl.BlockSpec((CELL_BLOCK, chan), lambda i: (i, 0)),
            compiler_params=params(),
            name=name,
        )(line, arrived)

    index = lax.axis_index(AXES)
    me = jnp.stack([index, lax.axis_size(AXES) - 1 - index]).astype(jnp.int32)
    scalars = pl.BlockSpec(memory_space=pltpu.SMEM)
    vmem = pl.BlockSpec(memory_space=pltpu.VMEM)
    first = splat(0, FIRST_CELLS, "splat_first", place_line)
    message = jax.ShapeDtypeStruct((272, chan), BF)
    top, own, even, odd = pl.pallas_call(
        rim_kernel,
        out_shape=(
            jax.ShapeDtypeStruct((256, chan), BF),
            jax.ShapeDtypeStruct((256, chan), F32),
            message,
            message,
        ),
        in_specs=[scalars, vmem, vmem, vmem],
        compiler_params=params(),
        name="rim",
    )(me, first, w_conv, labels)
    got_even = swapped(even, 0)
    got_odd = swapped(odd, 1)
    line_b, _ = lax.optimization_barrier((place_line, top))
    rest = splat(FIRST_CELLS, CELLS - FIRST_CELLS, "splat_rest", line_b)

    outgoing, tie, logits = pl.pallas_call(
        conv_take_kernel,
        out_shape=(pltpu.HBM((slots, chan), BF), tie_shape, jax.ShapeDtypeStruct(labels.shape, F32)),
        grid=(slots // TAKE_BLOCK,),
        in_specs=[
            scalars,
            scalars,
            whole((FIRST_CELLS, chan)),
            whole((CELLS - FIRST_CELLS, chan)),
            whole((256, chan)),
            whole((256, chan)),
            whole((272, chan)),
            whole((272, chan)),
            whole(w_conv.shape),
            whole(w_pred.shape),
            whole(labels.shape),
        ],
        out_specs=(slot_spec(TAKE_BLOCK), tie_spec, whole(labels.shape)),
        scratch_shapes=[pltpu.VMEM((2 * CELLS + 8, 128), F32), pltpu.VMEM((2 * TAKE_BLOCK, 128), F32)],
        compiler_params=params(),
        name="conv_take",
    )(me, place_twice, first, rest, top, own, got_even, got_odd, w_conv, w_pred, labels)
    returned = exchange(outgoing)

    half = slots // 2
    near, far, depth, row_line, slope = pl.pallas_call(
        again_kernel,
        out_shape=(
            jax.ShapeDtypeStruct((half, chan), BF),
            pltpu.HBM((half, chan), BF),
            jax.ShapeDtypeStruct((1, slots), F32),
            jax.ShapeDtypeStruct((lines, 128), jnp.int32),
            pltpu.HBM((rows, bins), F32),
        ),
        grid=(2,),
        in_specs=[whole(features.shape), whole(wd_t.shape), table, table, tie_spec],
        out_specs=(
            whole((half, chan)),
            whole((half, chan)),
            pl.BlockSpec((1, half), lambda i: (0, i)),
            whole((lines, 128)),
            whole((rows, bins)),
        ),
        scratch_shapes=[x_scratch, ids_scratch, pltpu.VMEM((lines, 128), jnp.int32), wide_scratch],
        compiler_params=params(),
        name="pick_again",
    )(features, wd_t, row_t, bin_t, tie)

    held = [pltpu.with_memory_space_constraint(v, pltpu.HBM) for v in (slope, far)]
    grad = pl.pallas_call(
        grad_kernel,
        out_shape=jax.ShapeDtypeStruct((imgs, pix, chan), F32),
        in_specs=[vmem] * 5 + [pl.BlockSpec(memory_space=pltpu.HBM)] * 2 + [vmem],
        scratch_shapes=[
            pltpu.VMEM((rows, chan), F32),
            pltpu.VMEM((rows, 128), F32),
            pltpu.VMEM((rows, bins), F32),
            pltpu.VMEM((half, chan), BF),
            pltpu.SemaphoreType.DMA((2,)),
        ],
        compiler_params=params(),
        name="grad",
    )(wd_t, row_line, bin_t, depth, near, *held, returned)
    return logits, grad


def solution(mesh):
    in_specs = (
        P("cam", "tile", None),
        P(),
        P(),
        P(),
        P(("cam", "tile"), None, None),
        P(("cam", "tile"), None, None),
        P(("cam", "tile"), None, None),
        P(None, ("cam", "tile"), None),
    )
    out_specs = (P(None, ("cam", "tile"), None), P("cam", "tile", None))
    return jax.shard_map(
        per_device, mesh=mesh, in_specs=in_specs, out_specs=out_specs, check_vma=False
    )
```

```python
import jax
import jax.numpy as jnp
import numpy as np
from jax import lax
from jax.experimental import pallas as pl
from jax.experimental.pallas import tpu as pltpu
from jax.sharding import PartitionSpec as P

loss_weight = 16.0
BF = jnp.bfloat16
F32 = jnp.float32
AXES = ("cam", "tile")
PICK_BLOCK = 2048
TAKE_BLOCK = 1024
TAKE_UNROLL = 4
FIRST_CELLS = 1536
CELL_BLOCK = 512
CELLS = 4096
IMG_PAD = 48
VMEM_LIMIT = 48 * 1024 * 1024


def snake(cams, tiles):
    side = 4
    path = []
    for x in range(cams // 2):
        for j in range(tiles // side):
            y = tiles // side - 1 - j if x % 2 else j
            for k in range(side):
                z = side - 1 - k if (x * (tiles // side) + j) % 2 else k
                for core in range(2):
                    path.append((2 * x + core) * tiles + y * side + z)
    return path


def sent(shard, pairs):
    return lax.ppermute(shard, AXES, pairs)


def swap_pairs(path, first):
    pairs = []
    for i in range(first, len(path) - 1, 2):
        pairs += [(path[i], path[i + 1]), (path[i + 1], path[i])]
    return pairs


def dot(a, b):
    return jnp.dot(a, b, preferred_element_type=F32)


def dot_t(a, b):
    return lax.dot_general(a, b, (((1,), (1,)), ((), ())), preferred_element_type=F32)


def sigmoid(v):
    return 1.0 / (1.0 + jnp.exp(-v))


def padded_row(row):
    return row + 4 * ((row * 1490) >> 16)


def cell_place(cell):
    u = cell >> 9
    v = cell & 511
    return jnp.where(u >= 8, -1, (u & 1) * 2048 + (v & 1) * 1024 + (u >> 1) * 256 + (v >> 1))


def splat_place(cell):
    u = cell >> 9
    v = cell & 511
    return jnp.where(u >= 8, -1, ((u + 1) & 7) * 512 + (v & 1) * 256 + (v >> 1))


def one_hot(mask):
    return jnp.where(mask, 1.0, 0.0).astype(BF)


def row_hot(rows, ids):
    hot = lax.broadcasted_iota(jnp.int16, (rows, ids.shape[1]), 0) == ids.astype(jnp.int16)
    return jnp.where(hot, jnp.ones((), BF), jnp.zeros((), BF))


def fill_rows(feat_ref, x_ref):
    for i in range(feat_ref.shape[0]):
        rows = feat_ref[i].astype(F32)
        rows = jnp.concatenate([rows, jnp.zeros((IMG_PAD - rows.shape[0], rows.shape[1]), F32)], axis=0)
        x_ref[i * IMG_PAD : (i + 1) * IMG_PAD, :] = rows.astype(BF)


def pick_rows(ids, x):
    groups, per = ids.shape
    rows = x.shape[0]
    chooser = one_hot(lax.broadcasted_iota(jnp.int32, (groups, per, rows), 2) == ids[:, :, None])
    return dot(chooser.reshape(groups * per, rows), x)


def pick_kernel(feat_ref, wd_ref, row_ref, bin_ref, pay_ref, tie_ref, x_ref, rid_ref, bid_ref):
    step = pl.program_id(0)

    @pl.when(step == 0)
    def _():
        fill_rows(feat_ref, x_ref)
        rid_ref[...] = padded_row(jnp.transpose(row_ref[...]))
        bid_ref[...] = jnp.transpose(bin_ref[...])
        tie_ref[...] = jnp.zeros_like(tie_ref)

    count = pay_ref.shape[0]
    per = rid_ref.shape[1]
    groups = count // per
    at = pl.ds(pl.multiple_of(step * groups, groups), groups)
    picked = pick_rows(rid_ref[at, :], x_ref[...])
    logits = dot_t(picked.astype(BF), wd_ref[...])
    bins = logits.shape[1]
    mask = lax.broadcasted_iota(jnp.int32, (groups, per, bins), 2) == bid_ref[at, :][:, :, None]
    chosen = jnp.sum(jnp.where(mask, logits.reshape(groups, per, bins), 0.0), axis=2, keepdims=True)
    pay_ref[...] = (sigmoid(chosen).reshape(count, 1) * picked).astype(BF)


def line_up(table_ref, wide_ref):
    per, partners = table_ref.shape
    wide_ref[:, 0:per] = jnp.transpose(table_ref[...])
    fold = 128 // per
    lane = lax.broadcasted_iota(jnp.int32, (partners // fold, 128), 1) // per
    out = jnp.zeros((partners // fold, 128), jnp.int32)
    for j in range(fold):
        part = wide_ref[pl.ds(j, partners // fold, stride=fold), :]
        if j:
            part = pltpu.roll(part, j * per, 1)
        out = jnp.where(lane == j, part, out)
    return out


def as_line(table):
    return jnp.concatenate([table[g : g + 1, :] for g in range(table.shape[0])], axis=1)


def places_kernel(cell_ref, order_ref, tie_ref, line_ref, twice_ref, wide_ref, moved_ref):
    cell = cell_ref[...]
    upper = dot((cell >> 6).astype(F32).astype(BF), order_ref[...])
    lower = dot((cell & 63).astype(F32).astype(BF), order_ref[...])
    moved_ref[...] = (64.0 * upper + lower).astype(jnp.int32)
    line_ref[...] = splat_place(line_up(moved_ref, wide_ref))
    place = cell_place(moved_ref[...])
    twice_ref[...] = 2 * jnp.where(place < 0, CELLS, place)


def again_kernel(
    feat_ref, wd_ref, row_ref, bin_ref, tie_ref, near_ref, far_ref, depth_ref, line_ref, slope_ref, x_ref, rid_ref, bid_ref, wide_ref
):
    step = pl.program_id(0)

    @pl.when(step == 0)
    def _():
        fill_rows(feat_ref, x_ref)
        rid_ref[...] = padded_row(jnp.transpose(row_ref[...]))
        line_ref[...] = padded_row(line_up(row_ref, wide_ref))
        bid_ref[...] = line_up(bin_ref, wide_ref)
        prob = sigmoid(dot_t(x_ref[...], wd_ref[...]))
        slope_ref[...] = prob * (1.0 - prob)

    count = near_ref.shape[0]
    groups = count // rid_ref.shape[1]
    at = pl.ds(pl.multiple_of(step * groups, groups), groups)
    picked = pick_rows(rid_ref[at, :], x_ref[...]).astype(BF)

    @pl.when(step == 0)
    def _():
        near_ref[...] = picked

    @pl.when(step == 1)
    def _():
        far_ref[...] = picked

    logits = dot_t(wd_ref[...], picked)
    lines = count // 128
    bins = as_line(bid_ref[pl.ds(pl.multiple_of(step * lines, lines), lines), :])
    mask = lax.broadcasted_iota(jnp.int32, logits.shape, 0) == bins
    depth_ref[...] = sigmoid(jnp.sum(jnp.where(mask, logits, 0.0), axis=0, keepdims=True))


def splat_kernel(first, line_ref, val_ref, out_ref):
    rows = out_ref.shape[0]
    place = as_line(line_ref[...]) - (first + pl.program_id(0) * rows)
    placer = one_hot(lax.broadcasted_iota(jnp.int32, (rows, place.shape[1]), 0) == place)
    out_ref[...] = dot(placer, val_ref[...]).astype(BF)


def shift_down(v):
    col = lax.broadcasted_iota(jnp.int32, v.shape, 0) & 255
    return jnp.where(col == 0, 0.0, pltpu.roll(v, 1, 0))


def shift_up(v):
    n = v.shape[0]
    col = lax.broadcasted_iota(jnp.int32, v.shape, 0) & 255
    return jnp.where(col == 255, 0.0, pltpu.roll(v, n - 1, 0))


def top_taps(ue, uo, w_ref):
    return dot(ue, w_ref[0, 1]) + dot(uo, w_ref[0, 2]) + shift_down(dot(uo, w_ref[0, 0]))


def lower_taps(ee, eo, oe, oo, w_ref):
    z = dot(ee, w_ref[1, 1]) + dot(eo, w_ref[1, 2])
    z = z + dot(oe, w_ref[2, 1]) + dot(oo, w_ref[2, 2])
    return z + shift_down(dot(eo, w_ref[1, 0]) + dot(oo, w_ref[2, 0]))


def rim_kernel(me_ref, first_ref, w_ref, lab_ref, top_ref, own_ref, even_ref, odd_ref):
    top = top_taps(first_ref[0:256, :], first_ref[256:512, :], w_ref).astype(BF)
    own = lower_taps(
        first_ref[512:768, :], first_ref[768:1024, :], first_ref[1024:1280, :], first_ref[1280:1536, :], w_ref
    )
    labels = lab_ref[:, 0, :].astype(F32).astype(BF)
    top_ref[...] = top
    own_ref[...] = own
    even_ref[256:272, :] = labels
    odd_ref[256:272, :] = labels
    leads = (me_ref[0] & 1) == 0

    @pl.when(leads)
    def _():
        even_ref[0:256, :] = top
        odd_ref[0:256, :] = own.astype(BF)

    @pl.when(jnp.logical_not(leads))
    def _():
        even_ref[0:256, :] = own.astype(BF)
        odd_ref[0:256, :] = top


def conv_take_kernel(
    me_ref,
    twice_ref,
    first_ref,
    rest_ref,
    top_ref,
    own_ref,
    even_ref,
    odd_ref,
    w_ref,
    wp_ref,
    lab_ref,
    out_ref,
    tie_ref,
    logit_ref,
    src_ref,
    dst_ref,
):
    step = pl.program_id(0)

    @pl.when(step == 0)
    def _():
        def put(at, rows):
            rows = rows.astype(BF).astype(F32)
            src_ref[pl.ds(2 * at, rows.shape[0], stride=2), :] = rows[:, :128]
            src_ref[pl.ds(2 * at + 1, rows.shape[0], stride=2), :] = rows[:, 128:]

        def half(odd, *grid_rows):
            parts = []
            for u in grid_rows:
                ref, at = (first_ref, (u + 1) & 7) if u < 2 or u == 7 else (rest_ref, u - 2)
                at = at * 512 + odd * 256
                parts.append(ref[at : at + 256, :])
            return jnp.concatenate(parts, axis=0)

        leads = (me_ref[0] & 1) == 0
        even = even_ref[...].astype(F32)
        odd = odd_ref[...].astype(F32)
        above = jnp.where(leads, odd[0:256], even[0:256])
        below = jnp.where(leads, even, odd)
        z = top_taps(half(0, 1, 3, 5), half(1, 1, 3, 5), w_ref)
        z = z + lower_taps(half(0, 2, 4, 6), half(1, 2, 4, 6), half(0, 3, 5, 7), half(1, 3, 5, 7), w_ref)
        z = jnp.concatenate([own_ref[...] + above, z, top_ref[...].astype(F32) + below[0:256]], axis=0)
        labels = jnp.concatenate([lab_ref[:, i, :].astype(F32) for i in range(4)] + [below[256:272]], axis=1)
        s = sigmoid(z)
        act = (z * s).astype(BF)
        logits = dot_t(wp_ref[...], act)
        for i in range(4):
            logit_ref[:, i, :] = logits[:, i * 256 : (i + 1) * 256]
        dlogit = (loss_weight * (sigmoid(logits) - labels)).astype(BF)
        grad_act = lax.dot_general(dlogit, wp_ref[...], (((0,), (0,)), ((), ())), preferred_element_type=F32)
        dz = grad_act * (s * (1.0 + z * (1.0 - s)))
        row = lax.broadcasted_iota(jnp.int32, dz.shape, 0)
        dz = jnp.where(row < jnp.where(me_ref[1] == 0, 1024, 1280), dz, 0.0)
        dzs = shift_up(dz).astype(BF)
        dz = dz.astype(BF)
        put(0, dot_t(dz[0:1024], w_ref[1, 1]))
        put(1024, dot_t(dz[0:1024], w_ref[1, 2]) + dot_t(dzs[0:1024], w_ref[1, 0]))
        put(2048, dot_t(dz[0:1024], w_ref[2, 1]) + dot_t(dz[256:1280], w_ref[0, 1]))
        put(
            3072,
            dot_t(dz[0:1024], w_ref[2, 2])
            + dot_t(dzs[0:1024], w_ref[2, 0])
            + dot_t(dz[256:1280], w_ref[0, 2])
            + dot_t(dzs[256:1280], w_ref[0, 0]),
        )
        src_ref[2 * CELLS : 2 * CELLS + 8, :] = jnp.zeros((8, 128), F32)
        tie_ref[...] = jnp.zeros_like(tie_ref)

    count = out_ref.shape[0]
    per = twice_ref.shape[0]
    groups = count // per
    turn = 2 * per * TAKE_UNROLL

    def some(g, carry):
        rows = dst_ref.at[pl.ds(pl.multiple_of(g * turn, turn), turn), :]
        for j in range(TAKE_UNROLL):
            for k in range(per):
                at = pl.multiple_of(twice_ref[k, step * groups + g * TAKE_UNROLL + j], 2)
                to = 2 * (j * per + k)
                rows[to : to + 2, :] = src_ref[pl.ds(at, 2), :]
        return carry

    lax.fori_loop(0, groups // TAKE_UNROLL, some, 0)
    out_ref[:, :128] = dst_ref[pl.ds(0, count, stride=2), :].astype(BF)
    out_ref[:, 128:] = dst_ref[pl.ds(1, count, stride=2), :].astype(BF)


def grad_kernel(
    wd_ref, line_ref, bin_ref, depth_ref, near_ref, slope_hbm, far_hbm, inc_ref, came_ref, out_ref, logit_ref, acc_ref, accd_ref, slope_ref, far_ref, sems
):
    fetch = pltpu.make_async_copy(far_hbm, far_ref, sems.at[0])
    fetch.start()
    fetch_slope = pltpu.make_async_copy(slope_hbm, slope_ref, sems.at[1])
    fetch_slope.start()
    logit_ref[...] = came_ref[...]
    bin_ids = jnp.transpose(bin_ref[...])
    rows = acc_ref.shape[0]
    count = near_ref.shape[0]
    per = bin_ids.shape[1]
    groups = count // per
    lines = count // 128
    for h in range(2):
        if h:
            fetch.wait()
            fetch_slope.wait()
        picked = (far_ref if h else near_ref)[...]
        inc = inc_ref[h * count : (h + 1) * count, :]
        terms = picked.astype(F32) * inc.astype(F32)
        terms = terms[:, :128] + terms[:, 128:]
        high = terms.astype(BF)
        halves = jnp.concatenate([high, (terms - high.astype(F32)).astype(BF)], axis=1)
        inner = dot(halves, jnp.ones((256, 128), BF)).reshape(groups, per, 128)
        mine = bin_ids[h * groups : (h + 1) * groups, :]
        mask = (lax.broadcasted_iota(jnp.int32, (groups, per, 128), 2) & 63) == mine[:, :, None]
        binned = jnp.where(mask, inner, 0.0).reshape(count, 128)
        high = binned.astype(BF).astype(F32)
        lane = lax.broadcasted_iota(jnp.int32, (count, 128), 1)
        both = jnp.where(lane < 64, high, binned - high).astype(BF)
        chooser = row_hot(rows, as_line(line_ref[h * lines : (h + 1) * lines, :]))
        taken = dot(chooser * depth_ref[:, h * count : (h + 1) * count].astype(BF), inc)
        sums = dot(chooser, both)
        if h:
            acc_ref[...] += taken
            accd_ref[...] += sums
        else:
            acc_ref[...] = taken
            accd_ref[...] = sums
    sums = accd_ref[...]
    grad_logit = (slope_ref[...] * (sums[:, :64] + sums[:, 64:])).astype(BF)
    total = acc_ref[...] + dot(grad_logit, wd_ref[...])
    for i in range(out_ref.shape[0]):
        out_ref[i] = total[i * IMG_PAD : i * IMG_PAD + out_ref.shape[1], :]


def params():
    return pltpu.CompilerParams(vmem_limit_bytes=VMEM_LIMIT)


def whole(shape):
    return pl.BlockSpec(shape, lambda i: (0,) * len(shape))


def path_index(tiles):
    cam, tile = lax.axis_index("cam"), lax.axis_index("tile")
    x, y = cam >> 1, tile >> 2
    line = x * (tiles // 4) + jnp.where((x & 1) == 1, tiles // 4 - 1 - y, y)
    k = jnp.where((line & 1) == 1, 3 - (tile & 3), tile & 3)
    return line * 8 + k * 2 + (cam & 1)


def per_device(features, w_depth, w_conv, w_pred, send_row, send_bin, recv_cell, labels):
    imgs, pix, chan = features.shape
    sources, cap = send_row.shape[1], send_row.shape[2]
    slots = sources * cap
    rows = imgs * IMG_PAD
    row_t = jnp.transpose(send_row.reshape(sources, cap))
    bin_t = jnp.transpose(send_bin.reshape(sources, cap))
    cell_t = jnp.transpose(recv_cell.reshape(sources, cap))
    tile_count = lax.axis_size("tile")
    path = snake(lax.axis_size("cam"), tile_count)
    over = [(i, path[i]) for i in range(sources)]
    home = [(path[i], i) for i in range(sources)]
    order = jnp.asarray(np.eye(sources)[:, path], BF)
    cell_t = sent(cell_t, over)
    labels = sent(labels, over)
    wd_t = jnp.transpose(w_depth)
    bins = wd_t.shape[0]
    table = whole((cap, sources))
    lines = slots // 128
    ids_scratch = pltpu.VMEM((sources, cap), jnp.int32)
    wide_scratch = pltpu.VMEM((sources, 128), jnp.int32)
    x_scratch = pltpu.VMEM((rows, chan), BF)
    tie_spec = whole((8, 128))
    tie_shape = jax.ShapeDtypeStruct((8, 128), F32)

    def slot_spec(block):
        return pl.BlockSpec((block, chan), lambda i: (i, 0))

    def exchange(v):
        out = lax.all_to_all(
            v.reshape(sources, cap, chan), AXES, split_axis=0, concat_axis=0, axis_index_groups=[path], tiled=True
        )
        return out.reshape(slots, chan)

    payload, tie = pl.pallas_call(
        pick_kernel,
        out_shape=(pltpu.HBM((slots, chan), BF), tie_shape),
        grid=(slots // PICK_BLOCK,),
        in_specs=[whole(features.shape), whole(wd_t.shape), table, table],
        out_specs=(slot_spec(PICK_BLOCK), tie_spec),
        scratch_shapes=[x_scratch, ids_scratch, ids_scratch],
        compiler_params=params(),
        name="pick",
    )(*(pltpu.with_memory_space_constraint(v, pltpu.HBM) for v in (features, wd_t, row_t, bin_t)))
    arrived = exchange(payload)

    place_line, place_twice = pl.pallas_call(
        places_kernel,
        out_shape=(
            jax.ShapeDtypeStruct((lines, 128), jnp.int32),
            jax.ShapeDtypeStruct((cap, sources), jnp.int32),
        ),
        grid=(1,),
        in_specs=[table, whole((sources, sources)), tie_spec],
        out_specs=(whole((lines, 128)), table),
        scratch_shapes=[wide_scratch, pltpu.VMEM((cap, sources), jnp.int32)],
        compiler_params=params(),
        name="places",
    )(cell_t, order, tie)

    def splat(first, count, name, line):
        return pl.pallas_call(
            lambda *refs: splat_kernel(first, *refs),
            out_shape=jax.ShapeDtypeStruct((count, chan), BF),
            grid=(count // CELL_BLOCK,),
            in_specs=[whole((lines, 128)), whole((slots, chan))],
            out_specs=pl.BlockSpec((CELL_BLOCK, chan), lambda i: (i, 0)),
            compiler_params=params(),
            name=name,
        )(line, arrived)

    index = path_index(tile_count)
    me = jnp.stack([index, sources - 1 - index]).astype(jnp.int32)
    scalars = pl.BlockSpec(memory_space=pltpu.SMEM)
    vmem = pl.BlockSpec(memory_space=pltpu.VMEM)
    first = splat(0, FIRST_CELLS, "splat_first", place_line)
    message = jax.ShapeDtypeStruct((272, chan), BF)
    top, own, even, odd = pl.pallas_call(
        rim_kernel,
        out_shape=(
            jax.ShapeDtypeStruct((256, chan), BF),
            jax.ShapeDtypeStruct((256, chan), F32),
            message,
            message,
        ),
        in_specs=[scalars, vmem, vmem, vmem],
        compiler_params=params(),
        name="rim",
    )(me, first, w_conv, labels)
    got_even = sent(even, swap_pairs(path, 0))
    got_odd = sent(odd, swap_pairs(path, 1))
    line_b, _ = lax.optimization_barrier((place_line, top))
    rest = splat(FIRST_CELLS, CELLS - FIRST_CELLS, "splat_rest", line_b)

    outgoing, tie, logits = pl.pallas_call(
        conv_take_kernel,
        out_shape=(pltpu.HBM((slots, chan), BF), tie_shape, jax.ShapeDtypeStruct(labels.shape, F32)),
        grid=(slots // TAKE_BLOCK,),
        in_specs=[
            scalars,
            scalars,
            whole((FIRST_CELLS, chan)),
            whole((CELLS - FIRST_CELLS, chan)),
            whole((256, chan)),
            whole((256, chan)),
            whole((272, chan)),
            whole((272, chan)),
            whole(w_conv.shape),
            whole(w_pred.shape),
            whole(labels.shape),
        ],
        out_specs=(slot_spec(TAKE_BLOCK), tie_spec, whole(labels.shape)),
        scratch_shapes=[pltpu.VMEM((2 * CELLS + 8, 128), F32), pltpu.VMEM((2 * TAKE_BLOCK, 128), F32)],
        compiler_params=params(),
        name="conv_take",
    )(me, place_twice, first, rest, top, own, got_even, got_odd, w_conv, w_pred, labels)
    returned = exchange(outgoing)
    logits = sent(logits, home)

    half = slots // 2
    near, far, depth, row_line, slope = pl.pallas_call(
        again_kernel,
        out_shape=(
            jax.ShapeDtypeStruct((half, chan), BF),
            pltpu.HBM((half, chan), BF),
            jax.ShapeDtypeStruct((1, slots), F32),
            jax.ShapeDtypeStruct((lines, 128), jnp.int32),
            pltpu.HBM((rows, bins), F32),
        ),
        grid=(2,),
        in_specs=[whole(features.shape), whole(wd_t.shape), table, table, tie_spec],
        out_specs=(
            whole((half, chan)),
            whole((half, chan)),
            pl.BlockSpec((1, half), lambda i: (0, i)),
            whole((lines, 128)),
            whole((rows, bins)),
        ),
        scratch_shapes=[x_scratch, ids_scratch, pltpu.VMEM((lines, 128), jnp.int32), wide_scratch],
        compiler_params=params(),
        name="pick_again",
    )(features, wd_t, row_t, bin_t, tie)

    held = [pltpu.with_memory_space_constraint(v, pltpu.HBM) for v in (slope, far)]
    grad, logits = pl.pallas_call(
        grad_kernel,
        out_shape=(jax.ShapeDtypeStruct((imgs, pix, chan), F32), jax.ShapeDtypeStruct(labels.shape, F32)),
        in_specs=[vmem] * 5 + [pl.BlockSpec(memory_space=pltpu.HBM)] * 2 + [vmem] * 2,
        scratch_shapes=[
            pltpu.VMEM((rows, chan), F32),
            pltpu.VMEM((rows, 128), F32),
            pltpu.VMEM((rows, bins), F32),
            pltpu.VMEM((half, chan), BF),
            pltpu.SemaphoreType.DMA((2,)),
        ],
        compiler_params=params(),
        name="grad",
    )(wd_t, row_line, bin_t, depth, near, *held, returned, logits)
    return logits, grad


def solution(mesh):
    in_specs = (
        P("cam", "tile", None),
        P(),
        P(),
        P(),
        P(("cam", "tile"), None, None),
        P(("cam", "tile"), None, None),
        P(("cam", "tile"), None, None),
        P(None, ("cam", "tile"), None),
    )
    out_specs = (P(None, ("cam", "tile"), None), P("cam", "tile", None))
    return jax.shard_map(
        per_device, mesh=mesh, in_specs=in_specs, out_specs=out_specs, check_vma=False
    )
```

```python
import jax
import jax.numpy as jnp
from jax import lax
from jax.experimental import pallas as pl
from jax.experimental.pallas import tpu as pltpu
from jax.sharding import PartitionSpec as P

loss_weight = 16.0
BF = jnp.bfloat16
F32 = jnp.float32
AXES = ("cam", "tile")
PICK_BLOCK = 2048
TAKE_BLOCK = 1024
TAKE_UNROLL = 4
FIRST_CELLS = 1536
CELLS = 4096
IMG_PAD = 48
VMEM_LIMIT = 48 * 1024 * 1024


def swapped(shard, first):
    pairs = []
    for i in range(first, lax.axis_size(AXES) - 1, 2):
        pairs += [(i, i + 1), (i + 1, i)]
    return lax.ppermute(shard, AXES, pairs)


def dot(a, b):
    return jnp.dot(a, b, preferred_element_type=F32)


def dot_t(a, b):
    return lax.dot_general(a, b, (((1,), (1,)), ((), ())), preferred_element_type=F32)


def sigmoid(v):
    return 1.0 / (1.0 + jnp.exp(-v))


def padded_row(row):
    return row + 4 * ((row * 1490) >> 16)


def cell_place(cell):
    u = cell >> 9
    v = cell & 511
    return jnp.where(u >= 8, -1, (u & 1) * 2048 + (v & 1) * 1024 + (u >> 1) * 256 + (v >> 1))


def splat_place(cell):
    u = cell >> 9
    v = cell & 511
    return jnp.where(u >= 8, -1, ((u + 1) & 7) * 512 + (v & 1) * 256 + (v >> 1))


def one_hot(mask):
    return jnp.where(mask, 1.0, 0.0).astype(BF)


def row_hot(rows, ids):
    hot = lax.broadcasted_iota(jnp.int16, (rows, ids.shape[1]), 0) == ids.astype(jnp.int16)
    return jnp.where(hot, jnp.ones((), BF), jnp.zeros((), BF))


def fill_rows(feat_ref, x_ref):
    for i in range(feat_ref.shape[0]):
        rows = feat_ref[i].astype(F32)
        rows = jnp.concatenate([rows, jnp.zeros((IMG_PAD - rows.shape[0], rows.shape[1]), F32)], axis=0)
        x_ref[i * IMG_PAD : (i + 1) * IMG_PAD, :] = rows.astype(BF)


def pick_rows(ids, x):
    groups, per = ids.shape
    rows = x.shape[0]
    chooser = one_hot(lax.broadcasted_iota(jnp.int32, (groups, per, rows), 2) == ids[:, :, None])
    return dot(chooser.reshape(groups * per, rows), x)


def pick_kernel(feat_ref, wd_ref, row_ref, bin_ref, pay_ref, tie_ref, x_ref, rid_ref, bid_ref):
    step = pl.program_id(0)

    @pl.when(step == 0)
    def _():
        fill_rows(feat_ref, x_ref)
        rid_ref[...] = padded_row(jnp.transpose(row_ref[...]))
        bid_ref[...] = jnp.transpose(bin_ref[...])
        tie_ref[...] = jnp.zeros_like(tie_ref)

    count = pay_ref.shape[0]
    per = rid_ref.shape[1]
    groups = count // per
    at = pl.ds(pl.multiple_of(step * groups, groups), groups)
    picked = pick_rows(rid_ref[at, :], x_ref[...])
    logits = dot_t(picked.astype(BF), wd_ref[...])
    bins = logits.shape[1]
    mask = lax.broadcasted_iota(jnp.int32, (groups, per, bins), 2) == bid_ref[at, :][:, :, None]
    chosen = jnp.sum(jnp.where(mask, logits.reshape(groups, per, bins), 0.0), axis=2, keepdims=True)
    pay_ref[...] = (sigmoid(chosen).reshape(count, 1) * picked).astype(BF)


def line_up(table_ref, wide_ref):
    per, partners = table_ref.shape
    wide_ref[:, 0:per] = jnp.transpose(table_ref[...])
    fold = 128 // per
    lane = lax.broadcasted_iota(jnp.int32, (partners // fold, 128), 1) // per
    out = jnp.zeros((partners // fold, 128), jnp.int32)
    for j in range(fold):
        part = wide_ref[pl.ds(j, partners // fold, stride=fold), :]
        if j:
            part = pltpu.roll(part, j * per, 1)
        out = jnp.where(lane == j, part, out)
    return out


def as_line(table):
    return jnp.concatenate([table[g : g + 1, :] for g in range(table.shape[0])], axis=1)


def places_kernel(cell_ref, tie_ref, line_ref, twice_ref, wide_ref):
    line_ref[...] = splat_place(line_up(cell_ref, wide_ref))
    place = cell_place(cell_ref[...])
    twice_ref[...] = 2 * jnp.where(place < 0, CELLS, place)


def again_kernel(
    feat_ref, wd_ref, row_ref, bin_ref, tie_ref, near_ref, far_ref, depth_ref, line_ref, slope_ref, x_ref, rid_ref, bid_ref, wide_ref
):
    step = pl.program_id(0)

    @pl.when(step == 0)
    def _():
        fill_rows(feat_ref, x_ref)
        rid_ref[...] = padded_row(jnp.transpose(row_ref[...]))
        line_ref[...] = padded_row(line_up(row_ref, wide_ref))
        bid_ref[...] = line_up(bin_ref, wide_ref)
        prob = sigmoid(dot_t(x_ref[...], wd_ref[...]))
        slope_ref[...] = prob * (1.0 - prob)

    count = near_ref.shape[0]
    groups = count // rid_ref.shape[1]
    at = pl.ds(pl.multiple_of(step * groups, groups), groups)
    picked = pick_rows(rid_ref[at, :], x_ref[...]).astype(BF)

    @pl.when(step == 0)
    def _():
        near_ref[...] = picked

    @pl.when(step == 1)
    def _():
        far_ref[...] = picked

    logits = dot_t(wd_ref[...], picked)
    lines = count // 128
    bins = as_line(bid_ref[pl.ds(pl.multiple_of(step * lines, lines), lines), :])
    mask = lax.broadcasted_iota(jnp.int32, logits.shape, 0) == bins
    depth_ref[...] = sigmoid(jnp.sum(jnp.where(mask, logits, 0.0), axis=0, keepdims=True))


def splat_kernel(first, line_ref, val_ref, out_ref):
    rows = out_ref.shape[0]
    place = as_line(line_ref[...]) - (first + pl.program_id(0) * rows)
    placer = one_hot(lax.broadcasted_iota(jnp.int32, (rows, place.shape[1]), 0) == place)
    out_ref[...] = dot(placer, val_ref[...]).astype(BF)


def shift_down(v):
    col = lax.broadcasted_iota(jnp.int32, v.shape, 0) & 255
    return jnp.where(col == 0, 0.0, pltpu.roll(v, 1, 0))


def shift_up(v):
    n = v.shape[0]
    col = lax.broadcasted_iota(jnp.int32, v.shape, 0) & 255
    return jnp.where(col == 255, 0.0, pltpu.roll(v, n - 1, 0))


def top_taps(ue, uo, w_ref):
    return dot(ue, w_ref[0, 1]) + dot(uo, w_ref[0, 2]) + shift_down(dot(uo, w_ref[0, 0]))


def lower_taps(ee, eo, oe, oo, w_ref):
    z = dot(ee, w_ref[1, 1]) + dot(eo, w_ref[1, 2])
    z = z + dot(oe, w_ref[2, 1]) + dot(oo, w_ref[2, 2])
    return z + shift_down(dot(eo, w_ref[1, 0]) + dot(oo, w_ref[2, 0]))


def rim_kernel(me_ref, first_ref, w_ref, lab_ref, top_ref, own_ref, odd_ref, even_ref):
    top = top_taps(first_ref[0:256, :], first_ref[256:512, :], w_ref).astype(BF)
    own = lower_taps(
        first_ref[512:768, :], first_ref[768:1024, :], first_ref[1024:1280, :], first_ref[1280:1536, :], w_ref
    )
    labels = lab_ref[:, 0, :].astype(F32).astype(BF)
    top_ref[...] = top
    own_ref[...] = own
    even_ref[256:272, :] = labels
    odd_ref[256:272, :] = labels
    leads = (me_ref[0] & 1) == 0

    @pl.when(leads)
    def _():
        even_ref[0:256, :] = top
        odd_ref[0:256, :] = own.astype(BF)

    @pl.when(jnp.logical_not(leads))
    def _():
        even_ref[0:256, :] = own.astype(BF)
        odd_ref[0:256, :] = top


def conv_take_kernel(
    me_ref,
    twice_ref,
    first_ref,
    rest_ref,
    top_ref,
    own_ref,
    odd_ref,
    even_ref,
    w_ref,
    wp_ref,
    lab_ref,
    out_ref,
    tie_ref,
    logit_ref,
    src_ref,
    dst_ref,
):
    step = pl.program_id(0)

    @pl.when(step == 0)
    def _():
        def put(at, rows):
            rows = rows.astype(BF).astype(F32)
            src_ref[pl.ds(2 * at, rows.shape[0], stride=2), :] = rows[:, :128]
            src_ref[pl.ds(2 * at + 1, rows.shape[0], stride=2), :] = rows[:, 128:]

        def half(odd, *grid_rows):
            parts = []
            for u in grid_rows:
                ref, at = (first_ref, (u + 1) & 7) if u < 2 or u == 7 else (rest_ref, u - 2)
                at = at * 512 + odd * 256
                parts.append(ref[at : at + 256, :])
            return jnp.concatenate(parts, axis=0)

        leads = (me_ref[0] & 1) == 0
        even = even_ref[...].astype(F32)
        odd = odd_ref[...].astype(F32)
        above = jnp.where(leads, odd[0:256], even[0:256])
        below = jnp.where(leads, even, odd)
        z = top_taps(half(0, 1, 3, 5), half(1, 1, 3, 5), w_ref)
        z = z + lower_taps(half(0, 2, 4, 6), half(1, 2, 4, 6), half(0, 3, 5, 7), half(1, 3, 5, 7), w_ref)
        z = jnp.concatenate([own_ref[...] + above, z, top_ref[...].astype(F32) + below[0:256]], axis=0)
        labels = jnp.concatenate([lab_ref[:, i, :].astype(F32) for i in range(4)] + [below[256:272]], axis=1)
        s = sigmoid(z)
        act = (z * s).astype(BF)
        logits = dot_t(wp_ref[...], act)
        for i in range(4):
            logit_ref[:, i, :] = logits[:, i * 256 : (i + 1) * 256]
        dlogit = (loss_weight * (sigmoid(logits) - labels)).astype(BF)
        grad_act = lax.dot_general(dlogit, wp_ref[...], (((0,), (0,)), ((), ())), preferred_element_type=F32)
        dz = grad_act * (s * (1.0 + z * (1.0 - s)))
        row = lax.broadcasted_iota(jnp.int32, dz.shape, 0)
        dz = jnp.where(row < jnp.where(me_ref[1] == 0, 1024, 1280), dz, 0.0)
        dzs = shift_up(dz).astype(BF)
        dz = dz.astype(BF)
        put(0, dot_t(dz[0:1024], w_ref[1, 1]))
        put(1024, dot_t(dz[0:1024], w_ref[1, 2]) + dot_t(dzs[0:1024], w_ref[1, 0]))
        put(2048, dot_t(dz[0:1024], w_ref[2, 1]) + dot_t(dz[256:1280], w_ref[0, 1]))
        put(
            3072,
            dot_t(dz[0:1024], w_ref[2, 2])
            + dot_t(dzs[0:1024], w_ref[2, 0])
            + dot_t(dz[256:1280], w_ref[0, 2])
            + dot_t(dzs[256:1280], w_ref[0, 0]),
        )
        src_ref[2 * CELLS : 2 * CELLS + 8, :] = jnp.zeros((8, 128), F32)
        tie_ref[...] = jnp.zeros_like(tie_ref)

    count = out_ref.shape[0]
    per = twice_ref.shape[0]
    groups = count // per
    turn = 2 * per * TAKE_UNROLL

    def some(g, carry):
        rows = dst_ref.at[pl.ds(pl.multiple_of(g * turn, turn), turn), :]
        for j in range(TAKE_UNROLL):
            for k in range(per):
                at = pl.multiple_of(twice_ref[k, step * groups + g * TAKE_UNROLL + j], 2)
                to = 2 * (j * per + k)
                rows[to : to + 2, :] = src_ref[pl.ds(at, 2), :]
        return carry

    lax.fori_loop(0, groups // TAKE_UNROLL, some, 0)
    out_ref[:, :128] = dst_ref[pl.ds(0, count, stride=2), :].astype(BF)
    out_ref[:, 128:] = dst_ref[pl.ds(1, count, stride=2), :].astype(BF)


def grad_kernel(
    wd_ref, line_ref, bin_ref, depth_ref, near_ref, slope_hbm, far_hbm, inc_ref, out_ref, acc_ref, accd_ref, slope_ref, far_ref, sems
):
    fetch = pltpu.make_async_copy(far_hbm, far_ref, sems.at[0])
    fetch.start()
    fetch_slope = pltpu.make_async_copy(slope_hbm, slope_ref, sems.at[1])
    fetch_slope.start()
    bin_ids = jnp.transpose(bin_ref[...])
    rows = acc_ref.shape[0]
    count = near_ref.shape[0]
    per = bin_ids.shape[1]
    groups = count // per
    lines = count // 128
    for h in range(2):
        if h:
            fetch.wait()
            fetch_slope.wait()
        picked = (far_ref if h else near_ref)[...]
        inc = inc_ref[h * count : (h + 1) * count, :]
        terms = picked.astype(F32) * inc.astype(F32)
        terms = terms[:, :128] + terms[:, 128:]
        high = terms.astype(BF)
        halves = jnp.concatenate([high, (terms - high.astype(F32)).astype(BF)], axis=1)
        inner = dot(halves, jnp.ones((256, 128), BF)).reshape(groups, per, 128)
        mine = bin_ids[h * groups : (h + 1) * groups, :]
        mask = (lax.broadcasted_iota(jnp.int32, (groups, per, 128), 2) & 63) == mine[:, :, None]
        binned = jnp.where(mask, inner, 0.0).reshape(count, 128)
        high = binned.astype(BF).astype(F32)
        lane = lax.broadcasted_iota(jnp.int32, (count, 128), 1)
        both = jnp.where(lane < 64, high, binned - high).astype(BF)
        chooser = row_hot(rows, as_line(line_ref[h * lines : (h + 1) * lines, :]))
        taken = dot(chooser * depth_ref[:, h * count : (h + 1) * count].astype(BF), inc)
        sums = dot(chooser, both)
        if h:
            acc_ref[...] += taken
            accd_ref[...] += sums
        else:
            acc_ref[...] = taken
            accd_ref[...] = sums
    sums = accd_ref[...]
    grad_logit = (slope_ref[...] * (sums[:, :64] + sums[:, 64:])).astype(BF)
    total = acc_ref[...] + dot(grad_logit, wd_ref[...])
    for i in range(out_ref.shape[0]):
        out_ref[i] = total[i * IMG_PAD : i * IMG_PAD + out_ref.shape[1], :]


def params():
    return pltpu.CompilerParams(vmem_limit_bytes=VMEM_LIMIT)


def whole(shape):
    return pl.BlockSpec(shape, lambda i: (0,) * len(shape))


def per_device(features, w_depth, w_conv, w_pred, send_row, send_bin, recv_cell, labels):
    imgs, pix, chan = features.shape
    sources, cap = send_row.shape[1], send_row.shape[2]
    slots = sources * cap
    rows = imgs * IMG_PAD
    row_t = jnp.transpose(send_row.reshape(sources, cap))
    bin_t = jnp.transpose(send_bin.reshape(sources, cap))
    cell_t = jnp.transpose(recv_cell.reshape(sources, cap))
    wd_t = jnp.transpose(w_depth)
    bins = wd_t.shape[0]
    table = whole((cap, sources))
    lines = slots // 128
    ids_scratch = pltpu.VMEM((sources, cap), jnp.int32)
    wide_scratch = pltpu.VMEM((sources, 128), jnp.int32)
    x_scratch = pltpu.VMEM((rows, chan), BF)
    tie_spec = whole((8, 128))
    tie_shape = jax.ShapeDtypeStruct((8, 128), F32)

    def slot_spec(block):
        return pl.BlockSpec((block, chan), lambda i: (i, 0))

    def exchange(v):
        out = lax.all_to_all(v.reshape(sources, cap, chan), AXES, split_axis=0, concat_axis=0, tiled=True)
        return out.reshape(slots, chan)

    payload, tie = pl.pallas_call(
        pick_kernel,
        out_shape=(pltpu.HBM((slots, chan), BF), tie_shape),
        grid=(slots // PICK_BLOCK,),
        in_specs=[whole(features.shape), whole(wd_t.shape), table, table],
        out_specs=(slot_spec(PICK_BLOCK), tie_spec),
        scratch_shapes=[x_scratch, ids_scratch, ids_scratch],
        compiler_params=params(),
        name="pick",
    )(*(pltpu.with_memory_space_constraint(v, pltpu.HBM) for v in (features, wd_t, row_t, bin_t)))
    arrived = exchange(payload)

    place_line, place_twice = pl.pallas_call(
        places_kernel,
        out_shape=(
            jax.ShapeDtypeStruct((lines, 128), jnp.int32),
            jax.ShapeDtypeStruct((cap, sources), jnp.int32),
        ),
        grid=(1,),
        in_specs=[table, tie_spec],
        out_specs=(whole((lines, 128)), table),
        scratch_shapes=[wide_scratch],
        compiler_params=params(),
        name="places",
    )(cell_t, tie)

    def splat(first, count, block, name, line):
        return pl.pallas_call(
            lambda *refs: splat_kernel(first, *refs),
            out_shape=jax.ShapeDtypeStruct((count, chan), BF),
            grid=(count // block,),
            in_specs=[whole((lines, 128)), whole((slots, chan))],
            out_specs=pl.BlockSpec((block, chan), lambda i: (i, 0)),
            compiler_params=params(),
            name=name,
        )(line, arrived)

    index = lax.axis_index(AXES)
    me = jnp.stack([index, lax.axis_size(AXES) - 1 - index]).astype(jnp.int32)
    scalars = pl.BlockSpec(memory_space=pltpu.SMEM)
    vmem = pl.BlockSpec(memory_space=pltpu.VMEM)
    first = splat(0, FIRST_CELLS, FIRST_CELLS // 2, "splat_first", place_line)
    message = jax.ShapeDtypeStruct((272, chan), BF)
    top, own, odd, even = pl.pallas_call(
        rim_kernel,
        out_shape=(
            jax.ShapeDtypeStruct((256, chan), BF),
            jax.ShapeDtypeStruct((256, chan), F32),
            message,
            message,
        ),
        in_specs=[scalars, vmem, vmem, vmem],
        compiler_params=params(),
        name="rim",
    )(me, first, w_conv, labels)
    got_odd = swapped(odd, 1)
    got_even = swapped(even, 0)
    line_b, _ = lax.optimization_barrier((place_line, top))
    rest = splat(FIRST_CELLS, CELLS - FIRST_CELLS, (CELLS - FIRST_CELLS) // 2, "splat_rest", line_b)

    outgoing, tie, logits = pl.pallas_call(
        conv_take_kernel,
        out_shape=(pltpu.HBM((slots, chan), BF), tie_shape, jax.ShapeDtypeStruct(labels.shape, F32)),
        grid=(slots // TAKE_BLOCK,),
        in_specs=[
            scalars,
            scalars,
            whole((FIRST_CELLS, chan)),
            whole((CELLS - FIRST_CELLS, chan)),
            whole((256, chan)),
            whole((256, chan)),
            whole((272, chan)),
            whole((272, chan)),
            whole(w_conv.shape),
            whole(w_pred.shape),
            whole(labels.shape),
        ],
        out_specs=(slot_spec(TAKE_BLOCK), tie_spec, whole(labels.shape)),
        scratch_shapes=[pltpu.VMEM((2 * CELLS + 8, 128), F32), pltpu.VMEM((2 * TAKE_BLOCK, 128), F32)],
        compiler_params=params(),
        name="conv_take",
    )(me, place_twice, first, rest, top, own, got_odd, got_even, w_conv, w_pred, labels)
    returned = exchange(outgoing)

    half = slots // 2
    near, far, depth, row_line, slope = pl.pallas_call(
        again_kernel,
        out_shape=(
            jax.ShapeDtypeStruct((half, chan), BF),
            pltpu.HBM((half, chan), BF),
            jax.ShapeDtypeStruct((1, slots), F32),
            jax.ShapeDtypeStruct((lines, 128), jnp.int32),
            pltpu.HBM((rows, bins), F32),
        ),
        grid=(2,),
        in_specs=[whole(features.shape), whole(wd_t.shape), table, table, tie_spec],
        out_specs=(
            whole((half, chan)),
            whole((half, chan)),
            pl.BlockSpec((1, half), lambda i: (0, i)),
            whole((lines, 128)),
            whole((rows, bins)),
        ),
        scratch_shapes=[x_scratch, ids_scratch, pltpu.VMEM((lines, 128), jnp.int32), wide_scratch],
        compiler_params=params(),
        name="pick_again",
    )(features, wd_t, row_t, bin_t, tie)

    held = [pltpu.with_memory_space_constraint(v, pltpu.HBM) for v in (slope, far)]
    grad = pl.pallas_call(
        grad_kernel,
        out_shape=jax.ShapeDtypeStruct((imgs, pix, chan), F32),
        in_specs=[vmem] * 5 + [pl.BlockSpec(memory_space=pltpu.HBM)] * 2 + [vmem],
        scratch_shapes=[
            pltpu.VMEM((rows, chan), F32),
            pltpu.VMEM((rows, 128), F32),
            pltpu.VMEM((rows, bins), F32),
            pltpu.VMEM((half, chan), BF),
            pltpu.SemaphoreType.DMA((2,)),
        ],
        compiler_params=params(),
        name="grad",
    )(wd_t, row_line, bin_t, depth, near, *held, returned)
    return logits, grad


def solution(mesh):
    in_specs = (
        P("cam", "tile", None),
        P(),
        P(),
        P(),
        P(("cam", "tile"), None, None),
        P(("cam", "tile"), None, None),
        P(("cam", "tile"), None, None),
        P(None, ("cam", "tile"), None),
    )
    out_specs = (P(None, ("cam", "tile"), None), P("cam", "tile", None))
    return jax.shard_map(
        per_device, mesh=mesh, in_specs=in_specs, out_specs=out_specs, check_vma=False
    )
```

```python
import jax
import jax.numpy as jnp
from jax import lax
from jax.experimental import pallas as pl
from jax.experimental.pallas import tpu as pltpu
from jax.sharding import PartitionSpec as P

loss_weight = 16.0
BF = jnp.bfloat16
F32 = jnp.float32
AXES = ("cam", "tile")
PICK_BLOCK = 2048
TAKE_BLOCK = 1024
TAKE_UNROLL = 4
FIRST_CELLS = 1536
CELLS = 4096
IMG_PAD = 48
VMEM_LIMIT = 48 * 1024 * 1024


def swapped(shard, first):
    pairs = []
    for i in range(first, lax.axis_size(AXES) - 1, 2):
        pairs += [(i, i + 1), (i + 1, i)]
    return lax.ppermute(shard, AXES, pairs)


def dot(a, b):
    return jnp.dot(a, b, preferred_element_type=F32)


def dot_t(a, b):
    return lax.dot_general(a, b, (((1,), (1,)), ((), ())), preferred_element_type=F32)


def sigmoid(v):
    return 1.0 / (1.0 + jnp.exp(-v))


def padded_row(row):
    return row + 4 * ((row * 1490) >> 16)


def cell_place(cell):
    u = cell >> 9
    v = cell & 511
    return jnp.where(u >= 8, -1, (u & 1) * 2048 + (v & 1) * 1024 + (u >> 1) * 256 + (v >> 1))


def splat_place(cell):
    u = cell >> 9
    v = cell & 511
    return jnp.where(u >= 8, -1, ((u + 1) & 7) * 512 + (v & 1) * 256 + (v >> 1))


def one_hot(mask):
    return jnp.where(mask, 1.0, 0.0).astype(BF)


def row_hot(rows, ids):
    hot = lax.broadcasted_iota(jnp.int16, (rows, ids.shape[1]), 0) == ids.astype(jnp.int16)
    return jnp.where(hot, jnp.ones((), BF), jnp.zeros((), BF))


def fill_rows(feat_ref, x_ref):
    for i in range(feat_ref.shape[0]):
        rows = feat_ref[i].astype(F32)
        rows = jnp.concatenate([rows, jnp.zeros((IMG_PAD - rows.shape[0], rows.shape[1]), F32)], axis=0)
        x_ref[i * IMG_PAD : (i + 1) * IMG_PAD, :] = rows.astype(BF)


def pick_rows(ids, x):
    groups, per = ids.shape
    rows = x.shape[0]
    chooser = one_hot(lax.broadcasted_iota(jnp.int32, (groups, per, rows), 2) == ids[:, :, None])
    return dot(chooser.reshape(groups * per, rows), x)


def pick_kernel(feat_ref, wd_ref, row_ref, bin_ref, pay_ref, tie_ref, x_ref, rid_ref, bid_ref):
    step = pl.program_id(0)

    @pl.when(step == 0)
    def _():
        fill_rows(feat_ref, x_ref)
        rid_ref[...] = padded_row(jnp.transpose(row_ref[...]))
        bid_ref[...] = jnp.transpose(bin_ref[...])
        tie_ref[...] = jnp.zeros_like(tie_ref)

    count = pay_ref.shape[0]
    per = rid_ref.shape[1]
    groups = count // per
    at = pl.ds(pl.multiple_of(step * groups, groups), groups)
    picked = pick_rows(rid_ref[at, :], x_ref[...])
    logits = dot_t(picked.astype(BF), wd_ref[...])
    bins = logits.shape[1]
    mask = lax.broadcasted_iota(jnp.int32, (groups, per, bins), 2) == bid_ref[at, :][:, :, None]
    chosen = jnp.sum(jnp.where(mask, logits.reshape(groups, per, bins), 0.0), axis=2, keepdims=True)
    pay_ref[...] = (sigmoid(chosen).reshape(count, 1) * picked).astype(BF)


def line_up(table_ref, wide_ref):
    per, partners = table_ref.shape
    wide_ref[:, 0:per] = jnp.transpose(table_ref[...])
    fold = 128 // per
    lane = lax.broadcasted_iota(jnp.int32, (partners // fold, 128), 1) // per
    out = jnp.zeros((partners // fold, 128), jnp.int32)
    for j in range(fold):
        part = wide_ref[pl.ds(j, partners // fold, stride=fold), :]
        if j:
            part = pltpu.roll(part, j * per, 1)
        out = jnp.where(lane == j, part, out)
    return out


def as_line(table):
    return jnp.concatenate([table[g : g + 1, :] for g in range(table.shape[0])], axis=1)


def places_kernel(cell_ref, tie_ref, line_ref, pair_ref, wide_ref, twice_ref):
    line_ref[...] = splat_place(line_up(cell_ref, wide_ref))
    place = cell_place(cell_ref[...])
    twice_ref[...] = 2 * jnp.where(place < 0, CELLS, place)
    half = pair_ref.shape[0]
    pair_ref[...] = twice_ref[pl.ds(0, half, stride=2), :] + 65536 * twice_ref[pl.ds(1, half, stride=2), :]


def again_kernel(
    feat_ref, wd_ref, row_ref, bin_ref, tie_ref, near_ref, far_ref, depth_ref, line_ref, slope_ref, x_ref, rid_ref, bid_ref, wide_ref
):
    step = pl.program_id(0)

    @pl.when(step == 0)
    def _():
        fill_rows(feat_ref, x_ref)
        rid_ref[...] = padded_row(jnp.transpose(row_ref[...]))
        line_ref[...] = padded_row(line_up(row_ref, wide_ref))
        bid_ref[...] = line_up(bin_ref, wide_ref)
        prob = sigmoid(dot_t(x_ref[...], wd_ref[...]))
        slope_ref[...] = prob * (1.0 - prob)

    count = near_ref.shape[0]
    groups = count // rid_ref.shape[1]
    at = pl.ds(pl.multiple_of(step * groups, groups), groups)
    picked = pick_rows(rid_ref[at, :], x_ref[...]).astype(BF)

    @pl.when(step == 0)
    def _():
        near_ref[...] = picked

    @pl.when(step == 1)
    def _():
        far_ref[...] = picked

    logits = dot_t(wd_ref[...], picked)
    lines = count // 128
    bins = as_line(bid_ref[pl.ds(pl.multiple_of(step * lines, lines), lines), :])
    mask = lax.broadcasted_iota(jnp.int32, logits.shape, 0) == bins
    depth_ref[...] = sigmoid(jnp.sum(jnp.where(mask, logits, 0.0), axis=0, keepdims=True))


def splat_kernel(first, line_ref, val_ref, out_ref):
    rows = out_ref.shape[0]
    place = as_line(line_ref[...]) - (first + pl.program_id(0) * rows)
    placer = one_hot(lax.broadcasted_iota(jnp.int32, (rows, place.shape[1]), 0) == place)
    out_ref[...] = dot(placer, val_ref[...]).astype(BF)


def shift_down(v):
    col = lax.broadcasted_iota(jnp.int32, v.shape, 0) & 255
    return jnp.where(col == 0, 0.0, pltpu.roll(v, 1, 0))


def shift_up(v):
    n = v.shape[0]
    col = lax.broadcasted_iota(jnp.int32, v.shape, 0) & 255
    return jnp.where(col == 255, 0.0, pltpu.roll(v, n - 1, 0))


def top_taps(ue, uo, w_ref):
    return dot(ue, w_ref[0, 1]) + dot(uo, w_ref[0, 2]) + shift_down(dot(uo, w_ref[0, 0]))


def lower_taps(ee, eo, oe, oo, w_ref):
    z = dot(ee, w_ref[1, 1]) + dot(eo, w_ref[1, 2])
    z = z + dot(oe, w_ref[2, 1]) + dot(oo, w_ref[2, 2])
    return z + shift_down(dot(eo, w_ref[1, 0]) + dot(oo, w_ref[2, 0]))


def rim_kernel(me_ref, first_ref, w_ref, lab_ref, top_ref, own_ref, even_ref, odd_ref):
    top = top_taps(first_ref[0:256, :], first_ref[256:512, :], w_ref).astype(BF)
    own = lower_taps(
        first_ref[512:768, :], first_ref[768:1024, :], first_ref[1024:1280, :], first_ref[1280:1536, :], w_ref
    )
    labels = lab_ref[:, 0, :].astype(F32).astype(BF)
    top_ref[...] = top
    own_ref[...] = own
    even_ref[256:272, :] = labels
    odd_ref[256:272, :] = labels
    leads = (me_ref[0] & 1) == 0

    @pl.when(leads)
    def _():
        even_ref[0:256, :] = top
        odd_ref[0:256, :] = own.astype(BF)

    @pl.when(jnp.logical_not(leads))
    def _():
        even_ref[0:256, :] = own.astype(BF)
        odd_ref[0:256, :] = top


def conv_take_kernel(
    me_ref,
    pair_ref,
    first_ref,
    rest_ref,
    top_ref,
    own_ref,
    even_ref,
    odd_ref,
    w_ref,
    wp_ref,
    lab_ref,
    out_ref,
    tie_ref,
    logit_ref,
    src_ref,
    dst_ref,
):
    step = pl.program_id(0)

    @pl.when(step == 0)
    def _():
        def put(at, rows):
            rows = rows.astype(BF).astype(F32)
            src_ref[pl.ds(2 * at, rows.shape[0], stride=2), :] = rows[:, :128]
            src_ref[pl.ds(2 * at + 1, rows.shape[0], stride=2), :] = rows[:, 128:]

        def half(odd, *grid_rows):
            parts = []
            for u in grid_rows:
                ref, at = (first_ref, (u + 1) & 7) if u < 2 or u == 7 else (rest_ref, u - 2)
                at = at * 512 + odd * 256
                parts.append(ref[at : at + 256, :])
            return jnp.concatenate(parts, axis=0)

        leads = (me_ref[0] & 1) == 0
        even = even_ref[...].astype(F32)
        odd = odd_ref[...].astype(F32)
        above = jnp.where(leads, odd[0:256], even[0:256])
        below = jnp.where(leads, even, odd)
        z = top_taps(half(0, 1, 3, 5), half(1, 1, 3, 5), w_ref)
        z = z + lower_taps(half(0, 2, 4, 6), half(1, 2, 4, 6), half(0, 3, 5, 7), half(1, 3, 5, 7), w_ref)
        z = jnp.concatenate([own_ref[...] + above, z, top_ref[...].astype(F32) + below[0:256]], axis=0)
        labels = jnp.concatenate([lab_ref[:, i, :].astype(F32) for i in range(4)] + [below[256:272]], axis=1)
        s = sigmoid(z)
        act = (z * s).astype(BF)
        logits = dot_t(wp_ref[...], act)
        for i in range(4):
            logit_ref[:, i, :] = logits[:, i * 256 : (i + 1) * 256]
        dlogit = (loss_weight * (sigmoid(logits) - labels)).astype(BF)
        grad_act = lax.dot_general(dlogit, wp_ref[...], (((0,), (0,)), ((), ())), preferred_element_type=F32)
        dz = grad_act * (s * (1.0 + z * (1.0 - s)))
        row = lax.broadcasted_iota(jnp.int32, dz.shape, 0)
        dz = jnp.where(row < jnp.where(me_ref[1] == 0, 1024, 1280), dz, 0.0)
        dzs = shift_up(dz).astype(BF)
        dz = dz.astype(BF)
        put(0, dot_t(dz[0:1024], w_ref[1, 1]))
        put(1024, dot_t(dz[0:1024], w_ref[1, 2]) + dot_t(dzs[0:1024], w_ref[1, 0]))
        put(2048, dot_t(dz[0:1024], w_ref[2, 1]) + dot_t(dz[256:1280], w_ref[0, 1]))
        put(
            3072,
            dot_t(dz[0:1024], w_ref[2, 2])
            + dot_t(dzs[0:1024], w_ref[2, 0])
            + dot_t(dz[256:1280], w_ref[0, 2])
            + dot_t(dzs[256:1280], w_ref[0, 0]),
        )
        src_ref[2 * CELLS : 2 * CELLS + 8, :] = jnp.zeros((8, 128), F32)
        tie_ref[...] = jnp.zeros_like(tie_ref)

    count = out_ref.shape[0]
    per = 2 * pair_ref.shape[0]
    groups = count // per
    turn = 2 * per * TAKE_UNROLL

    def some(g, carry):
        rows = dst_ref.at[pl.ds(pl.multiple_of(g * turn, turn), turn), :]
        for j in range(TAKE_UNROLL):
            for k in range(per // 2):
                pair = pair_ref[k, step * groups + g * TAKE_UNROLL + j]
                to = 2 * (j * per + 2 * k)
                rows[to : to + 2, :] = src_ref[pl.ds(pl.multiple_of(pair & 65535, 2), 2), :]
                rows[to + 2 : to + 4, :] = src_ref[pl.ds(pl.multiple_of(pair >> 16, 2), 2), :]
        return carry

    lax.fori_loop(0, groups // TAKE_UNROLL, some, 0)
    out_ref[:, :128] = dst_ref[pl.ds(0, count, stride=2), :].astype(BF)
    out_ref[:, 128:] = dst_ref[pl.ds(1, count, stride=2), :].astype(BF)


def grad_kernel(
    wd_ref, line_ref, bin_ref, depth_ref, near_ref, slope_hbm, far_hbm, inc_ref, out_ref, acc_ref, accd_ref, slope_ref, far_ref, sems
):
    fetch = pltpu.make_async_copy(far_hbm, far_ref, sems.at[0])
    fetch.start()
    fetch_slope = pltpu.make_async_copy(slope_hbm, slope_ref, sems.at[1])
    fetch_slope.start()
    bin_ids = jnp.transpose(bin_ref[...])
    rows = acc_ref.shape[0]
    count = near_ref.shape[0]
    per = bin_ids.shape[1]
    groups = count // per
    lines = count // 128
    for h in range(2):
        if h:
            fetch.wait()
            fetch_slope.wait()
        picked = (far_ref if h else near_ref)[...]
        inc = inc_ref[h * count : (h + 1) * count, :]
        terms = picked.astype(F32) * inc.astype(F32)
        terms = terms[:, :128] + terms[:, 128:]
        high = terms.astype(BF)
        halves = jnp.concatenate([high, (terms - high.astype(F32)).astype(BF)], axis=1)
        inner = dot(halves, jnp.ones((256, 128), BF)).reshape(groups, per, 128)
        mine = bin_ids[h * groups : (h + 1) * groups, :]
        mask = (lax.broadcasted_iota(jnp.int32, (groups, per, 128), 2) & 63) == mine[:, :, None]
        binned = jnp.where(mask, inner, 0.0).reshape(count, 128)
        high = binned.astype(BF).astype(F32)
        lane = lax.broadcasted_iota(jnp.int32, (count, 128), 1)
        both = jnp.where(lane < 64, high, binned - high).astype(BF)
        chooser = row_hot(rows, as_line(line_ref[h * lines : (h + 1) * lines, :]))
        taken = dot(chooser * depth_ref[:, h * count : (h + 1) * count].astype(BF), inc)
        sums = dot(chooser, both)
        if h:
            acc_ref[...] += taken
            accd_ref[...] += sums
        else:
            acc_ref[...] = taken
            accd_ref[...] = sums
    sums = accd_ref[...]
    grad_logit = (slope_ref[...] * (sums[:, :64] + sums[:, 64:])).astype(BF)
    total = acc_ref[...] + dot(grad_logit, wd_ref[...])
    for i in range(out_ref.shape[0]):
        out_ref[i] = total[i * IMG_PAD : i * IMG_PAD + out_ref.shape[1], :]


def params():
    return pltpu.CompilerParams(vmem_limit_bytes=VMEM_LIMIT)


def whole(shape):
    return pl.BlockSpec(shape, lambda i: (0,) * len(shape))


def per_device(features, w_depth, w_conv, w_pred, send_row, send_bin, recv_cell, labels):
    imgs, pix, chan = features.shape
    sources, cap = send_row.shape[1], send_row.shape[2]
    slots = sources * cap
    rows = imgs * IMG_PAD
    row_t = jnp.transpose(send_row.reshape(sources, cap))
    bin_t = jnp.transpose(send_bin.reshape(sources, cap))
    cell_t = jnp.transpose(recv_cell.reshape(sources, cap))
    wd_t = jnp.transpose(w_depth)
    bins = wd_t.shape[0]
    table = whole((cap, sources))
    lines = slots // 128
    ids_scratch = pltpu.VMEM((sources, cap), jnp.int32)
    wide_scratch = pltpu.VMEM((sources, 128), jnp.int32)
    x_scratch = pltpu.VMEM((rows, chan), BF)
    tie_spec = whole((8, 128))
    tie_shape = jax.ShapeDtypeStruct((8, 128), F32)

    def slot_spec(block):
        return pl.BlockSpec((block, chan), lambda i: (i, 0))

    def exchange(v):
        out = lax.all_to_all(v.reshape(sources, cap, chan), AXES, split_axis=0, concat_axis=0, tiled=True)
        return out.reshape(slots, chan)

    payload, tie = pl.pallas_call(
        pick_kernel,
        out_shape=(pltpu.HBM((slots, chan), BF), tie_shape),
        grid=(slots // PICK_BLOCK,),
        in_specs=[whole(features.shape), whole(wd_t.shape), table, table],
        out_specs=(slot_spec(PICK_BLOCK), tie_spec),
        scratch_shapes=[x_scratch, ids_scratch, ids_scratch],
        compiler_params=params(),
        name="pick",
    )(*(pltpu.with_memory_space_constraint(v, pltpu.HBM) for v in (features, wd_t, row_t, bin_t)))
    arrived = exchange(payload)

    place_line, place_pairs = pl.pallas_call(
        places_kernel,
        out_shape=(
            jax.ShapeDtypeStruct((lines, 128), jnp.int32),
            jax.ShapeDtypeStruct((cap // 2, sources), jnp.int32),
        ),
        grid=(1,),
        in_specs=[table, tie_spec],
        out_specs=(whole((lines, 128)), whole((cap // 2, sources))),
        scratch_shapes=[wide_scratch, pltpu.VMEM((cap, sources), jnp.int32)],
        compiler_params=params(),
        name="places",
    )(cell_t, tie)

    def splat(first, count, block, name, line):
        return pl.pallas_call(
            lambda *refs: splat_kernel(first, *refs),
            out_shape=jax.ShapeDtypeStruct((count, chan), BF),
            grid=(count // block,),
            in_specs=[whole((lines, 128)), whole((slots, chan))],
            out_specs=pl.BlockSpec((block, chan), lambda i: (i, 0)),
            compiler_params=params(),
            name=name,
        )(line, arrived)

    index = lax.axis_index(AXES)
    me = jnp.stack([index, lax.axis_size(AXES) - 1 - index]).astype(jnp.int32)
    scalars = pl.BlockSpec(memory_space=pltpu.SMEM)
    vmem = pl.BlockSpec(memory_space=pltpu.VMEM)
    first = splat(0, FIRST_CELLS, FIRST_CELLS // 2, "splat_first", place_line)
    message = jax.ShapeDtypeStruct((272, chan), BF)
    top, own, even, odd = pl.pallas_call(
        rim_kernel,
        out_shape=(
            jax.ShapeDtypeStruct((256, chan), BF),
            jax.ShapeDtypeStruct((256, chan), F32),
            message,
            message,
        ),
        in_specs=[scalars, vmem, vmem, vmem],
        compiler_params=params(),
        name="rim",
    )(me, first, w_conv, labels)
    got_even = swapped(even, 0)
    got_odd = swapped(odd, 1)
    line_b, _ = lax.optimization_barrier((place_line, top))
    rest = splat(FIRST_CELLS, CELLS - FIRST_CELLS, (CELLS - FIRST_CELLS) // 2, "splat_rest", line_b)

    outgoing, tie, logits = pl.pallas_call(
        conv_take_kernel,
        out_shape=(pltpu.HBM((slots, chan), BF), tie_shape, jax.ShapeDtypeStruct(labels.shape, F32)),
        grid=(slots // TAKE_BLOCK,),
        in_specs=[
            scalars,
            scalars,
            whole((FIRST_CELLS, chan)),
            whole((CELLS - FIRST_CELLS, chan)),
            whole((256, chan)),
            whole((256, chan)),
            whole((272, chan)),
            whole((272, chan)),
            whole(w_conv.shape),
            whole(w_pred.shape),
            whole(labels.shape),
        ],
        out_specs=(slot_spec(TAKE_BLOCK), tie_spec, whole(labels.shape)),
        scratch_shapes=[pltpu.VMEM((2 * CELLS + 8, 128), F32), pltpu.VMEM((2 * TAKE_BLOCK, 128), F32)],
        compiler_params=params(),
        name="conv_take",
    )(me, place_pairs, first, rest, top, own, got_even, got_odd, w_conv, w_pred, labels)
    returned = exchange(outgoing)

    half = slots // 2
    near, far, depth, row_line, slope = pl.pallas_call(
        again_kernel,
        out_shape=(
            jax.ShapeDtypeStruct((half, chan), BF),
            pltpu.HBM((half, chan), BF),
            jax.ShapeDtypeStruct((1, slots), F32),
            jax.ShapeDtypeStruct((lines, 128), jnp.int32),
            pltpu.HBM((rows, bins), F32),
        ),
        grid=(2,),
        in_specs=[whole(features.shape), whole(wd_t.shape), table, table, tie_spec],
        out_specs=(
            whole((half, chan)),
            whole((half, chan)),
            pl.BlockSpec((1, half), lambda i: (0, i)),
            whole((lines, 128)),
            whole((rows, bins)),
        ),
        scratch_shapes=[x_scratch, ids_scratch, pltpu.VMEM((lines, 128), jnp.int32), wide_scratch],
        compiler_params=params(),
        name="pick_again",
    )(features, wd_t, row_t, bin_t, tie)

    held = [pltpu.with_memory_space_constraint(v, pltpu.HBM) for v in (slope, far)]
    grad = pl.pallas_call(
        grad_kernel,
        out_shape=jax.ShapeDtypeStruct((imgs, pix, chan), F32),
        in_specs=[vmem] * 5 + [pl.BlockSpec(memory_space=pltpu.HBM)] * 2 + [vmem],
        scratch_shapes=[
            pltpu.VMEM((rows, chan), F32),
            pltpu.VMEM((rows, 128), F32),
            pltpu.VMEM((rows, bins), F32),
            pltpu.VMEM((half, chan), BF),
            pltpu.SemaphoreType.DMA((2,)),
        ],
        compiler_params=params(),
        name="grad",
    )(wd_t, row_line, bin_t, depth, near, *held, returned)
    return logits, grad


def solution(mesh):
    in_specs = (
        P("cam", "tile", None),
        P(),
        P(),
        P(),
        P(("cam", "tile"), None, None),
        P(("cam", "tile"), None, None),
        P(("cam", "tile"), None, None),
        P(None, ("cam", "tile"), None),
    )
    out_specs = (P(None, ("cam", "tile"), None), P("cam", "tile", None))
    return jax.shard_map(
        per_device, mesh=mesh, in_specs=in_specs, out_specs=out_specs, check_vma=False
    )
```

```python
import jax
import jax.numpy as jnp
from jax import lax
from jax.experimental import pallas as pl
from jax.experimental.pallas import tpu as pltpu
from jax.sharding import PartitionSpec as P

loss_weight = 16.0
BF = jnp.bfloat16
F32 = jnp.float32
AXES = ("cam", "tile")
PICK_BLOCK = 2048
TAKE_BLOCK = 1024
TAKE_UNROLL = 16
FIRST_CELLS = 1536
CELLS = 4096
IMG_PAD = 48
VMEM_LIMIT = 48 * 1024 * 1024


def swapped(shard, first):
    pairs = []
    for i in range(first, lax.axis_size(AXES) - 1, 2):
        pairs += [(i, i + 1), (i + 1, i)]
    return lax.ppermute(shard, AXES, pairs)


def dot(a, b):
    return jnp.dot(a, b, preferred_element_type=F32)


def dot_t(a, b):
    return lax.dot_general(a, b, (((1,), (1,)), ((), ())), preferred_element_type=F32)


def sigmoid(v):
    return 1.0 / (1.0 + jnp.exp(-v))


def padded_row(row):
    return row + 4 * ((row * 1490) >> 16)


def cell_place(cell):
    u = cell >> 9
    v = cell & 511
    return jnp.where(u >= 8, -1, (u & 1) * 2048 + (v & 1) * 1024 + (u >> 1) * 256 + (v >> 1))


def splat_place(cell):
    u = cell >> 9
    v = cell & 511
    return jnp.where(u >= 8, -1, ((u + 1) & 7) * 512 + (v & 1) * 256 + (v >> 1))


def one_hot(mask):
    return jnp.where(mask, 1.0, 0.0).astype(BF)


def row_hot(rows, ids):
    hot = lax.broadcasted_iota(jnp.int16, (rows, ids.shape[1]), 0) == ids.astype(jnp.int16)
    return jnp.where(hot, jnp.ones((), BF), jnp.zeros((), BF))


def fill_rows(feat_ref, x_ref):
    for i in range(feat_ref.shape[0]):
        rows = feat_ref[i].astype(F32)
        rows = jnp.concatenate([rows, jnp.zeros((IMG_PAD - rows.shape[0], rows.shape[1]), F32)], axis=0)
        x_ref[i * IMG_PAD : (i + 1) * IMG_PAD, :] = rows.astype(BF)


def pick_rows(ids, x):
    groups, per = ids.shape
    rows = x.shape[0]
    chooser = one_hot(lax.broadcasted_iota(jnp.int32, (groups, per, rows), 2) == ids[:, :, None])
    return dot(chooser.reshape(groups * per, rows), x)


def pick_kernel(feat_ref, wd_ref, row_ref, bin_ref, pay_ref, tie_ref, x_ref, rid_ref, bid_ref):
    step = pl.program_id(0)

    @pl.when(step == 0)
    def _():
        fill_rows(feat_ref, x_ref)
        rid_ref[...] = padded_row(jnp.transpose(row_ref[...]))
        bid_ref[...] = jnp.transpose(bin_ref[...])
        tie_ref[...] = jnp.zeros_like(tie_ref)

    count = pay_ref.shape[0]
    per = rid_ref.shape[1]
    groups = count // per
    at = pl.ds(pl.multiple_of(step * groups, groups), groups)
    picked = pick_rows(rid_ref[at, :], x_ref[...])
    logits = dot_t(picked.astype(BF), wd_ref[...])
    bins = logits.shape[1]
    mask = lax.broadcasted_iota(jnp.int32, (groups, per, bins), 2) == bid_ref[at, :][:, :, None]
    chosen = jnp.sum(jnp.where(mask, logits.reshape(groups, per, bins), 0.0), axis=2, keepdims=True)
    pay_ref[...] = (sigmoid(chosen).reshape(count, 1) * picked).astype(BF)


def line_up(table_ref, wide_ref):
    per, partners = table_ref.shape
    wide_ref[:, 0:per] = jnp.transpose(table_ref[...])
    fold = 128 // per
    lane = lax.broadcasted_iota(jnp.int32, (partners // fold, 128), 1) // per
    out = jnp.zeros((partners // fold, 128), jnp.int32)
    for j in range(fold):
        part = wide_ref[pl.ds(j, partners // fold, stride=fold), :]
        if j:
            part = pltpu.roll(part, j * per, 1)
        out = jnp.where(lane == j, part, out)
    return out


def as_line(table):
    return jnp.concatenate([table[g : g + 1, :] for g in range(table.shape[0])], axis=1)


def places_kernel(cell_ref, tie_ref, line_ref, pair_ref, wide_ref, twice_ref):
    line_ref[...] = splat_place(line_up(cell_ref, wide_ref))
    place = cell_place(cell_ref[...])
    twice_ref[...] = 2 * jnp.where(place < 0, CELLS, place)
    half = pair_ref.shape[0]
    pair_ref[...] = twice_ref[pl.ds(0, half, stride=2), :] + 65536 * twice_ref[pl.ds(1, half, stride=2), :]


def again_kernel(
    feat_ref, wd_ref, row_ref, bin_ref, tie_ref, near_ref, far_ref, depth_ref, line_ref, slope_ref, x_ref, rid_ref, bid_ref, wide_ref
):
    step = pl.program_id(0)

    @pl.when(step == 0)
    def _():
        fill_rows(feat_ref, x_ref)
        rid_ref[...] = padded_row(jnp.transpose(row_ref[...]))
        line_ref[...] = padded_row(line_up(row_ref, wide_ref))
        bid_ref[...] = line_up(bin_ref, wide_ref)
        prob = sigmoid(dot_t(x_ref[...], wd_ref[...]))
        slope_ref[...] = prob * (1.0 - prob)

    count = near_ref.shape[0]
    groups = count // rid_ref.shape[1]
    at = pl.ds(pl.multiple_of(step * groups, groups), groups)
    picked = pick_rows(rid_ref[at, :], x_ref[...]).astype(BF)

    @pl.when(step == 0)
    def _():
        near_ref[...] = picked

    @pl.when(step == 1)
    def _():
        far_ref[...] = picked

    logits = dot_t(wd_ref[...], picked)
    lines = count // 128
    bins = as_line(bid_ref[pl.ds(pl.multiple_of(step * lines, lines), lines), :])
    mask = lax.broadcasted_iota(jnp.int32, logits.shape, 0) == bins
    depth_ref[...] = sigmoid(jnp.sum(jnp.where(mask, logits, 0.0), axis=0, keepdims=True))


def splat_kernel(first, line_ref, val_ref, out_ref):
    rows = out_ref.shape[0]
    place = as_line(line_ref[...]) - (first + pl.program_id(0) * rows)
    placer = one_hot(lax.broadcasted_iota(jnp.int32, (rows, place.shape[1]), 0) == place)
    out_ref[...] = dot(placer, val_ref[...]).astype(BF)


def shift_down(v):
    col = lax.broadcasted_iota(jnp.int32, v.shape, 0) & 255
    return jnp.where(col == 0, 0.0, pltpu.roll(v, 1, 0))


def shift_up(v):
    n = v.shape[0]
    col = lax.broadcasted_iota(jnp.int32, v.shape, 0) & 255
    return jnp.where(col == 255, 0.0, pltpu.roll(v, n - 1, 0))


def top_taps(ue, uo, w_ref):
    return dot(ue, w_ref[0, 1]) + dot(uo, w_ref[0, 2]) + shift_down(dot(uo, w_ref[0, 0]))


def lower_taps(ee, eo, oe, oo, w_ref):
    z = dot(ee, w_ref[1, 1]) + dot(eo, w_ref[1, 2])
    z = z + dot(oe, w_ref[2, 1]) + dot(oo, w_ref[2, 2])
    return z + shift_down(dot(eo, w_ref[1, 0]) + dot(oo, w_ref[2, 0]))


def first_kernel(me_ref, line_ref, val_ref, w_ref, lab_ref, first_ref, top_ref, own_ref, even_ref, odd_ref):
    step = pl.program_id(0)
    rows = first_ref.shape[0] // 2
    base = pl.multiple_of(step * rows, rows)
    place = as_line(line_ref[...]) - base
    placer = one_hot(lax.broadcasted_iota(jnp.int32, (rows, place.shape[1]), 0) == place)
    first_ref[pl.ds(base, rows), :] = dot(placer, val_ref[...]).astype(BF)

    @pl.when(step == 1)
    def _():
        top = top_taps(first_ref[0:256, :], first_ref[256:512, :], w_ref).astype(BF)
        own = lower_taps(
            first_ref[512:768, :], first_ref[768:1024, :], first_ref[1024:1280, :], first_ref[1280:1536, :], w_ref
        )
        labels = lab_ref[:, 0, :].astype(F32).astype(BF)
        top_ref[...] = top
        own_ref[...] = own
        even_ref[256:272, :] = labels
        odd_ref[256:272, :] = labels
        leads = (me_ref[0] & 1) == 0

        @pl.when(leads)
        def _():
            even_ref[0:256, :] = top
            odd_ref[0:256, :] = own.astype(BF)

        @pl.when(jnp.logical_not(leads))
        def _():
            even_ref[0:256, :] = own.astype(BF)
            odd_ref[0:256, :] = top


def conv_take_kernel(
    me_ref,
    pair_ref,
    first_ref,
    rest_ref,
    top_ref,
    own_ref,
    even_ref,
    odd_ref,
    w_ref,
    wp_ref,
    lab_ref,
    out_ref,
    tie_ref,
    logit_ref,
    src_ref,
    dst_ref,
):
    step = pl.program_id(0)

    @pl.when(step == 0)
    def _():
        def put(at, rows):
            rows = rows.astype(BF).astype(F32)
            src_ref[pl.ds(2 * at, rows.shape[0], stride=2), :] = rows[:, :128]
            src_ref[pl.ds(2 * at + 1, rows.shape[0], stride=2), :] = rows[:, 128:]

        def half(odd, *grid_rows):
            parts = []
            for u in grid_rows:
                ref, at = (first_ref, (u + 1) & 7) if u < 2 or u == 7 else (rest_ref, u - 2)
                at = at * 512 + odd * 256
                parts.append(ref[at : at + 256, :])
            return jnp.concatenate(parts, axis=0)

        leads = (me_ref[0] & 1) == 0
        even = even_ref[...].astype(F32)
        odd = odd_ref[...].astype(F32)
        above = jnp.where(leads, odd[0:256], even[0:256])
        below = jnp.where(leads, even, odd)
        z = top_taps(half(0, 1, 3, 5), half(1, 1, 3, 5), w_ref)
        z = z + lower_taps(half(0, 2, 4, 6), half(1, 2, 4, 6), half(0, 3, 5, 7), half(1, 3, 5, 7), w_ref)
        z = jnp.concatenate([own_ref[...] + above, z, top_ref[...].astype(F32) + below[0:256]], axis=0)
        labels = jnp.concatenate([lab_ref[:, i, :].astype(F32) for i in range(4)] + [below[256:272]], axis=1)
        s = sigmoid(z)
        act = (z * s).astype(BF)
        logits = dot_t(wp_ref[...], act)
        for i in range(4):
            logit_ref[:, i, :] = logits[:, i * 256 : (i + 1) * 256]
        dlogit = (loss_weight * (sigmoid(logits) - labels)).astype(BF)
        grad_act = lax.dot_general(dlogit, wp_ref[...], (((0,), (0,)), ((), ())), preferred_element_type=F32)
        dz = grad_act * (s * (1.0 + z * (1.0 - s)))
        dz = jnp.concatenate([dz[0:1024], jnp.where(me_ref[1] == 0, 0.0, dz[1024:1280])], axis=0)
        dzs = shift_up(dz).astype(BF)
        dz = dz.astype(BF)
        put(0, dot_t(dz[0:1024], w_ref[1, 1]))
        put(1024, dot_t(dz[0:1024], w_ref[1, 2]) + dot_t(dzs[0:1024], w_ref[1, 0]))
        put(2048, dot_t(dz[0:1024], w_ref[2, 1]) + dot_t(dz[256:1280], w_ref[0, 1]))
        put(
            3072,
            dot_t(dz[0:1024], w_ref[2, 2])
            + dot_t(dzs[0:1024], w_ref[2, 0])
            + dot_t(dz[256:1280], w_ref[0, 2])
            + dot_t(dzs[256:1280], w_ref[0, 0]),
        )
        src_ref[2 * CELLS : 2 * CELLS + 8, :] = jnp.zeros((8, 128), F32)
        tie_ref[...] = jnp.zeros_like(tie_ref)

    count = out_ref.shape[0]
    per = 2 * pair_ref.shape[0]
    groups = count // per
    turn = 2 * per * TAKE_UNROLL

    def some(g, carry):
        rows = dst_ref.at[pl.ds(pl.multiple_of(g * turn, turn), turn), :]
        for j in range(TAKE_UNROLL):
            for k in range(per // 2):
                pair = pair_ref[k, step * groups + g * TAKE_UNROLL + j]
                to = 2 * (j * per + 2 * k)
                rows[to : to + 2, :] = src_ref[pl.ds(pl.multiple_of(pair & 65535, 2), 2), :]
                rows[to + 2 : to + 4, :] = src_ref[pl.ds(pl.multiple_of(pair >> 16, 2), 2), :]
        return carry

    lax.fori_loop(0, groups // TAKE_UNROLL, some, 0)
    out_ref[:, :128] = dst_ref[pl.ds(0, count, stride=2), :].astype(BF)
    out_ref[:, 128:] = dst_ref[pl.ds(1, count, stride=2), :].astype(BF)


def grad_kernel(
    wd_ref, line_ref, bin_ref, depth_ref, near_ref, slope_hbm, far_hbm, inc_ref, out_ref, acc_ref, accd_ref, slope_ref, far_ref, sems
):
    fetch = pltpu.make_async_copy(far_hbm, far_ref, sems.at[0])
    fetch.start()
    fetch_slope = pltpu.make_async_copy(slope_hbm, slope_ref, sems.at[1])
    fetch_slope.start()
    bin_ids = jnp.transpose(bin_ref[...])
    rows = acc_ref.shape[0]
    count = near_ref.shape[0]
    per = bin_ids.shape[1]
    groups = count // per
    lines = count // 128
    for h in range(2):
        if h:
            fetch.wait()
            fetch_slope.wait()
        picked = (far_ref if h else near_ref)[...]
        inc = inc_ref[h * count : (h + 1) * count, :]
        terms = picked.astype(F32) * inc.astype(F32)
        terms = terms[:, :128] + terms[:, 128:]
        high = terms.astype(BF)
        halves = jnp.concatenate([high, (terms - high.astype(F32)).astype(BF)], axis=1)
        inner = dot(halves, jnp.ones((256, 128), BF)).reshape(groups, per, 128)
        mine = bin_ids[h * groups : (h + 1) * groups, :]
        mask = (lax.broadcasted_iota(jnp.int32, (groups, per, 128), 2) & 63) == mine[:, :, None]
        binned = jnp.where(mask, inner, 0.0).reshape(count, 128)
        high = binned.astype(BF).astype(F32)
        lane = lax.broadcasted_iota(jnp.int32, (count, 128), 1)
        both = jnp.where(lane < 64, high, binned - high).astype(BF)
        chooser = row_hot(rows, as_line(line_ref[h * lines : (h + 1) * lines, :]))
        taken = dot(chooser * depth_ref[:, h * count : (h + 1) * count].astype(BF), inc)
        sums = dot(chooser, both)
        if h:
            acc_ref[...] += taken
            accd_ref[...] += sums
        else:
            acc_ref[...] = taken
            accd_ref[...] = sums
    sums = accd_ref[...]
    grad_logit = (slope_ref[...] * (sums[:, :64] + sums[:, 64:])).astype(BF)
    total = acc_ref[...] + dot(grad_logit, wd_ref[...])
    for i in range(out_ref.shape[0]):
        out_ref[i] = total[i * IMG_PAD : i * IMG_PAD + out_ref.shape[1], :]


def params():
    return pltpu.CompilerParams(vmem_limit_bytes=VMEM_LIMIT)


def whole(shape):
    return pl.BlockSpec(shape, lambda i: (0,) * len(shape))


def per_device(features, w_depth, w_conv, w_pred, send_row, send_bin, recv_cell, labels):
    imgs, pix, chan = features.shape
    sources, cap = send_row.shape[1], send_row.shape[2]
    slots = sources * cap
    rows = imgs * IMG_PAD
    row_t = jnp.transpose(send_row.reshape(sources, cap))
    bin_t = jnp.transpose(send_bin.reshape(sources, cap))
    cell_t = jnp.transpose(recv_cell.reshape(sources, cap))
    wd_t = jnp.transpose(w_depth)
    bins = wd_t.shape[0]
    table = whole((cap, sources))
    lines = slots // 128
    ids_scratch = pltpu.VMEM((sources, cap), jnp.int32)
    wide_scratch = pltpu.VMEM((sources, 128), jnp.int32)
    x_scratch = pltpu.VMEM((rows, chan), BF)
    tie_spec = whole((8, 128))
    tie_shape = jax.ShapeDtypeStruct((8, 128), F32)

    def slot_spec(block):
        return pl.BlockSpec((block, chan), lambda i: (i, 0))

    def exchange(v):
        out = lax.all_to_all(v.reshape(sources, cap, chan), AXES, split_axis=0, concat_axis=0, tiled=True)
        return out.reshape(slots, chan)

    payload, tie = pl.pallas_call(
        pick_kernel,
        out_shape=(pltpu.HBM((slots, chan), BF), tie_shape),
        grid=(slots // PICK_BLOCK,),
        in_specs=[whole(features.shape), whole(wd_t.shape), table, table],
        out_specs=(slot_spec(PICK_BLOCK), tie_spec),
        scratch_shapes=[x_scratch, ids_scratch, ids_scratch],
        compiler_params=params(),
        name="pick",
    )(*(pltpu.with_memory_space_constraint(v, pltpu.HBM) for v in (features, wd_t, row_t, bin_t)))
    arrived = exchange(payload)

    place_line, place_pairs = pl.pallas_call(
        places_kernel,
        out_shape=(
            jax.ShapeDtypeStruct((lines, 128), jnp.int32),
            jax.ShapeDtypeStruct((cap // 2, sources), jnp.int32),
        ),
        grid=(1,),
        in_specs=[table, tie_spec],
        out_specs=(whole((lines, 128)), whole((cap // 2, sources))),
        scratch_shapes=[wide_scratch, pltpu.VMEM((cap, sources), jnp.int32)],
        compiler_params=params(),
        name="places",
    )(cell_t, tie)

    def splat(first, count, block, name, line):
        return pl.pallas_call(
            lambda *refs: splat_kernel(first, *refs),
            out_shape=jax.ShapeDtypeStruct((count, chan), BF),
            grid=(count // block,),
            in_specs=[whole((lines, 128)), whole((slots, chan))],
            out_specs=pl.BlockSpec((block, chan), lambda i: (i, 0)),
            compiler_params=params(),
            name=name,
        )(line, arrived)

    index = lax.axis_index(AXES)
    me = jnp.stack([index, lax.axis_size(AXES) - 1 - index]).astype(jnp.int32)
    scalars = pl.BlockSpec(memory_space=pltpu.SMEM)
    vmem = pl.BlockSpec(memory_space=pltpu.VMEM)
    message = jax.ShapeDtypeStruct((272, chan), BF)
    first, top, own, even, odd = pl.pallas_call(
        first_kernel,
        out_shape=(
            jax.ShapeDtypeStruct((FIRST_CELLS, chan), BF),
            jax.ShapeDtypeStruct((256, chan), BF),
            jax.ShapeDtypeStruct((256, chan), F32),
            message,
            message,
        ),
        grid=(2,),
        in_specs=[
            scalars,
            whole((lines, 128)),
            whole((slots, chan)),
            whole(w_conv.shape),
            whole(labels.shape),
        ],
        out_specs=tuple(whole((n, chan)) for n in (FIRST_CELLS, 256, 256, 272, 272)),
        compiler_params=params(),
        name="first_rows",
    )(me, place_line, arrived, w_conv, labels)
    got_even = swapped(even, 0)
    got_odd = swapped(odd, 1)
    line_b, _ = lax.optimization_barrier((place_line, top))
    rest = splat(FIRST_CELLS, CELLS - FIRST_CELLS, (CELLS - FIRST_CELLS) // 2, "splat_rest", line_b)

    outgoing, tie, logits = pl.pallas_call(
        conv_take_kernel,
        out_shape=(pltpu.HBM((slots, chan), BF), tie_shape, jax.ShapeDtypeStruct(labels.shape, F32)),
        grid=(slots // TAKE_BLOCK,),
        in_specs=[
            scalars,
            scalars,
            whole((FIRST_CELLS, chan)),
            whole((CELLS - FIRST_CELLS, chan)),
            whole((256, chan)),
            whole((256, chan)),
            whole((272, chan)),
            whole((272, chan)),
            whole(w_conv.shape),
            whole(w_pred.shape),
            whole(labels.shape),
        ],
        out_specs=(slot_spec(TAKE_BLOCK), tie_spec, whole(labels.shape)),
        scratch_shapes=[pltpu.VMEM((2 * CELLS + 8, 128), F32), pltpu.VMEM((2 * TAKE_BLOCK, 128), F32)],
        compiler_params=params(),
        name="conv_take",
    )(me, place_pairs, first, rest, top, own, got_even, got_odd, w_conv, w_pred, labels)
    returned = exchange(outgoing)

    half = slots // 2
    near, far, depth, row_line, slope = pl.pallas_call(
        again_kernel,
        out_shape=(
            jax.ShapeDtypeStruct((half, chan), BF),
            pltpu.HBM((half, chan), BF),
            jax.ShapeDtypeStruct((1, slots), F32),
            jax.ShapeDtypeStruct((lines, 128), jnp.int32),
            pltpu.HBM((rows, bins), F32),
        ),
        grid=(2,),
        in_specs=[whole(features.shape), whole(wd_t.shape), table, table, tie_spec],
        out_specs=(
            whole((half, chan)),
            whole((half, chan)),
            pl.BlockSpec((1, half), lambda i: (0, i)),
            whole((lines, 128)),
            whole((rows, bins)),
        ),
        scratch_shapes=[x_scratch, ids_scratch, pltpu.VMEM((lines, 128), jnp.int32), wide_scratch],
        compiler_params=params(),
        name="pick_again",
    )(features, wd_t, row_t, bin_t, tie)

    held = [pltpu.with_memory_space_constraint(v, pltpu.HBM) for v in (slope, far)]
    grad = pl.pallas_call(
        grad_kernel,
        out_shape=jax.ShapeDtypeStruct((imgs, pix, chan), F32),
        in_specs=[vmem] * 5 + [pl.BlockSpec(memory_space=pltpu.HBM)] * 2 + [vmem],
        scratch_shapes=[
            pltpu.VMEM((rows, chan), F32),
            pltpu.VMEM((rows, 128), F32),
            pltpu.VMEM((rows, bins), F32),
            pltpu.VMEM((half, chan), BF),
            pltpu.SemaphoreType.DMA((2,)),
        ],
        compiler_params=params(),
        name="grad",
    )(wd_t, row_line, bin_t, depth, near, *held, returned)
    return logits, grad


def solution(mesh):
    in_specs = (
        P("cam", "tile", None),
        P(),
        P(),
        P(),
        P(("cam", "tile"), None, None),
        P(("cam", "tile"), None, None),
        P(("cam", "tile"), None, None),
        P(None, ("cam", "tile"), None),
    )
    out_specs = (P(None, ("cam", "tile"), None), P("cam", "tile", None))
    return jax.shard_map(
        per_device, mesh=mesh, in_specs=in_specs, out_specs=out_specs, check_vma=False
    )
```

```python
import jax
import jax.numpy as jnp
from jax import lax
from jax.experimental import pallas as pl
from jax.experimental.pallas import tpu as pltpu
from jax.sharding import PartitionSpec as P

loss_weight = 16.0
BF = jnp.bfloat16
F32 = jnp.float32
AXES = ("cam", "tile")
PICK_BLOCK = 2048
TAKE_BLOCK = 1024
TAKE_UNROLL = 16
FIRST_CELLS = 1536
CELLS = 4096
IMG_PAD = 48
VMEM_LIMIT = 48 * 1024 * 1024


def swapped(shard, first):
    pairs = []
    for i in range(first, lax.axis_size(AXES) - 1, 2):
        pairs += [(i, i + 1), (i + 1, i)]
    return lax.ppermute(shard, AXES, pairs)


def dot(a, b):
    return jnp.dot(a, b, preferred_element_type=F32)


def dot_t(a, b):
    return lax.dot_general(a, b, (((1,), (1,)), ((), ())), preferred_element_type=F32)


def sigmoid(v):
    return jax.nn.sigmoid(v)


def padded_row(row):
    return row + 4 * ((row * 1490) >> 16)


def cell_place(cell):
    u = cell >> 9
    v = cell & 511
    return jnp.where(u >= 8, -1, (u & 1) * 2048 + (v & 1) * 1024 + (u >> 1) * 256 + (v >> 1))


def splat_place(cell):
    u = cell >> 9
    v = cell & 511
    return jnp.where(u >= 8, -1, ((u + 1) & 7) * 512 + (v & 1) * 256 + (v >> 1))


def one_hot(mask):
    return jnp.where(mask, 1.0, 0.0).astype(BF)


def row_hot(rows, ids):
    hot = lax.broadcasted_iota(jnp.int16, (rows, ids.shape[1]), 0) == ids.astype(jnp.int16)
    return jnp.where(hot, jnp.ones((), BF), jnp.zeros((), BF))


def fill_rows(feat_ref, x_ref):
    for i in range(feat_ref.shape[0]):
        rows = feat_ref[i].astype(F32)
        rows = jnp.concatenate([rows, jnp.zeros((IMG_PAD - rows.shape[0], rows.shape[1]), F32)], axis=0)
        x_ref[i * IMG_PAD : (i + 1) * IMG_PAD, :] = rows.astype(BF)


def pick_rows(ids, x):
    groups, per = ids.shape
    rows = x.shape[0]
    chooser = one_hot(lax.broadcasted_iota(jnp.int32, (groups, per, rows), 2) == ids[:, :, None])
    return dot(chooser.reshape(groups * per, rows), x)


def pick_kernel(feat_ref, wd_ref, row_ref, bin_ref, pay_ref, tie_ref, x_ref, rid_ref, bid_ref):
    step = pl.program_id(0)

    @pl.when(step == 0)
    def _():
        fill_rows(feat_ref, x_ref)
        rid_ref[...] = padded_row(jnp.transpose(row_ref[...]))
        bid_ref[...] = jnp.transpose(bin_ref[...])
        tie_ref[...] = jnp.zeros_like(tie_ref)

    count = pay_ref.shape[0]
    per = rid_ref.shape[1]
    groups = count // per
    at = pl.ds(pl.multiple_of(step * groups, groups), groups)
    picked = pick_rows(rid_ref[at, :], x_ref[...])
    logits = dot_t(picked.astype(BF), wd_ref[...])
    bins = logits.shape[1]
    mask = lax.broadcasted_iota(jnp.int32, (groups, per, bins), 2) == bid_ref[at, :][:, :, None]
    chosen = jnp.sum(jnp.where(mask, logits.reshape(groups, per, bins), 0.0), axis=2, keepdims=True)
    pay_ref[...] = (sigmoid(chosen).reshape(count, 1) * picked).astype(BF)


def line_up(table_ref, wide_ref):
    per, partners = table_ref.shape
    wide_ref[:, 0:per] = jnp.transpose(table_ref[...])
    fold = 128 // per
    lane = lax.broadcasted_iota(jnp.int32, (partners // fold, 128), 1) // per
    out = jnp.zeros((partners // fold, 128), jnp.int32)
    for j in range(fold):
        part = wide_ref[pl.ds(j, partners // fold, stride=fold), :]
        if j:
            part = pltpu.roll(part, j * per, 1)
        out = jnp.where(lane == j, part, out)
    return out


def as_line(table):
    return jnp.concatenate([table[g : g + 1, :] for g in range(table.shape[0])], axis=1)


def places_kernel(cell_ref, tie_ref, line_ref, pair_ref, wide_ref, twice_ref):
    line_ref[...] = splat_place(line_up(cell_ref, wide_ref))
    place = cell_place(cell_ref[...])
    twice_ref[...] = 2 * jnp.where(place < 0, CELLS, place)
    half = pair_ref.shape[0]
    pair_ref[...] = twice_ref[pl.ds(0, half, stride=2), :] + 65536 * twice_ref[pl.ds(1, half, stride=2), :]


def again_kernel(
    feat_ref, wd_ref, row_ref, bin_ref, tie_ref, near_ref, far_ref, depth_ref, line_ref, slope_ref, x_ref, rid_ref, bid_ref, wide_ref
):
    step = pl.program_id(0)

    @pl.when(step == 0)
    def _():
        fill_rows(feat_ref, x_ref)
        rid_ref[...] = padded_row(jnp.transpose(row_ref[...]))
        line_ref[...] = padded_row(line_up(row_ref, wide_ref))
        bid_ref[...] = line_up(bin_ref, wide_ref)
        prob = sigmoid(dot_t(x_ref[...], wd_ref[...]))
        slope_ref[...] = prob * (1.0 - prob)

    count = near_ref.shape[0]
    groups = count // rid_ref.shape[1]
    at = pl.ds(pl.multiple_of(step * groups, groups), groups)
    picked = pick_rows(rid_ref[at, :], x_ref[...]).astype(BF)

    @pl.when(step == 0)
    def _():
        near_ref[...] = picked

    @pl.when(step == 1)
    def _():
        far_ref[...] = picked

    logits = dot_t(wd_ref[...], picked)
    lines = count // 128
    bins = as_line(bid_ref[pl.ds(pl.multiple_of(step * lines, lines), lines), :])
    mask = lax.broadcasted_iota(jnp.int32, logits.shape, 0) == bins
    depth_ref[...] = sigmoid(jnp.sum(jnp.where(mask, logits, 0.0), axis=0, keepdims=True))


def splat_kernel(first, line_ref, val_ref, out_ref):
    rows = out_ref.shape[0]
    place = as_line(line_ref[...]) - (first + pl.program_id(0) * rows)
    placer = one_hot(lax.broadcasted_iota(jnp.int32, (rows, place.shape[1]), 0) == place)
    out_ref[...] = dot(placer, val_ref[...]).astype(BF)


def shift_down(v):
    col = lax.broadcasted_iota(jnp.int32, v.shape, 0) & 255
    return jnp.where(col == 0, 0.0, pltpu.roll(v, 1, 0))


def shift_up(v):
    n = v.shape[0]
    col = lax.broadcasted_iota(jnp.int32, v.shape, 0) & 255
    return jnp.where(col == 255, 0.0, pltpu.roll(v, n - 1, 0))


def top_taps(ue, uo, w_ref):
    return dot(ue, w_ref[0, 1]) + dot(uo, w_ref[0, 2]) + shift_down(dot(uo, w_ref[0, 0]))


def lower_taps(ee, eo, oe, oo, w_ref):
    z = dot(ee, w_ref[1, 1]) + dot(eo, w_ref[1, 2])
    z = z + dot(oe, w_ref[2, 1]) + dot(oo, w_ref[2, 2])
    return z + shift_down(dot(eo, w_ref[1, 0]) + dot(oo, w_ref[2, 0]))


def first_kernel(me_ref, line_ref, val_ref, w_ref, lab_ref, first_ref, top_ref, own_ref, even_ref, odd_ref):
    step = pl.program_id(0)
    rows = first_ref.shape[0] // 2
    base = pl.multiple_of(step * rows, rows)
    place = as_line(line_ref[...]) - base
    placer = one_hot(lax.broadcasted_iota(jnp.int32, (rows, place.shape[1]), 0) == place)
    first_ref[pl.ds(base, rows), :] = dot(placer, val_ref[...]).astype(BF)

    @pl.when(step == 1)
    def _():
        top = top_taps(first_ref[0:256, :], first_ref[256:512, :], w_ref).astype(BF)
        own = lower_taps(
            first_ref[512:768, :], first_ref[768:1024, :], first_ref[1024:1280, :], first_ref[1280:1536, :], w_ref
        )
        labels = lab_ref[:, 0, :].astype(F32).astype(BF)
        top_ref[...] = top
        own_ref[...] = own
        even_ref[256:272, :] = labels
        odd_ref[256:272, :] = labels
        leads = (me_ref[0] & 1) == 0

        @pl.when(leads)
        def _():
            even_ref[0:256, :] = top
            odd_ref[0:256, :] = own.astype(BF)

        @pl.when(jnp.logical_not(leads))
        def _():
            even_ref[0:256, :] = own.astype(BF)
            odd_ref[0:256, :] = top


def conv_take_kernel(
    me_ref,
    pair_ref,
    first_ref,
    rest_ref,
    top_ref,
    own_ref,
    even_ref,
    odd_ref,
    w_ref,
    wp_ref,
    lab_ref,
    out_ref,
    tie_ref,
    logit_ref,
    src_ref,
    dst_ref,
):
    step = pl.program_id(0)

    @pl.when(step == 0)
    def _():
        def put(at, rows):
            rows = rows.astype(BF).astype(F32)
            src_ref[pl.ds(2 * at, rows.shape[0], stride=2), :] = rows[:, :128]
            src_ref[pl.ds(2 * at + 1, rows.shape[0], stride=2), :] = rows[:, 128:]

        def half(odd, *grid_rows):
            parts = []
            for u in grid_rows:
                ref, at = (first_ref, (u + 1) & 7) if u < 2 or u == 7 else (rest_ref, u - 2)
                at = at * 512 + odd * 256
                parts.append(ref[at : at + 256, :])
            return jnp.concatenate(parts, axis=0)

        leads = (me_ref[0] & 1) == 0
        even = even_ref[...].astype(F32)
        odd = odd_ref[...].astype(F32)
        above = jnp.where(leads, odd[0:256], even[0:256])
        below = jnp.where(leads, even, odd)
        z = top_taps(half(0, 1, 3, 5), half(1, 1, 3, 5), w_ref)
        z = z + lower_taps(half(0, 2, 4, 6), half(1, 2, 4, 6), half(0, 3, 5, 7), half(1, 3, 5, 7), w_ref)
        z = jnp.concatenate([own_ref[...] + above, z, top_ref[...].astype(F32) + below[0:256]], axis=0)
        labels = jnp.concatenate([lab_ref[:, i, :].astype(F32) for i in range(4)] + [below[256:272]], axis=1)
        s = sigmoid(z)
        act = (z * s).astype(BF)
        logits = dot_t(wp_ref[...], act)
        for i in range(4):
            logit_ref[:, i, :] = logits[:, i * 256 : (i + 1) * 256]
        dlogit = (loss_weight * (sigmoid(logits) - labels)).astype(BF)
        grad_act = lax.dot_general(dlogit, wp_ref[...], (((0,), (0,)), ((), ())), preferred_element_type=F32)
        dz = grad_act * (s * (1.0 + z * (1.0 - s)))
        dz = jnp.concatenate([dz[0:1024], jnp.where(me_ref[1] == 0, 0.0, dz[1024:1280])], axis=0)
        dzs = shift_up(dz).astype(BF)
        dz = dz.astype(BF)
        put(0, dot_t(dz[0:1024], w_ref[1, 1]))
        put(1024, dot_t(dz[0:1024], w_ref[1, 2]) + dot_t(dzs[0:1024], w_ref[1, 0]))
        put(2048, dot_t(dz[0:1024], w_ref[2, 1]) + dot_t(dz[256:1280], w_ref[0, 1]))
        put(
            3072,
            dot_t(dz[0:1024], w_ref[2, 2])
            + dot_t(dzs[0:1024], w_ref[2, 0])
            + dot_t(dz[256:1280], w_ref[0, 2])
            + dot_t(dzs[256:1280], w_ref[0, 0]),
        )
        src_ref[2 * CELLS : 2 * CELLS + 8, :] = jnp.zeros((8, 128), F32)
        tie_ref[...] = jnp.zeros_like(tie_ref)

    count = out_ref.shape[0]
    per = 2 * pair_ref.shape[0]
    groups = count // per
    turn = 2 * per * TAKE_UNROLL

    def some(g, carry):
        rows = dst_ref.at[pl.ds(pl.multiple_of(g * turn, turn), turn), :]
        for j in range(TAKE_UNROLL):
            for k in range(per // 2):
                pair = pair_ref[k, step * groups + g * TAKE_UNROLL + j]
                to = 2 * (j * per + 2 * k)
                rows[to : to + 2, :] = src_ref[pl.ds(pl.multiple_of(pair & 65535, 2), 2), :]
                rows[to + 2 : to + 4, :] = src_ref[pl.ds(pl.multiple_of(pair >> 16, 2), 2), :]
        return carry

    lax.fori_loop(0, groups // TAKE_UNROLL, some, 0)
    out_ref[:, :128] = dst_ref[pl.ds(0, count, stride=2), :].astype(BF)
    out_ref[:, 128:] = dst_ref[pl.ds(1, count, stride=2), :].astype(BF)


def grad_kernel(
    wd_ref, line_ref, bin_ref, depth_ref, near_ref, slope_hbm, far_hbm, inc_ref, out_ref, acc_ref, accd_ref, slope_ref, far_ref, sems
):
    fetch = pltpu.make_async_copy(far_hbm, far_ref, sems.at[0])
    fetch.start()
    fetch_slope = pltpu.make_async_copy(slope_hbm, slope_ref, sems.at[1])
    fetch_slope.start()
    bin_ids = jnp.transpose(bin_ref[...])
    rows = acc_ref.shape[0]
    count = near_ref.shape[0]
    per = bin_ids.shape[1]
    groups = count // per
    lines = count // 128
    for h in range(2):
        if h:
            fetch.wait()
            fetch_slope.wait()
        picked = (far_ref if h else near_ref)[...]
        inc = inc_ref[h * count : (h + 1) * count, :]
        terms = picked.astype(F32) * inc.astype(F32)
        terms = terms[:, :128] + terms[:, 128:]
        high = terms.astype(BF)
        halves = jnp.concatenate([high, (terms - high.astype(F32)).astype(BF)], axis=1)
        inner = dot(halves, jnp.ones((256, 128), BF)).reshape(groups, per, 128)
        mine = bin_ids[h * groups : (h + 1) * groups, :]
        mask = (lax.broadcasted_iota(jnp.int32, (groups, per, 128), 2) & 63) == mine[:, :, None]
        binned = jnp.where(mask, inner, 0.0).reshape(count, 128)
        high = binned.astype(BF).astype(F32)
        lane = lax.broadcasted_iota(jnp.int32, (count, 128), 1)
        both = jnp.where(lane < 64, high, binned - high).astype(BF)
        chooser = row_hot(rows, as_line(line_ref[h * lines : (h + 1) * lines, :]))
        taken = dot(chooser * depth_ref[:, h * count : (h + 1) * count].astype(BF), inc)
        sums = dot(chooser, both)
        if h:
            acc_ref[...] += taken
            accd_ref[...] += sums
        else:
            acc_ref[...] = taken
            accd_ref[...] = sums
    sums = accd_ref[...]
    grad_logit = (slope_ref[...] * (sums[:, :64] + sums[:, 64:])).astype(BF)
    total = acc_ref[...] + dot(grad_logit, wd_ref[...])
    for i in range(out_ref.shape[0]):
        out_ref[i] = total[i * IMG_PAD : i * IMG_PAD + out_ref.shape[1], :]


def params():
    return pltpu.CompilerParams(vmem_limit_bytes=VMEM_LIMIT)


def whole(shape):
    return pl.BlockSpec(shape, lambda i: (0,) * len(shape))


def per_device(features, w_depth, w_conv, w_pred, send_row, send_bin, recv_cell, labels):
    imgs, pix, chan = features.shape
    sources, cap = send_row.shape[1], send_row.shape[2]
    slots = sources * cap
    rows = imgs * IMG_PAD
    row_t = jnp.transpose(send_row.reshape(sources, cap))
    bin_t = jnp.transpose(send_bin.reshape(sources, cap))
    cell_t = jnp.transpose(recv_cell.reshape(sources, cap))
    wd_t = jnp.transpose(w_depth)
    bins = wd_t.shape[0]
    table = whole((cap, sources))
    lines = slots // 128
    ids_scratch = pltpu.VMEM((sources, cap), jnp.int32)
    wide_scratch = pltpu.VMEM((sources, 128), jnp.int32)
    x_scratch = pltpu.VMEM((rows, chan), BF)
    tie_spec = whole((8, 128))
    tie_shape = jax.ShapeDtypeStruct((8, 128), F32)

    def slot_spec(block):
        return pl.BlockSpec((block, chan), lambda i: (i, 0))

    def exchange(v):
        out = lax.all_to_all(v.reshape(sources, cap, chan), AXES, split_axis=0, concat_axis=0, tiled=True)
        return out.reshape(slots, chan)

    payload, tie = pl.pallas_call(
        pick_kernel,
        out_shape=(pltpu.HBM((slots, chan), BF), tie_shape),
        grid=(slots // PICK_BLOCK,),
        in_specs=[whole(features.shape), whole(wd_t.shape), table, table],
        out_specs=(slot_spec(PICK_BLOCK), tie_spec),
        scratch_shapes=[x_scratch, ids_scratch, ids_scratch],
        compiler_params=params(),
        name="pick",
    )(*(pltpu.with_memory_space_constraint(v, pltpu.HBM) for v in (features, wd_t, row_t, bin_t)))
    arrived = exchange(payload)

    place_line, place_pairs = pl.pallas_call(
        places_kernel,
        out_shape=(
            jax.ShapeDtypeStruct((lines, 128), jnp.int32),
            jax.ShapeDtypeStruct((cap // 2, sources), jnp.int32),
        ),
        grid=(1,),
        in_specs=[table, tie_spec],
        out_specs=(whole((lines, 128)), whole((cap // 2, sources))),
        scratch_shapes=[wide_scratch, pltpu.VMEM((cap, sources), jnp.int32)],
        compiler_params=params(),
        name="places",
    )(cell_t, tie)

    def splat(first, count, block, name, line):
        return pl.pallas_call(
            lambda *refs: splat_kernel(first, *refs),
            out_shape=jax.ShapeDtypeStruct((count, chan), BF),
            grid=(count // block,),
            in_specs=[whole((lines, 128)), whole((slots, chan))],
            out_specs=pl.BlockSpec((block, chan), lambda i: (i, 0)),
            compiler_params=params(),
            name=name,
        )(line, arrived)

    index = lax.axis_index(AXES)
    me = jnp.stack([index, lax.axis_size(AXES) - 1 - index]).astype(jnp.int32)
    scalars = pl.BlockSpec(memory_space=pltpu.SMEM)
    vmem = pl.BlockSpec(memory_space=pltpu.VMEM)
    message = jax.ShapeDtypeStruct((272, chan), BF)
    first, top, own, even, odd = pl.pallas_call(
        first_kernel,
        out_shape=(
            jax.ShapeDtypeStruct((FIRST_CELLS, chan), BF),
            jax.ShapeDtypeStruct((256, chan), BF),
            jax.ShapeDtypeStruct((256, chan), F32),
            message,
            message,
        ),
        grid=(2,),
        in_specs=[
            scalars,
            whole((lines, 128)),
            whole((slots, chan)),
            whole(w_conv.shape),
            whole(labels.shape),
        ],
        out_specs=tuple(whole((n, chan)) for n in (FIRST_CELLS, 256, 256, 272, 272)),
        compiler_params=params(),
        name="first_rows",
    )(me, place_line, arrived, w_conv, labels)
    got_even = swapped(even, 0)
    got_odd = swapped(odd, 1)
    line_b, _ = lax.optimization_barrier((place_line, top))
    rest = splat(FIRST_CELLS, CELLS - FIRST_CELLS, (CELLS - FIRST_CELLS) // 2, "splat_rest", line_b)

    outgoing, tie, logits = pl.pallas_call(
        conv_take_kernel,
        out_shape=(pltpu.HBM((slots, chan), BF), tie_shape, jax.ShapeDtypeStruct(labels.shape, F32)),
        grid=(slots // TAKE_BLOCK,),
        in_specs=[
            scalars,
            scalars,
            whole((FIRST_CELLS, chan)),
            whole((CELLS - FIRST_CELLS, chan)),
            whole((256, chan)),
            whole((256, chan)),
            whole((272, chan)),
            whole((272, chan)),
            whole(w_conv.shape),
            whole(w_pred.shape),
            whole(labels.shape),
        ],
        out_specs=(slot_spec(TAKE_BLOCK), tie_spec, whole(labels.shape)),
        scratch_shapes=[pltpu.VMEM((2 * CELLS + 8, 128), F32), pltpu.VMEM((2 * TAKE_BLOCK, 128), F32)],
        compiler_params=params(),
        name="conv_take",
    )(me, place_pairs, first, rest, top, own, got_even, got_odd, w_conv, w_pred, labels)
    returned = exchange(outgoing)

    half = slots // 2
    near, far, depth, row_line, slope = pl.pallas_call(
        again_kernel,
        out_shape=(
            jax.ShapeDtypeStruct((half, chan), BF),
            pltpu.HBM((half, chan), BF),
            jax.ShapeDtypeStruct((1, slots), F32),
            jax.ShapeDtypeStruct((lines, 128), jnp.int32),
            pltpu.HBM((rows, bins), F32),
        ),
        grid=(2,),
        in_specs=[whole(features.shape), whole(wd_t.shape), table, table, tie_spec],
        out_specs=(
            whole((half, chan)),
            whole((half, chan)),
            pl.BlockSpec((1, half), lambda i: (0, i)),
            whole((lines, 128)),
            whole((rows, bins)),
        ),
        scratch_shapes=[x_scratch, ids_scratch, pltpu.VMEM((lines, 128), jnp.int32), wide_scratch],
        compiler_params=params(),
        name="pick_again",
    )(features, wd_t, row_t, bin_t, tie)

    held = [pltpu.with_memory_space_constraint(v, pltpu.HBM) for v in (slope, far)]
    grad = pl.pallas_call(
        grad_kernel,
        out_shape=jax.ShapeDtypeStruct((imgs, pix, chan), F32),
        in_specs=[vmem] * 5 + [pl.BlockSpec(memory_space=pltpu.HBM)] * 2 + [vmem],
        scratch_shapes=[
            pltpu.VMEM((rows, chan), F32),
            pltpu.VMEM((rows, 128), F32),
            pltpu.VMEM((rows, bins), F32),
            pltpu.VMEM((half, chan), BF),
            pltpu.SemaphoreType.DMA((2,)),
        ],
        compiler_params=params(),
        name="grad",
    )(wd_t, row_line, bin_t, depth, near, *held, returned)
    return logits, grad


def solution(mesh):
    in_specs = (
        P("cam", "tile", None),
        P(),
        P(),
        P(),
        P(("cam", "tile"), None, None),
        P(("cam", "tile"), None, None),
        P(("cam", "tile"), None, None),
        P(None, ("cam", "tile"), None),
    )
    out_specs = (P(None, ("cam", "tile"), None), P("cam", "tile", None))
    return jax.shard_map(
        per_device, mesh=mesh, in_specs=in_specs, out_specs=out_specs, check_vma=False
    )
```
